128 devices in a mesh: stream: 32 (over x_hi, y, z), span: 4 (over x_lo, core).
Axes of the slice: x: 4 (x_hi: 2, x_lo: 2; x = x_hi * 2 + x_lo), y: 4, z: 4, core: 2. Of those that a mesh axis runs over, the one named last changes fastest.
Arguments:
- velocity: float32 [3, 256, 128, 512], P(None, 'stream', None, 'span'), may hold values from -3 to 3
- fraction: float32 [256, 128, 512], P('stream', None, 'span'), may hold values from 0 to 1
- pressure_now: float32 [256, 128, 512], P('stream', None, 'span'), may hold values from -6 to 6
- pressure_old: float32 [256, 128, 512], P('stream', None, 'span'), may hold values from -6 to 6
- inflow: float32 [2, 128], replicated, may hold values from 0 to 1
Outputs:
- velocity_out: float32 [3, 256, 128, 512], P(None, 'stream', None, 'span')
- fraction_out: float32 [256, 128, 512], P('stream', None, 'span')
- pressure_out: float32 [256, 128, 512], P('stream', None, 'span')
- pressure_prev: float32 [256, 128, 512], P('stream', None, 'span')
The draws below stay inside these ranges and needn't reach their ends.
All inputs are finite; a program needn't handle non-finite values.
Results may differ from the reference program's by a relative error of at most 0.0001.
Values sent between devices are 32-bit elements; how exact they have to be, the bound alone decides.
No kernel may reach another device: no remote copies, remote signals or barrier semaphores. Data moves between devices by JAX's collectives and lax.ppermute only.
A program may use at most 128 MiB of HBM per device.

```python
import math
import jax
import jax.numpy as jnp
from jax import lax

NY = 128
NZ = 512
SWEEPS = 7
STEPS = 2
NX = 256


def block_levels(own_key, shape, pieces, smallest, high):
    loudness = 1.0
    for position, blocks in pieces:
        draws = jax.random.uniform(jax.random.fold_in(jax.random.fold_in(own_key, 6), position), (blocks,), jnp.float32, smallest / len(pieces), high / len(pieces))
        loudness = loudness * jnp.repeat(jnp.exp(draws), shape[position] // blocks).reshape((-1,) + (1,) * (len(shape) - 1 - position))
    return loudness


def normal_values(stream_key, shape, deviation, bound, cuts=(), kind=jnp.bfloat16):
    drawn = jax.random.normal(stream_key, shape, jnp.float32) * deviation
    if len(cuts) > 0:
        drawn = block_levels(stream_key, shape, cuts, -0.22, 0.18) * drawn
    return jnp.clip(drawn, min=-bound, max=bound).astype(kind)


def setup_inputs(seed: int = 0) -> dict:
    streams_of = jax.random.split(jax.random.key(seed), 6)
    return {
        "velocity": normal_values(streams_of[0], (3, NX, NY, NZ), 0.5, 3.0, ((1, 32), (3, 4)), jnp.float32),
        "fraction": jnp.clip(1.0 * jax.random.uniform(streams_of[1], (NX, NY, NZ), jnp.float32) ** block_levels(streams_of[1], (NX, NY, NZ), ((0, 32), (2, 4)), -0.2, 0.2), 0.0, 1.0),
        "pressure_now": normal_values(streams_of[2], (NX, NY, NZ), 1.0, 6.0, ((0, 32), (2, 4)), jnp.float32),
        "pressure_old": normal_values(streams_of[3], (NX, NY, NZ), 1.0, 6.0, ((0, 32), (2, 4)), jnp.float32),
        "inflow": jnp.clip(jax.random.uniform(streams_of[4], (2, NY), jnp.float32, 0.0, 1.0), 0.0, 1.0),
    }


TIME_STEP = 0.1
RHO_LIQUID = 1.0
RHO_GAS = 0.5
MU_LIQUID = 0.05
MU_GAS = 0.02
TENSION = 0.5
WALL_SPEED = 1.0
SLOPE_FLOOR = 0.5
DIRECTIONS = ((1, 0, 0), (0, 1, 0), (0, 0, 1))

def shifted(field, first_off, gap_off, span_off):
    return field[1 + first_off:field.shape[0] - 1 + first_off, 1 + gap_off:field.shape[1] - 1 + gap_off, 1 + span_off:field.shape[2] - 1 + span_off]

def central(field, axis):
    direction = DIRECTIONS[axis]
    ahead = shifted(field, direction[0], direction[1], direction[2])
    behind = shifted(field, -direction[0], -direction[1], -direction[2])
    return (ahead - behind) * 0.5

def second(field, axis):
    direction = DIRECTIONS[axis]
    ahead = shifted(field, direction[0], direction[1], direction[2])
    behind = shifted(field, -direction[0], -direction[1], -direction[2])
    return ahead - 2.0 * shifted(field, 0, 0, 0) + behind

def mixed(field, one_axis, other_axis):
    first_dir = DIRECTIONS[one_axis]
    other_dir = DIRECTIONS[other_axis]
    total = jnp.zeros_like(shifted(field, 0, 0, 0))
    for sign_one in (1, -1):
        for sign_two in (1, -1):
            offsets = [sign_one * first_dir[k] + sign_two * other_dir[k] for k in range(3)]
            total = total + sign_one * sign_two * shifted(field, offsets[0], offsets[1], offsets[2])
    return total * 0.25

def close_ends(padded, inflow, first, last):
    zero_row = jnp.zeros_like(inflow[0])
    profile = jnp.stack([inflow[0], zero_row, zero_row, inflow[1], zero_row, zero_row])
    target = (6, 2, padded.shape[2], padded.shape[3])
    lower = jnp.broadcast_to(profile[:, None, :, None], target).astype(padded.dtype)
    keeping = jnp.asarray([1.0, 1.0, 1.0, 1.0, 0.0, 0.0], jnp.float32).reshape(6, 1, 1, 1)
    upper = jnp.broadcast_to(padded[:, -3:-2] * keeping, target)
    return jnp.concatenate([jnp.where(first, lower, padded[:, :2]), padded[:, 2:-2], jnp.where(last, upper, padded[:, -2:])], axis=1)

def pad_gap(padded):
    signs = jnp.asarray([-1.0, -1.0, -1.0, 1.0, 1.0, 1.0], jnp.float32).reshape(6, 1, 1, 1)
    offsets = jnp.asarray([2.0 * WALL_SPEED, 0.0, 0.0, 0.0, 0.0, 0.0], jnp.float32).reshape(6, 1, 1, 1)
    bottom = signs * padded[:, :, :1] + offsets
    top = signs * padded[:, :, -1:]
    return jnp.concatenate([bottom, padded, top], axis=2)

def predict(padded):
    speeds = [padded[0], padded[1], padded[2]]
    volume = padded[3]
    guess = 2.0 * padded[4] - padded[5]
    centre = [shifted(field, 0, 0, 0) for field in speeds]
    volume_centre = shifted(volume, 0, 0, 0)
    density = RHO_GAS + (RHO_LIQUID - RHO_GAS) * volume_centre
    kinematic = (MU_GAS + (MU_LIQUID - MU_GAS) * volume_centre) / density
    slopes = [central(volume, axis) for axis in range(3)]
    magnitude = jnp.maximum(jnp.sqrt(slopes[0] * slopes[0] + slopes[1] * slopes[1] + slopes[2] * slopes[2]), SLOPE_FLOOR)
    normals = [slope / magnitude for slope in slopes]
    laplace_volume = second(volume, 0) + second(volume, 1) + second(volume, 2)
    bending = jnp.zeros_like(volume_centre)
    for one_axis in range(3):
        for other_axis in range(3):
            if one_axis == other_axis:
                hessian = second(volume, one_axis)
            else:
                hessian = mixed(volume, one_axis, other_axis)
            bending = bending + normals[one_axis] * normals[other_axis] * hessian
    curvature = -(laplace_volume - bending) / magnitude
    provisional = []
    for comp in range(3):
        field = speeds[comp]
        transport = jnp.zeros_like(volume_centre)
        diffusion = jnp.zeros_like(volume_centre)
        for axis in range(3):
            curve = second(field, axis)
            transport = transport + centre[axis] * central(field, axis) - 0.5 * jnp.abs(centre[axis]) * curve
            diffusion = diffusion + curve
        tension = TENSION * curvature * slopes[comp] / density
        provisional.append(centre[comp] + TIME_STEP * (-transport + kinematic * diffusion + tension))
    guess_slopes = [central(guess, axis) for axis in range(3)]
    fluxes = [RHO_GAS / TIME_STEP * provisional[axis] + (1.0 - RHO_GAS / density) * guess_slopes[axis] for axis in range(3)]
    net = jnp.zeros_like(volume_centre)
    for axis in range(3):
        direction = DIRECTIONS[axis]
        speed_ahead = shifted(speeds[axis], direction[0], direction[1], direction[2])
        speed_behind = shifted(speeds[axis], -direction[0], -direction[1], -direction[2])
        volume_ahead = shifted(volume, direction[0], direction[1], direction[2])
        volume_behind = shifted(volume, -direction[0], -direction[1], -direction[2])
        face_ahead = (centre[axis] + speed_ahead) * 0.5
        face_behind = (speed_behind + centre[axis]) * 0.5
        leaving = jnp.maximum(face_ahead, 0.0) * volume_centre + jnp.minimum(face_ahead, 0.0) * volume_ahead
        entering = jnp.maximum(face_behind, 0.0) * volume_behind + jnp.minimum(face_behind, 0.0) * volume_centre
        net = net + (leaving - entering)
    fraction_new = volume_centre - TIME_STEP * net
    return (provisional, fluxes, fraction_new, density, guess_slopes)

def interior(frame):
    return frame[1:-1, :, 1:-1]

def divergence(fluxes):
    first_part = (fluxes[0][2:, :, 1:-1] - fluxes[0][:-2, :, 1:-1]) * 0.5
    gap_flux = fluxes[1][1:-1, :, 1:-1]
    zero_row = jnp.zeros_like(gap_flux[:, :1])
    gap_part = (jnp.concatenate([gap_flux[:, 1:], zero_row], axis=1) - jnp.concatenate([zero_row, gap_flux[:, :-1]], axis=1)) * 0.5
    span_part = (fluxes[2][1:-1, :, 2:] - fluxes[2][1:-1, :, :-2]) * 0.5
    return first_part + gap_part + span_part

def transform_tables():
    index = jnp.arange(NZ, dtype=jnp.int32)
    wave = jnp.where(index <= NZ // 2, index, index - NZ // 2).astype(jnp.int32)
    phase = index[:, None] * wave[None, :] % NZ
    angle = phase.astype(jnp.float32) * (2.0 * math.pi / NZ)
    forward = jnp.where(index[None, :] <= NZ // 2, jnp.cos(angle), jnp.sin(angle))
    weight = jnp.where((index == 0) | (index == NZ // 2), 1.0 / NZ, 2.0 / NZ).astype(jnp.float32)
    inverse = jnp.transpose(forward) * weight[:, None]
    eigen = 2.0 - 2.0 * jnp.cos(wave.astype(jnp.float32) * (2.0 * math.pi / NZ))
    return (forward, inverse, eigen)

def gap_pair(field):
    above = jnp.concatenate([field[..., 1:], field[..., -1:]], axis=-1)
    below = jnp.concatenate([field[..., :1], field[..., :-1]], axis=-1)
    return above + below

def pressure_slopes(cycle):
    cycle = jnp.concatenate([cycle[:, :1], cycle, cycle[:, -1:]], axis=1)
    return [central(cycle, axis) for axis in range(3)]

def correct(provisional, density, guess_slopes, slopes):
    inner_density = interior(density)
    speeds = []
    for axis in range(3):
        change = slopes[axis] / RHO_GAS + (1.0 / inner_density - 1.0 / RHO_GAS) * interior(guess_slopes[axis])
        speeds.append(interior(provisional[axis]) - TIME_STEP * change)
    return jnp.stack(speeds)

def solve_pressure(source):
    forward, inverse, eigen = transform_tables()
    spectrum = jnp.einsum('xyz,zc->cxy', source, forward, precision=lax.Precision.HIGHEST)
    diagonal = (4.0 + eigen)[:, None, None]
    modal = -spectrum / diagonal
    for sweep in range(SWEEPS - 1):
        padded = jnp.pad(modal, ((0, 0), (1, 1), (0, 0)))
        beside_all = padded[:, 2:] + padded[:, :-2] + gap_pair(modal)
        modal = (beside_all - spectrum) / diagonal
    return jnp.einsum('cxy,cz->xyz', modal, inverse, precision=lax.Precision.HIGHEST)

def advance(state, inflow):
    wrapped = jnp.concatenate([state[..., -2:], state, state[..., :2]], axis=-1)
    padded = jnp.pad(wrapped, ((0, 0), (2, 2), (0, 0), (0, 0)))
    padded = pad_gap(close_ends(padded, inflow, True, True))
    provisional, fluxes, fraction_new, density, guess_slopes = predict(padded)
    source = divergence(fluxes)
    pressure = solve_pressure(source)
    cycle = jnp.concatenate([pressure[..., -1:], pressure, pressure[..., :1]], axis=-1)
    cycle = jnp.pad(cycle, ((1, 1), (0, 0), (0, 0)))
    speeds = correct(provisional, density, guess_slopes, pressure_slopes(cycle))
    return jnp.concatenate([speeds, interior(fraction_new)[None], pressure[None], state[4:5]], axis=0)

def reference(velocity, fraction, pressure_now, pressure_old, inflow):
    state = jnp.concatenate([velocity, fraction[None], pressure_now[None], pressure_old[None]], axis=0)
    for step in range(STEPS):
        state = advance(state, inflow)
    return (state[:3], state[3], state[4], state[5])
```

```python
import functools
import math

import jax
import jax.numpy as jnp
import numpy as np
from jax import lax
from jax.experimental import pallas as pl
from jax.experimental.pallas import tpu as pltpu
from jax.sharding import PartitionSpec as P

STEPS = 2
POWERS = 7
NX, NY, NZ = 8, 128, 128
TOP = 8
ROWS = NY + 2 * TOP
BLOCKS = 4
F32 = jnp.float32
BF16 = jnp.bfloat16
HIGHEST = lax.Precision.HIGHEST
VMEM_LIMIT = 60 * 1024 * 1024


def comb(n, k):
    return math.comb(n, k) if 0 <= k <= n else 0


RATIO = 3.0 - 2.0 * math.sqrt(2.0)


def line_kernel(power, n):
    return RATIO ** (power + n) * sum(
        comb(power - 1 + n + k, power - 1) * comb(power - 1 + k, power - 1) * RATIO ** (2 * k)
        for k in range(40)
    )


def far_kernel(power, j, z):
    return RATIO ** (power + 1 + z) * sum(
        comb(power - 1 + k, power - 1) * RATIO ** (2 * k) * comb(power + z + k, power - 1 - j)
        for k in range(40)
    )


@functools.cache
def solve_table():
    near = np.zeros((POWERS, 144, NZ + 2))
    for m in range(POWERS):
        kernel = np.array([line_kernel(m + 1, n) for n in range(NZ + 2)])
        z = np.arange(-1, NZ + 1)
        own = np.arange(NZ)
        near[m, :NZ] = kernel[np.abs(z[None, :] - own[:, None])]
        far = np.array([[far_kernel(m + 1, j, t) for t in z] for j in range(POWERS)])
        near[m, NZ : NZ + POWERS] = far
        near[m, NZ + POWERS : NZ + 2 * POWERS] = far[:, ::-1]
        near[m, NZ + 14] = -2.5 * near[m, 0]
        near[m, NZ + 15] = 2.5 * near[m, NZ - 1]
    value = near[:, :, 1:-1]
    slope = 0.5 * (near[:, :, 2:] - near[:, :, :-2])
    wide = np.concatenate([value, slope]).transpose(1, 0, 2).reshape(144, 2 * POWERS * NZ)
    wide = wide.astype(np.float32)
    head = wide.astype(jnp.bfloat16)
    tail = (wide - head.astype(np.float32)).astype(jnp.bfloat16)
    table = np.zeros((512, wide.shape[1]), jnp.bfloat16)
    table[0:128] = head[:NZ]
    table[128:256] = head[:NZ]
    table[256:384] = tail[:NZ]
    table[384:400] = head[NZ:]
    table[400:416] = head[NZ:]
    table[416:432] = tail[NZ:]
    return table


@functools.cache
def moment_table():
    table = np.zeros((2, NZ, 128), np.float32)
    for z in range(NZ):
        for j in range(POWERS):
            table[0, z, j] = comb(z, j) * RATIO**z
            table[0, z, POWERS + j] = comb(NZ - 1 - z, j) * RATIO ** (NZ - 1 - z)
    table[1, 0, 14] = 1.0
    table[1, NZ - 1, 15] = 1.0
    return table


@functools.cache
def combine_table():
    small = np.zeros((BLOCKS, 16, 16))
    end = [comb(NZ - 1, a) * RATIO ** (NZ - 1) for a in range(POWERS)]
    for o in range(1, 2 * BLOCKS + 1):
        gap = NZ * (o - 1)
        for j in range(POWERS):
            for a in range(j + 1):
                factor = comb(gap, j - a) * RATIO**gap
                left = -o
                small[left % BLOCKS, POWERS + a, j] += factor
                small[(left - 1) % BLOCKS, 15, j] += factor * end[a] * -2.5
                small[(left + 1) % BLOCKS, 14, j] += factor * (2.5 if a == 0 else 0.0)
                right = o
                small[right % BLOCKS, a, POWERS + j] += factor
                small[(right - 1) % BLOCKS, 15, POWERS + j] += factor * (-2.5 if a == 0 else 0.0)
                small[(right + 1) % BLOCKS, 14, POWERS + j] += factor * end[a] * 2.5
    small[-1 % BLOCKS, 15, 14] += 1.0
    small[1 % BLOCKS, 14, 15] += 1.0
    table = np.zeros((BLOCKS, 128, 128), np.float32)
    for x in range(NX):
        table[:, 16 * x : 16 * x + 16, 16 * x : 16 * x + 16] = small
    return table


def lanes(rows):
    return lax.broadcasted_iota(jnp.int32, (rows, 128), 1)


def pack_columns(fields):
    lane = lanes(NY)
    packed = jnp.zeros((NY, 128), F32)
    for k in range(5):
        for x in range(NX):
            pair = 12 * k + x + 2
            keep = (lane == 2 * pair + 1) | (lane == 2 * pair + 2)
            packed = jnp.where(keep, pltpu.roll(fields(k, x), 2 * pair + 2, 1), packed)
    return packed


def pack_body(vel, frac, now, old, right, left, packed, guess):
    for x in range(NX):
        guess[x] = 2.0 * now[x] - old[x]
    emit_faces(vel, frac, guess, right, left, packed)


def emit_faces(vel, frac, guess, right, left, packed):
    right[0:2] = vel[0, 6:8]
    right[2] = vel[1, 7]
    right[3] = vel[2, 7]
    right[4:6] = frac[6:8]
    right[6:8] = guess[6:8]
    left[0:2] = vel[0, 0:2]
    left[2] = vel[1, 0]
    left[3] = vel[2, 0]
    left[4:6] = frac[0:2]
    left[6:8] = guess[0:2]

    def field(k, x):
        return vel[k, x] if k < 3 else (frac[x] if k == 3 else guess[x])

    packed[...] = pack_columns(field)


def predict_body(
    flags, vel, frac, guess, low, high, sides, sides_low, sides_high, profile, moments,
    mid, frac_new, source, pack,
    U, V, W, F, G, FM, FP, Z, end_mid, sem,
):
    own = pl.ds(TOP, NY)
    copies = []

    def fetch(src, dst):
        copy = pltpu.make_async_copy(src, dst, sem.at[len(copies)])
        copy.start()
        copies.append(copy)

    for k, buf in enumerate((U, V, W)):
        fetch(vel.at[k], buf.at[pl.ds(2, NX), own])
    fetch(frac, F.at[pl.ds(2, NX), own])
    fetch(guess, G.at[pl.ds(2, NX), own])
    for msg, far, near in ((low, 0, 1), (high, 10, 10)):
        fetch(msg.at[pl.ds(0, 2)], U.at[pl.ds(far, 2), own])
        fetch(msg.at[2], V.at[near, own])
        fetch(msg.at[3], W.at[near, own])
        fetch(msg.at[pl.ds(4, 2)], F.at[pl.ds(far, 2), own])
        fetch(msg.at[pl.ds(6, 2)], G.at[pl.ds(far, 2), own])

    first = flags[0] == 1
    last = flags[1] == 1
    lane = lanes(NY)
    place = lane // 2
    slot = place % 12
    group = place // 12
    merged = sides[...]
    below = pltpu.roll(sides_low[...], 112, 1)
    above = pltpu.roll(sides_high[...], 16, 1)
    below_wall = jnp.where(group == 0, profile[0], jnp.where(group == 3, profile[1], 0.0))
    above_wall = jnp.where(slot == 10, pltpu.roll(merged, 2, 1), pltpu.roll(merged, 4, 1))
    below = jnp.where(first, below_wall, below)
    above = jnp.where(last, above_wall, above)
    Z[...] = jnp.where(slot < 2, below, jnp.where(slot >= 10, above, merged))

    for copy in copies:
        copy.wait()

    @pl.when(first)
    def _():
        for e in range(2):
            U[e, own] = profile[0]
            F[e, own] = profile[1]

    @pl.when(last)
    def _():
        for e in (10, 11):
            U[e, own] = U[9, own]
            F[e, own] = F[9, own]
        V[10, own] = V[9, own]
        W[10, own] = W[9, own]

    def shift_fraction(e, carry):
        lane = lanes(NY)
        centre = F[e, own]
        ends = pltpu.roll(Z[...], 128 - 2 * (36 + e) - 1, 1)
        FM[e, own] = jnp.where(lane == 0, ends, pltpu.roll(centre, 1, 1))
        FP[e, own] = jnp.where(lane == 127, ends, pltpu.roll(centre, 127, 1))
        for buf in (F, FM, FP):
            buf[e, pl.ds(TOP - 1, 1)] = buf[e, pl.ds(TOP, 1)]
            buf[e, pl.ds(TOP + NY, 1)] = buf[e, pl.ds(TOP + NY - 1, 1)]
        G[e, pl.ds(TOP - 1, 1)] = G[e, pl.ds(TOP, 1)]
        G[e, pl.ds(TOP + NY, 1)] = G[e, pl.ds(TOP + NY - 1, 1)]
        for buf, wall in ((U, 2.0), (V, 0.0), (W, 0.0)):
            buf[e, pl.ds(TOP - 1, 1)] = wall - buf[e, pl.ds(TOP, 1)]
            buf[e, pl.ds(TOP + NY, 1)] = -buf[e, pl.ds(TOP + NY - 1, 1)]
        return carry

    lax.fori_loop(0, 12, shift_fraction, 0)

    def cells(e, y, components):
        lane = lanes(8)
        at_low = lane == 0
        at_high = lane == 127
        here, up, down = pl.ds(y + TOP, 8), pl.ds(y + TOP + 1, 8), pl.ds(y + TOP - 1, 8)
        ends_all = Z[pl.ds(y, 8), :]

        def star(buf, k):
            centre = buf[e, here]
            ends = pltpu.roll(ends_all, 128 - 2 * (12 * k + e) - 1, 1)
            behind = jnp.where(at_low, ends, pltpu.roll(centre, 1, 1))
            ahead = jnp.where(at_high, ends, pltpu.roll(centre, 127, 1))
            return centre, (
                (buf[e + 1, here], buf[e - 1, here]),
                (buf[e, up], buf[e, down]),
                (ahead, behind),
            )

        c = F[e, here]
        around = ((F[e + 1, here], F[e - 1, here]), (F[e, up], F[e, down]), (FP[e, here], FM[e, here]))
        d = [p - m for p, m in around]
        second = [p + m - 2.0 * c for p, m in around]
        mxy = (F[e + 1, up] - F[e + 1, down]) - (F[e - 1, up] - F[e - 1, down])
        mxz = (FP[e + 1, here] - FM[e + 1, here]) - (FP[e - 1, here] - FM[e - 1, here])
        myz = (FP[e, up] - FM[e, up]) - (FP[e, down] - FM[e, down])
        dd = [v * v for v in d]
        inverse = lax.rsqrt(jnp.maximum(dd[0] + dd[1] + dd[2], 1.0))
        bend = (dd[0] * second[0] + dd[1] * second[1] + dd[2] * second[2]) + 0.5 * (
            d[0] * (d[1] * mxy + d[2] * mxz) + d[1] * d[2] * myz
        )
        laplace = second[0] + second[1] + second[2]
        volume = 1.0 / (0.5 + 0.5 * c)
        pull = (bend * (inverse * inverse) - laplace) * (0.5 * inverse) * volume
        nu = (0.02 + 0.03 * c) * volume
        if len(components) == 3:
            stars = [star(buf, k) for k, buf in enumerate((U, V, W))]
            centres = [s[0] for s in stars]
        else:
            stars = [star(U, 0)]
            centres = [stars[0][0], V[e, here], W[e, here]]
        speeds = [jnp.abs(v) for v in centres]
        if len(components) == 3:
            guesses = star(G, 4)[1]
        else:
            guesses = ((G[e + 1, here], G[e - 1, here]),)
        lift = 2.0 - volume
        out = []
        for k in components:
            centre, sides_ = stars[k]
            twice = 2.0 * centre
            transport = 0.0
            diffusion = 0.0
            for a in range(3):
                p, m = sides_[a]
                curve = p + m - twice
                transport = transport + (centres[a] * (p - m) - speeds[a] * curve)
                diffusion = diffusion + curve
            change = nu * diffusion + pull * d[k] - 0.5 * transport
            p, m = guesses[k]
            out.append(centre + 0.1 * (change + 0.5 * (lift * (p - m))))
        if len(components) == 1:
            return out
        net = 0.0
        for a in range(3):
            p, m = stars[a][1][a]
            fp, fm = around[a]
            ahead = centres[a] + p
            behind = centres[a] + m
            net = net + (
                (jnp.maximum(ahead, 0.0) - jnp.minimum(behind, 0.0)) * c
                + (jnp.minimum(ahead, 0.0) * fp - jnp.maximum(behind, 0.0) * fm)
            )
        return out + [c - 0.05 * net]

    def block(i, carry):
        x = i // 16
        y = pl.multiple_of((i % 16) * 8, 8)
        u, v, w, f = cells(x + 2, y, (0, 1, 2))
        rows = pl.ds(y, 8)
        mid[0, x, rows] = u
        mid[1, x, rows] = v
        mid[2, x, rows] = w
        frac_new[x, rows] = f
        return carry

    lax.fori_loop(0, 16 * NX, block, 0)

    def end_block(i, carry):
        side = i // 16
        y = pl.multiple_of((i % 16) * 8, 8)
        (u,) = cells(1 + 9 * side, y, (0,))
        end_mid[side, pl.ds(y, 8)] = u
        return carry

    lax.fori_loop(0, 32, end_block, 0)

    lane = lanes(NY)
    row = lax.broadcasted_iota(jnp.int32, (NY, 128), 0)
    pack[...] = jnp.zeros((NY, 128), F32)
    for x in range(NX):
        before = mid[0, x - 1] if x > 0 else end_mid[0]
        after = mid[0, x + 1] if x < NX - 1 else end_mid[1]
        v = mid[1, x]
        w = mid[2, x]
        v_up = jnp.where(row == NY - 1, 0.0, pltpu.roll(v, NY - 1, 0))
        v_down = jnp.where(row == 0, 0.0, pltpu.roll(v, 1, 0))
        w_up = jnp.where(lane == NZ - 1, 0.0, pltpu.roll(w, NZ - 1, 1))
        w_down = jnp.where(lane == 0, 0.0, pltpu.roll(w, 1, 1))
        s = 2.5 * ((after - before) + (v_up - v_down) + (w_up - w_down))
        source[x] = s
        part = jnp.dot(s, moments[0], precision=HIGHEST, preferred_element_type=F32) + jnp.dot(
            w, moments[1], precision=HIGHEST, preferred_element_type=F32
        )
        pack[...] += pltpu.roll(part, 16 * x, 1) if x else part


def combine_body(a, b, c, d, table, out):
    total = 0.0
    for k, ref in enumerate((a, b, c, d)):
        total = total + jnp.dot(ref[...], table[k], precision=HIGHEST, preferred_element_type=F32)
    out[...] = total


def solve_body(more, *refs):
    (flags, mid, frac, now, source, low, high, far, far_low, far_high, table) = refs[:11]
    vel, pressure = refs[11:13]
    U, Q, lhs = refs[-3:]
    if more:
        right, left, packed, guess = refs[13:17]
    first = flags[0] == 1
    last = flags[1] == 1
    halo = POWERS

    def terms(plane, values, moments, start):
        lane = lanes(NY)
        head = values.astype(BF16)
        tail = (values - head.astype(F32)).astype(BF16)
        m_head = moments.astype(BF16).astype(F32)
        m_tail = moments - m_head
        side = jnp.where(
            lane < 16,
            m_head,
            jnp.where(
                lane < 32,
                pltpu.roll(m_tail, 16, 1),
                jnp.where(lane < 48, pltpu.roll(m_head, 32, 1), 0.0),
            ),
        )
        lhs[:, 0:128] = head
        lhs[:, 128:256] = tail
        lhs[:, 256:384] = head
        lhs[:, 384:512] = side.astype(BF16)
        left_side = lhs[...]
        for kind, out in enumerate((U, Q)):
            base = kind * POWERS * 128
            result = jnp.dot(
                left_side,
                table[:, base + start * 128 : base + POWERS * 128],
                preferred_element_type=F32,
            )
            for m in range(start, POWERS):
                out[m, plane, pl.ds(TOP, NY)] = result[:, (m - start) * 128 : (m - start + 1) * 128]
                ghosts(out, m, plane)

    def ghosts(out, m, plane):
        out[m, plane, pl.ds(TOP - 1, 1)] = out[m, plane, pl.ds(TOP, 1)]
        out[m, plane, pl.ds(TOP + NY, 1)] = out[m, plane, pl.ds(TOP + NY - 1, 1)]

    def own_plane(x, carry):
        moments = pltpu.roll(far[...], (128 - 16 * x) % 128, 1)
        terms(x + halo, source[x], moments, 0)
        return carry

    lax.fori_loop(0, NX, own_plane, 0)
    for k in range(1, halo + 1):
        x = NX - k
        moments = pltpu.roll(far_low[...], (128 - 16 * x) % 128, 1)
        terms(halo - k, low[x], moments, k - 1)
        x = k - 1
        moments = pltpu.roll(far_high[...], (128 - 16 * x) % 128, 1)
        terms(halo + NX - 1 + k, high[x], moments, k - 1)

    for m in range(POWERS - 2, -1, -1):
        for out, extra in ((U, 1), (Q, 0)):
            reach = m + extra

            def sweep(plane, carry, out=out, m=m):
                inside = ((plane >= halo) | jnp.logical_not(first)) & (
                    (plane < halo + NX) | jnp.logical_not(last)
                )
                keep = jnp.where(inside, 1.0, 0.0).astype(F32)
                for y in range(0, NY, 32):
                    here = pl.ds(TOP + y, 32)
                    beside = (out[m + 1, plane - 1, here] + out[m + 1, plane + 1, here]) + (
                        out[m + 1, plane, pl.ds(TOP + y - 1, 32)]
                        + out[m + 1, plane, pl.ds(TOP + y + 1, 32)]
                    )
                    out[m, plane, here] += keep * beside
                ghosts(out, m, plane)
                return carry

            lax.fori_loop(halo - reach, halo + NX + reach, sweep, 0)

    def correct(x, carry):
        plane = x + halo
        for y in range(0, NY, 32):
            here = pl.ds(TOP + y, 32)
            rows = pl.ds(y, 32)
            p = -U[0, plane, here]
            pressure[x, rows] = p
            vel[0, x, rows] = mid[0, x, rows] + 0.1 * (U[0, plane + 1, here] - U[0, plane - 1, here])
            vel[1, x, rows] = mid[1, x, rows] + 0.1 * (
                U[0, plane, pl.ds(TOP + y + 1, 32)] - U[0, plane, pl.ds(TOP + y - 1, 32)]
            )
            vel[2, x, rows] = mid[2, x, rows] + 0.2 * Q[0, plane, here]
            if more:
                guess[x, rows] = 2.0 * p - now[x, rows]
        return carry

    lax.fori_loop(0, NX, correct, 0)
    if more:
        emit_faces(vel, frac, guess, right, left, packed)


def shape(*dims):
    return jax.ShapeDtypeStruct(dims, F32)


IN_VMEM = pl.BlockSpec(memory_space=pltpu.VMEM)
IN_SMEM = pl.BlockSpec(memory_space=pltpu.SMEM)
ANYWHERE = pl.BlockSpec(memory_space=pl.ANY)
PARAMS = pltpu.CompilerParams(vmem_limit_bytes=VMEM_LIMIT)
BLOCK = (NX, NY, NZ)


def pack_call(velocity, fraction, now, old):
    return pl.pallas_call(
        pack_body,
        out_shape=(shape(*BLOCK), shape(*BLOCK), shape(NY, 128), shape(*BLOCK)),
        in_specs=[IN_VMEM] * 4,
        out_specs=(IN_VMEM,) * 4,
        compiler_params=PARAMS,
        name="pack",
    )(velocity, fraction, now, old)


def predict_call(flags, velocity, fraction, guess, low, high, sides, sides_low, sides_high, profile, moments):
    padded = pltpu.VMEM((12, ROWS, NZ), F32)
    return pl.pallas_call(
        predict_body,
        out_shape=(shape(3, *BLOCK), shape(*BLOCK), shape(*BLOCK), shape(NY, 128)),
        in_specs=[IN_SMEM] + [ANYWHERE] * 5 + [IN_VMEM] * 5,
        out_specs=(IN_VMEM,) * 4,
        scratch_shapes=[padded] * 7
        + [
            pltpu.VMEM((NY, 128), F32),
            pltpu.VMEM((2, NY, NZ), F32),
            pltpu.SemaphoreType.DMA((15,)),
        ],
        compiler_params=PARAMS,
        name="predict",
    )(flags, velocity, fraction, guess, low, high, sides, sides_low, sides_high, profile, moments)


def combine_call(packs, table):
    return pl.pallas_call(
        combine_body,
        out_shape=shape(NY, 128),
        in_specs=[IN_VMEM] * 5,
        out_specs=IN_VMEM,
        compiler_params=PARAMS,
        name="combine",
    )(*packs, table)


def solve_call(more, flags, mid, frac, now, source, low, high, far, far_low, far_high, table):
    outs = [shape(3, *BLOCK), shape(*BLOCK)]
    if more:
        outs += [shape(*BLOCK), shape(*BLOCK), shape(NY, 128), shape(*BLOCK)]
    planes = NX + 2 * POWERS
    return pl.pallas_call(
        functools.partial(solve_body, more),
        out_shape=tuple(outs),
        in_specs=[IN_SMEM] + [IN_VMEM] * 10,
        out_specs=(IN_VMEM,) * len(outs),
        scratch_shapes=[
            pltpu.VMEM((POWERS, planes, ROWS, NZ), F32),
            pltpu.VMEM((POWERS, planes, ROWS, NZ), F32),
            pltpu.VMEM((NY, 512), BF16),
        ],
        compiler_params=PARAMS,
        name="solve",
    )(flags, mid, frac, now, source, low, high, far, far_low, far_high, table)


def per_device(velocity, fraction, pressure_now, pressure_old, inflow):
    stream = lax.axis_index("stream")
    count = lax.axis_size("stream")
    flags = jnp.stack([stream == 0, stream == count - 1]).astype(jnp.int32)
    forward = [(i, i + 1) for i in range(count - 1)]
    backward = [(i + 1, i) for i in range(count - 1)]

    def along(block, step):
        return lax.ppermute(block, "stream", forward if step > 0 else backward)

    def around(block, offset):
        return lax.ppermute(
            block, "span", [((i + offset) % BLOCKS, i) for i in range(BLOCKS)]
        )

    profile = jnp.broadcast_to(inflow[:, :, None], (2, NY, NZ))
    odd = lanes(NY) % 2 == 1
    moments = jnp.asarray(moment_table())
    combine = jnp.asarray(combine_table())
    table = jnp.asarray(solve_table())

    right, left, packed, guess = pack_call(velocity, fraction, pressure_now, pressure_old)
    now = pressure_now
    for step in range(STEPS):
        more = step < STEPS - 1
        low = along(right, 1)
        high = along(left, -1)
        sides = jnp.where(odd, around(packed, -1), jnp.roll(around(packed, 1), -2, axis=1))
        sides_low = along(sides, 1)
        sides_high = along(sides, -1)
        mid, fraction, source, pack = predict_call(
            flags, velocity, fraction, guess, low, high, sides, sides_low, sides_high, profile, moments
        )
        source_low = along(source, 1)
        source_high = along(source, -1)
        far = combine_call([pack] + [around(pack, o) for o in (1, 2, 3)], combine)
        far_low = along(far, 1)
        far_high = along(far, -1)
        results = solve_call(
            more, flags, mid, fraction, now, source, source_low, source_high, far, far_low, far_high, table
        )
        velocity, pressure = results[:2]
        old, now = now, pressure
        if more:
            right, left, packed, guess = results[2:]
    return (velocity, fraction, now, old)


def solution(mesh):
    return jax.shard_map(
        per_device,
        mesh=mesh,
        in_specs=(
            P(None, "stream", None, "span"),
            P("stream", None, "span"),
            P("stream", None, "span"),
            P("stream", None, "span"),
            P(),
        ),
        out_specs=(
            P(None, "stream", None, "span"),
            P("stream", None, "span"),
            P("stream", None, "span"),
            P("stream", None, "span"),
        ),
        check_vma=False,
    )
```

```python
import functools
import math

import jax
import jax.numpy as jnp
import numpy as np
from jax import lax
from jax.experimental import pallas as pl
from jax.experimental.pallas import tpu as pltpu
from jax.sharding import PartitionSpec as P

STEPS = 2
POWERS = 7
NX, NY, NZ = 8, 128, 128
TOP = 8
ROWS = NY + 2 * TOP
BLOCKS = 4
F32 = jnp.float32
BF16 = jnp.bfloat16
HIGHEST = lax.Precision.HIGHEST
MIB = 1024 * 1024


def comb(n, k):
    return math.comb(n, k) if 0 <= k <= n else 0


RATIO = 3.0 - 2.0 * math.sqrt(2.0)


def line_kernel(power, n):
    return RATIO ** (power + n) * sum(
        comb(power - 1 + n + k, power - 1) * comb(power - 1 + k, power - 1) * RATIO ** (2 * k)
        for k in range(40)
    )


def far_kernel(power, j, z):
    return RATIO ** (power + 1 + z) * sum(
        comb(power - 1 + k, power - 1) * RATIO ** (2 * k) * comb(power + z + k, power - 1 - j)
        for k in range(40)
    )


@functools.cache
def solve_table():
    near = np.zeros((POWERS, 144, NZ + 2))
    for m in range(POWERS):
        kernel = np.array([line_kernel(m + 1, n) for n in range(NZ + 2)])
        z = np.arange(-1, NZ + 1)
        own = np.arange(NZ)
        near[m, :NZ] = kernel[np.abs(z[None, :] - own[:, None])]
        far = np.array([[far_kernel(m + 1, j, t) for t in z] for j in range(POWERS)])
        near[m, NZ : NZ + POWERS] = far
        near[m, NZ + POWERS : NZ + 2 * POWERS] = far[:, ::-1]
        near[m, NZ + 14] = -2.5 * near[m, 0]
        near[m, NZ + 15] = 2.5 * near[m, NZ - 1]
    wide = np.zeros((144, (POWERS + 1) * NZ))
    wide[:, : POWERS * NZ] = near[:, :, 1:-1].transpose(1, 0, 2).reshape(144, POWERS * NZ)
    for m in range(POWERS):
        wide[:, POWERS * NZ + 2 * m] = near[m, :, -1]
        wide[:, POWERS * NZ + 2 * m + 1] = near[m, :, 0]
    wide = wide.astype(np.float32)
    head = wide.astype(jnp.bfloat16)
    tail = (wide - head.astype(np.float32)).astype(jnp.bfloat16)
    table = np.zeros((512, wide.shape[1]), jnp.bfloat16)
    table[0:128] = head[:NZ]
    table[128:256] = head[:NZ]
    table[256:384] = tail[:NZ]
    table[384:400] = head[NZ:]
    table[400:416] = head[NZ:]
    table[416:432] = tail[NZ:]
    return table


@functools.cache
def moment_table():
    table = np.zeros((2, NZ, 128), np.float32)
    for z in range(NZ):
        for j in range(POWERS):
            table[0, z, j] = comb(z, j) * RATIO**z
            table[0, z, POWERS + j] = comb(NZ - 1 - z, j) * RATIO ** (NZ - 1 - z)
    table[1, 0, 14] = 1.0
    table[1, NZ - 1, 15] = 1.0
    return table


@functools.cache
def combine_table():
    small = np.zeros((BLOCKS, 16, 16))
    end = [comb(NZ - 1, a) * RATIO ** (NZ - 1) for a in range(POWERS)]
    for o in range(1, 2 * BLOCKS + 1):
        gap = NZ * (o - 1)
        for j in range(POWERS):
            for a in range(j + 1):
                factor = comb(gap, j - a) * RATIO**gap
                left = -o
                small[left % BLOCKS, POWERS + a, j] += factor
                small[(left - 1) % BLOCKS, 15, j] += factor * end[a] * -2.5
                small[(left + 1) % BLOCKS, 14, j] += factor * (2.5 if a == 0 else 0.0)
                right = o
                small[right % BLOCKS, a, POWERS + j] += factor
                small[(right - 1) % BLOCKS, 15, POWERS + j] += factor * (-2.5 if a == 0 else 0.0)
                small[(right + 1) % BLOCKS, 14, POWERS + j] += factor * end[a] * 2.5
    small[-1 % BLOCKS, 15, 14] += 1.0
    small[1 % BLOCKS, 14, 15] += 1.0
    table = np.zeros((BLOCKS, 128, 128), np.float32)
    for x in range(NX):
        table[:, 16 * x : 16 * x + 16, 16 * x : 16 * x + 16] = small
    return table


def lanes(rows):
    return lax.broadcasted_iota(jnp.int32, (rows, 128), 1)


def pack_columns(fields):
    lane = lanes(NY)
    packed = jnp.zeros((NY, 128), F32)
    for k in range(5):
        for x in range(NX):
            pair = 12 * k + x + 2
            keep = (lane == 2 * pair + 1) | (lane == 2 * pair + 2)
            packed = jnp.where(keep, pltpu.roll(fields(k, x), 2 * pair + 2, 1), packed)
    return packed


def pack_body(flags, vel, frac, now, old, paired, other, packed, guess):
    for x in range(NX):
        guess[x] = 2.0 * now[x] - old[x]
    emit_faces(flags, vel, frac, guess, paired, other, packed)


def emit_faces(flags, vel, frac, guess, paired, other, packed):
    even = flags[2] == 1
    for out, upper in ((paired, even), (other, jnp.logical_not(even))):
        two = jnp.where(upper, NX - 2, 0)
        one = jnp.where(upper, NX - 1, 0)
        for k in range(2):
            out[k] = vel[0, two + k]
            out[4 + k] = frac[two + k]
            out[6 + k] = guess[two + k]
        out[2] = vel[1, one]
        out[3] = vel[2, one]

    def field(k, x):
        return vel[k, x] if k < 3 else (frac[x] if k == 3 else guess[x])

    packed[...] = pack_columns(field)


def predict_body(
    flags, vel, frac, guess, paired, other, sides, profile, moments,
    mid, frac_new, source, pack,
    U, V, W, F, G, FM, FP, Z, Z_ends, end_mid, sem,
):
    own = pl.ds(TOP, NY)
    copies = []

    def fetch(src, dst):
        copy = pltpu.make_async_copy(src, dst, sem.at[len(copies)])
        copy.start()
        copies.append(copy)

    for k, buf in enumerate((U, V, W)):
        fetch(vel.at[k], buf.at[pl.ds(2, NX), own])
    fetch(frac, F.at[pl.ds(2, NX), own])
    fetch(guess, G.at[pl.ds(2, NX), own])
    even = flags[2] == 1
    for msg, upper in ((paired, even), (other, jnp.logical_not(even))):
        far = jnp.where(upper, 10, 0)
        near = jnp.where(upper, 10, 1)
        fetch(msg.at[pl.ds(0, 2)], U.at[pl.ds(far, 2), own])
        fetch(msg.at[2], V.at[near, own])
        fetch(msg.at[3], W.at[near, own])
        fetch(msg.at[pl.ds(4, 2)], F.at[pl.ds(far, 2), own])
        fetch(msg.at[pl.ds(6, 2)], G.at[pl.ds(far, 2), own])
        fetch(msg.at[8], Z_ends.at[jnp.where(upper, 1, 0)])
    for copy in copies:
        copy.wait()

    first = flags[0] == 1
    last = flags[1] == 1
    lane = lanes(NY)
    place = lane // 2
    slot = place % 12
    group = place // 12
    merged = sides[...]
    below = pltpu.roll(Z_ends[0], 112, 1)
    above = pltpu.roll(Z_ends[1], 16, 1)
    below_wall = jnp.where(group == 0, profile[0], jnp.where(group == 3, profile[1], 0.0))
    above_wall = jnp.where(slot == 10, pltpu.roll(merged, 2, 1), pltpu.roll(merged, 4, 1))
    below = jnp.where(first, below_wall, below)
    above = jnp.where(last, above_wall, above)
    Z[...] = jnp.where(slot < 2, below, jnp.where(slot >= 10, above, merged))

    @pl.when(first)
    def _():
        for e in range(2):
            U[e, own] = profile[0]
            F[e, own] = profile[1]

    @pl.when(last)
    def _():
        for e in (10, 11):
            U[e, own] = U[9, own]
            F[e, own] = F[9, own]
        V[10, own] = V[9, own]
        W[10, own] = W[9, own]

    def shift_fraction(e, carry):
        lane = lanes(NY)
        centre = F[e, own]
        ends = pltpu.roll(Z[...], 128 - 2 * (36 + e) - 1, 1)
        FM[e, own] = jnp.where(lane == 0, ends, pltpu.roll(centre, 1, 1))
        FP[e, own] = jnp.where(lane == 127, ends, pltpu.roll(centre, 127, 1))
        for buf in (F, FM, FP):
            buf[e, pl.ds(TOP - 1, 1)] = buf[e, pl.ds(TOP, 1)]
            buf[e, pl.ds(TOP + NY, 1)] = buf[e, pl.ds(TOP + NY - 1, 1)]
        G[e, pl.ds(TOP - 1, 1)] = G[e, pl.ds(TOP, 1)]
        G[e, pl.ds(TOP + NY, 1)] = G[e, pl.ds(TOP + NY - 1, 1)]
        for buf, wall in ((U, 2.0), (V, 0.0), (W, 0.0)):
            buf[e, pl.ds(TOP - 1, 1)] = wall - buf[e, pl.ds(TOP, 1)]
            buf[e, pl.ds(TOP + NY, 1)] = -buf[e, pl.ds(TOP + NY - 1, 1)]
        return carry

    lax.fori_loop(0, 12, shift_fraction, 0)

    def cells(e, y, components):
        lane = lanes(8)
        at_low = lane == 0
        at_high = lane == 127
        here, up, down = pl.ds(y + TOP, 8), pl.ds(y + TOP + 1, 8), pl.ds(y + TOP - 1, 8)
        ends_all = Z[pl.ds(y, 8), :]

        def star(buf, k):
            centre = buf[e, here]
            ends = pltpu.roll(ends_all, 128 - 2 * (12 * k + e) - 1, 1)
            behind = jnp.where(at_low, ends, pltpu.roll(centre, 1, 1))
            ahead = jnp.where(at_high, ends, pltpu.roll(centre, 127, 1))
            return centre, (
                (buf[e + 1, here], buf[e - 1, here]),
                (buf[e, up], buf[e, down]),
                (ahead, behind),
            )

        c = F[e, here]
        around = ((F[e + 1, here], F[e - 1, here]), (F[e, up], F[e, down]), (FP[e, here], FM[e, here]))
        d = [p - m for p, m in around]
        second = [p + m - 2.0 * c for p, m in around]
        mxy = (F[e + 1, up] - F[e + 1, down]) - (F[e - 1, up] - F[e - 1, down])
        mxz = (FP[e + 1, here] - FM[e + 1, here]) - (FP[e - 1, here] - FM[e - 1, here])
        myz = (FP[e, up] - FM[e, up]) - (FP[e, down] - FM[e, down])
        dd = [v * v for v in d]
        inverse = lax.rsqrt(jnp.maximum(dd[0] + dd[1] + dd[2], 1.0))
        bend = (dd[0] * second[0] + dd[1] * second[1] + dd[2] * second[2]) + 0.5 * (
            d[0] * (d[1] * mxy + d[2] * mxz) + d[1] * d[2] * myz
        )
        laplace = second[0] + second[1] + second[2]
        volume = 1.0 / (0.5 + 0.5 * c)
        pull = (bend * (inverse * inverse) - laplace) * (0.5 * inverse) * volume
        nu = (0.02 + 0.03 * c) * volume
        if len(components) == 3:
            stars = [star(buf, k) for k, buf in enumerate((U, V, W))]
            centres = [s[0] for s in stars]
        else:
            stars = [star(U, 0)]
            centres = [stars[0][0], V[e, here], W[e, here]]
        speeds = [jnp.abs(v) for v in centres]
        if len(components) == 3:
            guesses = star(G, 4)[1]
        else:
            guesses = ((G[e + 1, here], G[e - 1, here]),)
        lift = 2.0 - volume
        out = []
        for k in components:
            centre, sides_ = stars[k]
            twice = 2.0 * centre
            transport = 0.0
            diffusion = 0.0
            for a in range(3):
                p, m = sides_[a]
                curve = p + m - twice
                transport = transport + (centres[a] * (p - m) - speeds[a] * curve)
                diffusion = diffusion + curve
            change = nu * diffusion + pull * d[k] - 0.5 * transport
            p, m = guesses[k]
            out.append(centre + 0.1 * (change + 0.5 * (lift * (p - m))))
        if len(components) == 1:
            return out
        net = 0.0
        for a in range(3):
            p, m = stars[a][1][a]
            fp, fm = around[a]
            ahead = centres[a] + p
            behind = centres[a] + m
            net = net + (
                (jnp.maximum(ahead, 0.0) - jnp.minimum(behind, 0.0)) * c
                + (jnp.minimum(ahead, 0.0) * fp - jnp.maximum(behind, 0.0) * fm)
            )
        return out + [c - 0.05 * net]

    def block(i, carry):
        x = i // 16
        y = pl.multiple_of((i % 16) * 8, 8)
        u, v, w, f = cells(x + 2, y, (0, 1, 2))
        rows = pl.ds(y, 8)
        mid[0, x, rows] = u
        mid[1, x, rows] = v
        mid[2, x, rows] = w
        frac_new[x, rows] = f
        return carry

    lax.fori_loop(0, 16 * NX, block, 0, unroll=4)

    def end_block(i, carry):
        side = i // 16
        y = pl.multiple_of((i % 16) * 8, 8)
        (u,) = cells(1 + 9 * side, y, (0,))
        end_mid[side, pl.ds(y, 8)] = u
        return carry

    lax.fori_loop(0, 32, end_block, 0, unroll=4)

    lane = lanes(NY)
    row = lax.broadcasted_iota(jnp.int32, (NY, 128), 0)
    pack[...] = jnp.zeros((NY, 128), F32)
    for x in range(NX):
        before = mid[0, x - 1] if x > 0 else end_mid[0]
        after = mid[0, x + 1] if x < NX - 1 else end_mid[1]
        v = mid[1, x]
        w = mid[2, x]
        v_up = jnp.where(row == NY - 1, 0.0, pltpu.roll(v, NY - 1, 0))
        v_down = jnp.where(row == 0, 0.0, pltpu.roll(v, 1, 0))
        w_up = jnp.where(lane == NZ - 1, 0.0, pltpu.roll(w, NZ - 1, 1))
        w_down = jnp.where(lane == 0, 0.0, pltpu.roll(w, 1, 1))
        s = 2.5 * ((after - before) + (v_up - v_down) + (w_up - w_down))
        source[x] = s
        part = jnp.dot(s, moments[0], precision=HIGHEST, preferred_element_type=F32) + jnp.dot(
            w, moments[1], precision=HIGHEST, preferred_element_type=F32
        )
        pack[...] += pltpu.roll(part, 16 * x, 1) if x else part


def combine_body(a, b, c, d, table, _, message, out, sem):
    total = 0.0
    for k, ref in enumerate((a, b, c, d)):
        total = total + jnp.dot(ref[...], table[k], precision=HIGHEST, preferred_element_type=F32)
    out[...] = total
    copy = pltpu.make_async_copy(out, message.at[NX], sem)
    copy.start()
    copy.wait()


def merge_body(before, after, _, __, right, left, out, sem):
    lane = lanes(NY)
    out[...] = jnp.where(lane % 2 == 1, before[...], pltpu.roll(after[...], 126, 1))
    copies = [pltpu.make_async_copy(out, m.at[NX], sem.at[k]) for k, m in enumerate((right, left))]
    for copy in copies:
        copy.start()
    for copy in copies:
        copy.wait()


def solve_body(more, *refs):
    (flags, mid, frac, now, source, paired, other, far, table) = refs[:9]
    vel, pressure = refs[9:11]
    U, E, lhs = refs[-3:]
    if more:
        faces_paired, faces_other, packed, guess = refs[11:15]
    first = flags[0] == 1
    last = flags[1] == 1
    halo = POWERS

    def terms(plane, values, moments, start):
        lane = lanes(NY)
        head = values.astype(BF16)
        tail = (values - head.astype(F32)).astype(BF16)
        m_head = moments.astype(BF16).astype(F32)
        m_tail = moments - m_head
        side = jnp.where(
            lane < 16,
            m_head,
            jnp.where(
                lane < 32,
                pltpu.roll(m_tail, 16, 1),
                jnp.where(lane < 48, pltpu.roll(m_head, 32, 1), 0.0),
            ),
        )
        lhs[:, 0:128] = head
        lhs[:, 128:256] = tail
        lhs[:, 256:384] = head
        lhs[:, 384:512] = side.astype(BF16)
        result = jnp.dot(lhs[...], table[:, start * 128 :], preferred_element_type=F32)
        for m in range(start, POWERS):
            U[m, plane, pl.ds(TOP, NY)] = result[:, (m - start) * 128 : (m - start + 1) * 128]
            ghosts(U, m, plane)
        ends = result[:, (POWERS - start) * 128 :]
        group, offset = plane // 8, 16 * (plane % 8)
        E[group] += pltpu.roll(ends, offset, 1)

    def inside(plane):
        kept = ((plane >= halo) | jnp.logical_not(first)) & ((plane < halo + NX) | jnp.logical_not(last))
        return jnp.where(kept, 1.0, 0.0).astype(F32)

    def ghosts(out, m, plane):
        out[m, plane, pl.ds(TOP - 1, 1)] = out[m, plane, pl.ds(TOP, 1)]
        out[m, plane, pl.ds(TOP + NY, 1)] = out[m, plane, pl.ds(TOP + NY - 1, 1)]

    def own_plane(x, carry):
        moments = pltpu.roll(far[...], (128 - 16 * x) % 128, 1)
        terms(x + halo, source[x], moments, 0)
        return carry

    E[...] = jnp.zeros((3, NY, 128), F32)
    lax.fori_loop(0, NX, own_plane, 0)
    even = flags[2] == 1
    for k in range(1, halo + 1):
        for message, upper in ((paired, even), (other, jnp.logical_not(even))):
            x = jnp.where(upper, k - 1, NX - k)
            moments = pltpu.roll(message[NX], (128 - 16 * x) % 128, 1)
            terms(jnp.where(upper, halo + NX - 1 + k, halo - k), message[x], moments, k - 1)

    for m in range(POWERS - 2, -1, -1):
        reach = m + 1

        def sweep(plane, carry, m=m):
            keep = inside(plane)
            for y in range(0, NY, 32):
                here = pl.ds(TOP + y, 32)
                beside = (U[m + 1, plane - 1, here] + U[m + 1, plane + 1, here]) + (
                    U[m + 1, plane, pl.ds(TOP + y - 1, 32)]
                    + U[m + 1, plane, pl.ds(TOP + y + 1, 32)]
                )
                U[m, plane, here] += keep * beside
            ghosts(U, m, plane)
            return carry

        lax.fori_loop(halo - reach, halo + NX + reach, sweep, 0)

    lane = lanes(NY)
    row = lax.broadcasted_iota(jnp.int32, (NY, 128), 0)
    used = lane % 16 < 14
    keeps = []
    for g in range(3):
        plane = 8 * g + lane // 16
        keeps.append(jnp.where(used, inside(plane), 0.0))
    start = [E[g] for g in range(3)]
    ends = start
    for m in range(POWERS - 1):
        before = [pltpu.roll(e, 14, 1) for e in ends]
        after = [pltpu.roll(e, 110, 1) for e in ends]
        same = [pltpu.roll(e, 126, 1) for e in ends]
        updated = []
        for g in range(3):
            behind = jnp.where(lane < 16, before[g - 1], before[g]) if g else before[0]
            ahead = jnp.where(lane >= 112, after[g + 1], after[g]) if g < 2 else after[2]
            up = jnp.where(row == NY - 1, same[g], pltpu.roll(same[g], NY - 1, 0))
            down = jnp.where(row == 0, same[g], pltpu.roll(same[g], 1, 0))
            updated.append(start[g] + keeps[g] * ((behind + ahead) + (up + down)))
        ends = updated
    for g in range(3):
        E[g] = ends[g]

    def correct(x, carry):
        plane = x + halo
        lane = lanes(NY)
        turned = pltpu.roll(E[plane // 8], (128 - 16 * (plane % 8) - 1) % 128, 1)
        centre = U[0, plane, pl.ds(TOP, NY)]
        ahead = jnp.where(lane == NZ - 1, turned, pltpu.roll(centre, NZ - 1, 1))
        behind = jnp.where(lane == 0, turned, pltpu.roll(centre, 1, 1))
        vel[2, x] = mid[2, x] + 0.1 * (ahead - behind)
        for y in range(0, NY, 32):
            here = pl.ds(TOP + y, 32)
            rows = pl.ds(y, 32)
            p = -U[0, plane, here]
            pressure[x, rows] = p
            vel[0, x, rows] = mid[0, x, rows] + 0.1 * (U[0, plane + 1, here] - U[0, plane - 1, here])
            vel[1, x, rows] = mid[1, x, rows] + 0.1 * (
                U[0, plane, pl.ds(TOP + y + 1, 32)] - U[0, plane, pl.ds(TOP + y - 1, 32)]
            )
            if more:
                guess[x, rows] = 2.0 * p - now[x, rows]
        return carry

    lax.fori_loop(0, NX, correct, 0)
    if more:
        emit_faces(flags, vel, frac, guess, faces_paired, faces_other, packed)


def shape(*dims):
    return jax.ShapeDtypeStruct(dims, F32)


IN_VMEM = pl.BlockSpec(memory_space=pltpu.VMEM)
IN_SMEM = pl.BlockSpec(memory_space=pltpu.SMEM)
ANYWHERE = pl.BlockSpec(memory_space=pl.ANY)
BLOCK = (NX, NY, NZ)
MESSAGE = (NX + 1, NY, NZ)


def pack_call(flags, velocity, fraction, now, old):
    return pl.pallas_call(
        pack_body,
        out_shape=(shape(*MESSAGE), shape(*MESSAGE), shape(NY, 128), shape(*BLOCK)),
        in_specs=[IN_SMEM] + [IN_VMEM] * 4,
        out_specs=(IN_VMEM,) * 4,
        compiler_params=pltpu.CompilerParams(vmem_limit_bytes=10 * MIB),
        name="pack",
    )(flags, velocity, fraction, now, old)


def predict_call(flags, velocity, fraction, guess, paired, other, sides, profile, moments):
    padded = pltpu.VMEM((12, ROWS, NZ), F32)
    return pl.pallas_call(
        predict_body,
        out_shape=(shape(3, *BLOCK), shape(*BLOCK), shape(*MESSAGE), shape(NY, 128)),
        in_specs=[IN_SMEM] + [ANYWHERE] * 5 + [IN_VMEM] * 3,
        out_specs=(IN_VMEM,) * 4,
        scratch_shapes=[padded] * 7
        + [
            pltpu.VMEM((NY, 128), F32),
            pltpu.VMEM((2, NY, 128), F32),
            pltpu.VMEM((2, NY, NZ), F32),
            pltpu.SemaphoreType.DMA((17,)),
        ],
        compiler_params=pltpu.CompilerParams(vmem_limit_bytes=18 * MIB),
        name="predict",
    )(flags, velocity, fraction, guess, paired, other, sides, profile, moments)


def combine_call(packs, table, message):
    return pl.pallas_call(
        combine_body,
        out_shape=(shape(*MESSAGE), shape(NY, 128)),
        in_specs=[IN_VMEM] * 5 + [ANYWHERE],
        out_specs=(ANYWHERE, IN_VMEM),
        scratch_shapes=[pltpu.SemaphoreType.DMA],
        input_output_aliases={5: 0},
        compiler_params=pltpu.CompilerParams(vmem_limit_bytes=4 * MIB),
        name="combine",
    )(*packs, table, message)


def merge_call(before, after, right, left):
    return pl.pallas_call(
        merge_body,
        out_shape=(shape(*MESSAGE), shape(*MESSAGE), shape(NY, 128)),
        in_specs=[IN_VMEM] * 2 + [ANYWHERE] * 2,
        out_specs=(ANYWHERE, ANYWHERE, IN_VMEM),
        scratch_shapes=[pltpu.SemaphoreType.DMA((2,))],
        input_output_aliases={2: 0, 3: 1},
        compiler_params=pltpu.CompilerParams(vmem_limit_bytes=4 * MIB),
        name="merge",
    )(before, after, right, left)


def solve_call(more, flags, mid, frac, now, source, paired, other, far, table):
    outs = [shape(3, *BLOCK), shape(*BLOCK)]
    if more:
        outs += [shape(*MESSAGE), shape(*MESSAGE), shape(NY, 128), shape(*BLOCK)]
    planes = NX + 2 * POWERS
    return pl.pallas_call(
        functools.partial(solve_body, more),
        out_shape=tuple(outs),
        in_specs=[IN_SMEM] + [IN_VMEM] * 8,
        out_specs=(IN_VMEM,) * len(outs),
        scratch_shapes=[
            pltpu.VMEM((POWERS, planes, ROWS, NZ), F32),
            pltpu.VMEM((3, NY, 128), F32),
            pltpu.VMEM((NY, 512), BF16),
        ],
        compiler_params=pltpu.CompilerParams(vmem_limit_bytes=24 * MIB),
        name="solve",
    )(flags, mid, frac, now, source, paired, other, far, table)


def per_device(velocity, fraction, pressure_now, pressure_old, inflow):
    stream = lax.axis_index("stream")
    count = lax.axis_size("stream")
    flags = jnp.stack([stream == 0, stream == count - 1, stream % 2 == 0]).astype(jnp.int32)
    pairs = [(i, i ^ 1) for i in range(count)]
    others = [(i, ((i + 1) ^ 1) - 1) for i in range(1, count - 1)]

    def exchange(block, with_pair):
        return lax.ppermute(block, "stream", pairs if with_pair else others)

    def around(block, offset):
        return lax.ppermute(
            block, "span", [((i + offset) % BLOCKS, i) for i in range(BLOCKS)]
        )

    profile = jnp.broadcast_to(inflow[:, :, None], (2, NY, NZ))
    moments = jnp.asarray(moment_table())
    combine = jnp.asarray(combine_table())
    table = jnp.asarray(solve_table())

    paired, other, packed, guess = pack_call(flags, velocity, fraction, pressure_now, pressure_old)
    now = pressure_now
    for step in range(STEPS):
        more = step < STEPS - 1
        paired, other, sides = merge_call(around(packed, -1), around(packed, 1), paired, other)
        other = exchange(other, False)
        paired = exchange(paired, True)
        mid, fraction, source, pack = predict_call(
            flags, velocity, fraction, guess, paired, other, sides, profile, moments
        )
        source, far = combine_call([pack] + [around(pack, o) for o in (1, 2, 3)], combine, source)
        results = solve_call(
            more, flags, mid, fraction, now, source, exchange(source, True), exchange(source, False), far, table
        )
        velocity, pressure = results[:2]
        old, now = now, pressure
        if more:
            paired, other, packed, guess = results[2:]
    return (velocity, fraction, now, old)


def solution(mesh):
    return jax.shard_map(
        per_device,
        mesh=mesh,
        in_specs=(
            P(None, "stream", None, "span"),
            P("stream", None, "span"),
            P("stream", None, "span"),
            P("stream", None, "span"),
            P(),
        ),
        out_specs=(
            P(None, "stream", None, "span"),
            P("stream", None, "span"),
            P("stream", None, "span"),
            P("stream", None, "span"),
        ),
        check_vma=False,
    )
```

```python
import functools
import math

import jax
import jax.numpy as jnp
import numpy as np
from jax import lax
from jax.experimental import pallas as pl
from jax.experimental.pallas import tpu as pltpu
from jax.sharding import PartitionSpec as P

STEPS = 2
POWERS = 7
NX, NY, NZ = 8, 128, 128
TOP = 8
ROWS = NY + 2 * TOP
BLOCKS = 4
F32 = jnp.float32
BF16 = jnp.bfloat16
HIGHEST = lax.Precision.HIGHEST
MIB = 1024 * 1024


def comb(n, k):
    return math.comb(n, k) if 0 <= k <= n else 0


RATIO = 3.0 - 2.0 * math.sqrt(2.0)


def line_kernel(power, n):
    return RATIO ** (power + n) * sum(
        comb(power - 1 + n + k, power - 1) * comb(power - 1 + k, power - 1) * RATIO ** (2 * k)
        for k in range(40)
    )


def far_kernel(power, j, z):
    return RATIO ** (power + 1 + z) * sum(
        comb(power - 1 + k, power - 1) * RATIO ** (2 * k) * comb(power + z + k, power - 1 - j)
        for k in range(40)
    )


@functools.cache
def solve_table():
    near = np.zeros((POWERS, 144, NZ + 2))
    for m in range(POWERS):
        kernel = np.array([line_kernel(m + 1, n) for n in range(NZ + 2)])
        z = np.arange(-1, NZ + 1)
        own = np.arange(NZ)
        near[m, :NZ] = kernel[np.abs(z[None, :] - own[:, None])]
        far = np.array([[far_kernel(m + 1, j, t) for t in z] for j in range(POWERS)])
        near[m, NZ : NZ + POWERS] = far
        near[m, NZ + POWERS : NZ + 2 * POWERS] = far[:, ::-1]
        near[m, NZ + 14] = -2.5 * near[m, 0]
        near[m, NZ + 15] = 2.5 * near[m, NZ - 1]
    wide = np.zeros((144, (POWERS + 1) * NZ))
    wide[:, : POWERS * NZ] = near[:, :, 1:-1].transpose(1, 0, 2).reshape(144, POWERS * NZ)
    for m in range(POWERS):
        wide[:, POWERS * NZ + 2 * m] = near[m, :, -1]
        wide[:, POWERS * NZ + 2 * m + 1] = near[m, :, 0]
    wide = wide.astype(np.float32)
    head = wide.astype(jnp.bfloat16)
    tail = (wide - head.astype(np.float32)).astype(jnp.bfloat16)
    table = np.zeros((512, wide.shape[1]), jnp.bfloat16)
    table[0:128] = head[:NZ]
    table[128:256] = head[:NZ]
    table[256:384] = tail[:NZ]
    table[384:400] = head[NZ:]
    table[400:416] = head[NZ:]
    table[416:432] = tail[NZ:]
    return table


@functools.cache
def moment_table():
    table = np.zeros((2, NZ, 128), np.float32)
    for z in range(NZ):
        for j in range(POWERS):
            table[0, z, j] = comb(z, j) * RATIO**z
            table[0, z, POWERS + j] = comb(NZ - 1 - z, j) * RATIO ** (NZ - 1 - z)
    table[1, 0, 14] = 1.0
    table[1, NZ - 1, 15] = 1.0
    return table


@functools.cache
def combine_table():
    small = np.zeros((BLOCKS, 16, 16))
    end = [comb(NZ - 1, a) * RATIO ** (NZ - 1) for a in range(POWERS)]
    for o in range(1, 2 * BLOCKS + 1):
        gap = NZ * (o - 1)
        for j in range(POWERS):
            for a in range(j + 1):
                factor = comb(gap, j - a) * RATIO**gap
                left = -o
                small[left % BLOCKS, POWERS + a, j] += factor
                small[(left - 1) % BLOCKS, 15, j] += factor * end[a] * -2.5
                small[(left + 1) % BLOCKS, 14, j] += factor * (2.5 if a == 0 else 0.0)
                right = o
                small[right % BLOCKS, a, POWERS + j] += factor
                small[(right - 1) % BLOCKS, 15, POWERS + j] += factor * (-2.5 if a == 0 else 0.0)
                small[(right + 1) % BLOCKS, 14, POWERS + j] += factor * end[a] * 2.5
    small[-1 % BLOCKS, 15, 14] += 1.0
    small[1 % BLOCKS, 14, 15] += 1.0
    table = np.zeros((BLOCKS, 128, 128), np.float32)
    for x in range(NX):
        table[:, 16 * x : 16 * x + 16, 16 * x : 16 * x + 16] = small
    return table


def lanes(rows):
    return lax.broadcasted_iota(jnp.int32, (rows, 128), 1)


def pack_columns(fields):
    lane = lanes(NY)
    packed = jnp.zeros((NY, 128), F32)
    for k in range(5):
        for x in range(NX):
            pair = 12 * k + x + 2
            keep = (lane == 2 * pair + 1) | (lane == 2 * pair + 2)
            packed = jnp.where(keep, pltpu.roll(fields(k, x), 2 * pair + 2, 1), packed)
    return packed


def pack_body(flags, vel, frac, now, old, paired, other, packed, guess):
    for x in range(NX):
        guess[x] = 2.0 * now[x] - old[x]
    emit_faces(flags, vel, frac, guess, paired, other, packed)


def emit_faces(flags, vel, frac, guess, paired, other, packed):
    even = flags[2] == 1
    for out, upper in ((paired, even), (other, jnp.logical_not(even))):
        two = jnp.where(upper, NX - 2, 0)
        one = jnp.where(upper, NX - 1, 0)
        for k in range(2):
            out[k] = vel[0, two + k]
            out[4 + k] = frac[two + k]
            out[6 + k] = guess[two + k]
        out[2] = vel[1, one]
        out[3] = vel[2, one]

    def field(k, x):
        return vel[k, x] if k < 3 else (frac[x] if k == 3 else guess[x])

    packed[...] = pack_columns(field)


def fill_shifts(buffers, ends, planes, slots):
    U, V, W, F, G, FM, FP = buffers
    own = pl.ds(TOP, NY)
    below, above = pl.ds(TOP - 1, 1), pl.ds(TOP + NY, 1)
    bottom, top = pl.ds(TOP, 1), pl.ds(TOP + NY - 1, 1)
    lane = lanes(NY)
    for e, slot in zip(planes, slots):
        centre = F[e, own]
        turned = pltpu.roll(ends, 128 - 2 * (36 + slot) - 1, 1)
        FM[e, own] = jnp.where(lane == 0, turned, pltpu.roll(centre, 1, 1))
        FP[e, own] = jnp.where(lane == 127, turned, pltpu.roll(centre, 127, 1))
        for buf in (F, FM, FP, G):
            buf[e, below] = buf[e, bottom]
            buf[e, above] = buf[e, top]
        for buf, wall in ((U, 2.0), (V, 0.0), (W, 0.0)):
            buf[e, below] = wall - buf[e, bottom]
            buf[e, above] = -buf[e, top]


def cells(low, at, high, Z, e, y, components):
    U, V, W, F, G, FM, FP = range(7)

    def get(plane, k, rows):
        return plane[0][k][plane[1], rows]

    lane = lanes(8)
    at_low = lane == 0
    at_high = lane == 127
    here, up, down = pl.ds(y + TOP, 8), pl.ds(y + TOP + 1, 8), pl.ds(y + TOP - 1, 8)
    ends_all = Z[pl.ds(y, 8), :]

    def star(k, group):
        centre = get(at, k, here)
        ends = pltpu.roll(ends_all, 128 - 2 * (12 * group + e) - 1, 1)
        behind = jnp.where(at_low, ends, pltpu.roll(centre, 1, 1))
        ahead = jnp.where(at_high, ends, pltpu.roll(centre, 127, 1))
        return centre, (
            (get(high, k, here), get(low, k, here)),
            (get(at, k, up), get(at, k, down)),
            (ahead, behind),
        )

    c = get(at, F, here)
    around = ((get(high, F, here), get(low, F, here)), (get(at, F, up), get(at, F, down)), (get(at, FP, here), get(at, FM, here)))
    d = [p - m for p, m in around]
    second = [p + m - 2.0 * c for p, m in around]
    mxy = (get(high, F, up) - get(high, F, down)) - (get(low, F, up) - get(low, F, down))
    mxz = (get(high, FP, here) - get(high, FM, here)) - (get(low, FP, here) - get(low, FM, here))
    myz = (get(at, FP, up) - get(at, FM, up)) - (get(at, FP, down) - get(at, FM, down))
    dd = [v * v for v in d]
    inverse = lax.rsqrt(jnp.maximum(dd[0] + dd[1] + dd[2], 1.0))
    bend = (dd[0] * second[0] + dd[1] * second[1] + dd[2] * second[2]) + 0.5 * (
        d[0] * (d[1] * mxy + d[2] * mxz) + d[1] * d[2] * myz
    )
    laplace = second[0] + second[1] + second[2]
    volume = 1.0 / (0.5 + 0.5 * c)
    pull = (bend * (inverse * inverse) - laplace) * (0.5 * inverse) * volume
    nu = (0.02 + 0.03 * c) * volume
    if len(components) == 3:
        stars = [star(k, k) for k in (U, V, W)]
        centres = [s[0] for s in stars]
    else:
        stars = [star(U, 0)]
        centres = [stars[0][0], get(at, V, here), get(at, W, here)]
    speeds = [jnp.abs(v) for v in centres]
    if len(components) == 3:
        guesses = star(G, 4)[1]
    else:
        guesses = ((get(high, G, here), get(low, G, here)),)
    lift = 2.0 - volume
    out = []
    for k in components:
        centre, sides_ = stars[k]
        twice = 2.0 * centre
        transport = 0.0
        diffusion = 0.0
        for a in range(3):
            p, m = sides_[a]
            curve = p + m - twice
            transport = transport + (centres[a] * (p - m) - speeds[a] * curve)
            diffusion = diffusion + curve
        change = nu * diffusion + pull * d[k] - 0.5 * transport
        p, m = guesses[k]
        out.append(centre + 0.1 * (change + 0.5 * (lift * (p - m))))
    if len(components) == 1:
        return out
    net = 0.0
    for a in range(3):
        p, m = stars[a][1][a]
        fp, fm = around[a]
        ahead = centres[a] + p
        behind = centres[a] + m
        net = net + (
            (jnp.maximum(ahead, 0.0) - jnp.minimum(behind, 0.0)) * c
            + (jnp.minimum(ahead, 0.0) * fp - jnp.maximum(behind, 0.0) * fm)
        )
    return out + [c - 0.05 * net]


def source_plane(x, before, after, mid, mx, moments, source, pack):
    lane = lanes(NY)
    row = lax.broadcasted_iota(jnp.int32, (NY, 128), 0)
    v = mid[1, mx]
    w = mid[2, mx]
    v_up = jnp.where(row == NY - 1, 0.0, pltpu.roll(v, NY - 1, 0))
    v_down = jnp.where(row == 0, 0.0, pltpu.roll(v, 1, 0))
    w_up = jnp.where(lane == NZ - 1, 0.0, pltpu.roll(w, NZ - 1, 1))
    w_down = jnp.where(lane == 0, 0.0, pltpu.roll(w, 1, 1))
    s = 2.5 * ((after - before) + (v_up - v_down) + (w_up - w_down))
    source[x] = s
    part = jnp.dot(s, moments[0], precision=HIGHEST, preferred_element_type=F32) + jnp.dot(
        w, moments[1], precision=HIGHEST, preferred_element_type=F32
    )
    pack[...] += pltpu.roll(part, 16 * x, 1) if x else part


def start_copies(pairs, sem):
    copies = [pltpu.make_async_copy(src, dst, sem.at[k]) for k, (src, dst) in enumerate(pairs)]
    for copy in copies:
        copy.start()
    return copies


def inner_body(vel, frac, guess, sides, moments, *refs):
    buffers = refs[:7]
    mid, frac_new, source, pack, sem = refs[7:]
    U, V, W, F, G = buffers[:5]
    own = pl.ds(TOP, NY)
    sources = [vel.at[0], vel.at[1], vel.at[2], frac, guess]
    copies = start_copies([(src, buf.at[pl.ds(0, NX), own]) for src, buf in zip(sources, (U, V, W, F, G))], sem)
    pack[...] = jnp.zeros((NY, 128), F32)
    for copy in copies:
        copy.wait()
    fill_shifts(buffers, sides[...], range(NX), range(2, 2 + NX))

    def block(i, carry):
        x = 1 + i // 16
        y = pl.multiple_of((i % 16) * 8, 8)
        rows = pl.ds(y, 8)
        mid[0, x, rows], mid[1, x, rows], mid[2, x, rows], frac_new[x, rows] = cells(
            (buffers, x - 1), (buffers, x), (buffers, x + 1), sides, x + 2, y, (0, 1, 2)
        )
        return carry

    lax.fori_loop(0, 16 * (NX - 2), block, 0, unroll=4)
    for x in range(2, NX - 2):
        source_plane(x, mid[0, x - 1], mid[0, x + 1], mid, x, moments, source, pack)


def outer_body(flags, paired, other, sides, profile, moments, *refs):
    given, (given_mid, given_frac, given_source, given_pack) = refs[:7], refs[7:11]
    mid, frac_new, source, pack = refs[11:15]
    buffers = refs[15:22]
    Z, Z_ends, end_mid, sem, keep_sem = refs[22:]
    U, V, W, F, G = buffers[:5]
    own = pl.ds(TOP, NY)
    middle = pl.ds(1, NX - 2)
    kept = [(given_mid.at[k, middle], mid.at[k, middle]) for k in range(3)]
    kept += [(given_frac.at[middle], frac_new.at[middle])]
    kept += [(given_source.at[pl.ds(2, NX - 4)], source.at[pl.ds(2, NX - 4)])]
    kept = start_copies(kept, keep_sem)
    even = flags[2] == 1
    pairs = []
    for msg, upper in ((paired, even), (other, jnp.logical_not(even))):
        far = jnp.where(upper, 2, 0)
        near = jnp.where(upper, 2, 1)
        pairs += [
            (msg.at[pl.ds(0, 2)], U.at[pl.ds(far, 2), own]),
            (msg.at[2], V.at[near, own]),
            (msg.at[3], W.at[near, own]),
            (msg.at[pl.ds(4, 2)], F.at[pl.ds(far, 2), own]),
            (msg.at[pl.ds(6, 2)], G.at[pl.ds(far, 2), own]),
            (msg.at[8], Z_ends.at[jnp.where(upper, 1, 0)]),
        ]
    for copy in start_copies(pairs, sem):
        copy.wait()

    first = flags[0] == 1
    last = flags[1] == 1
    lane = lanes(NY)
    place = lane // 2
    slot = place % 12
    group = place // 12
    merged = sides[...]
    below = pltpu.roll(Z_ends[0], 112, 1)
    above = pltpu.roll(Z_ends[1], 16, 1)
    below_wall = jnp.where(group == 0, profile[0], jnp.where(group == 3, profile[1], 0.0))
    above_wall = jnp.where(slot == 10, pltpu.roll(merged, 2, 1), pltpu.roll(merged, 4, 1))
    below = jnp.where(first, below_wall, below)
    above = jnp.where(last, above_wall, above)
    Z[...] = jnp.where(slot < 2, below, jnp.where(slot >= 10, above, merged))

    @pl.when(first)
    def _():
        for e in range(2):
            U[e, own] = profile[0]
            F[e, own] = profile[1]

    @pl.when(last)
    def _():
        for e in (2, 3):
            U[e, own] = given[0][NX - 1, own]
            F[e, own] = given[3][NX - 1, own]
        V[2, own] = given[1][NX - 1, own]
        W[2, own] = given[2][NX - 1, own]

    fill_shifts(buffers, Z[...], range(4), (0, 1, 10, 11))
    line = [(buffers, 0), (buffers, 1), (given, 0), (given, 1)]
    line_high = [(given, NX - 2), (given, NX - 1), (buffers, 2), (buffers, 3)]

    def block(i, carry):
        y = pl.multiple_of(i * 8, 8)
        rows = pl.ds(y, 8)
        for x, end, planes in ((0, 0, line), (NX - 1, 1, line_high)):
            inner, outer = (planes[1:], planes[:3]) if x == 0 else (planes[:3], planes[1:])
            mid[0, x, rows], mid[1, x, rows], mid[2, x, rows], frac_new[x, rows] = cells(
                *inner, Z, x + 2, y, (0, 1, 2)
            )
            (end_mid[end, rows],) = cells(*outer, Z, 1 + 9 * end, y, (0,))
        return carry

    lax.fori_loop(0, 16, block, 0)
    pack[...] = given_pack[...]
    source_plane(0, end_mid[0], given_mid[0, 1], mid, 0, moments, source, pack)
    source_plane(1, mid[0, 0], given_mid[0, 2], given_mid, 1, moments, source, pack)
    source_plane(6, given_mid[0, 5], mid[0, 7], given_mid, 6, moments, source, pack)
    source_plane(7, given_mid[0, 6], end_mid[1], mid, 7, moments, source, pack)
    for copy in kept:
        copy.wait()


def combine_body(a, b, c, d, table, _, message, out, sem):
    total = 0.0
    for k, ref in enumerate((a, b, c, d)):
        total = total + jnp.dot(ref[...], table[k], precision=HIGHEST, preferred_element_type=F32)
    out[...] = total
    copy = pltpu.make_async_copy(out, message.at[NX], sem)
    copy.start()
    copy.wait()


def merge_body(before, after, _, __, right, left, out, sem):
    lane = lanes(NY)
    out[...] = jnp.where(lane % 2 == 1, before[...], pltpu.roll(after[...], 126, 1))
    copies = [pltpu.make_async_copy(out, m.at[NX], sem.at[k]) for k, m in enumerate((right, left))]
    for copy in copies:
        copy.start()
    for copy in copies:
        copy.wait()


HALO = POWERS


def ghosts(out, m, plane):
    out[m, plane, pl.ds(TOP - 1, 1)] = out[m, plane, pl.ds(TOP, 1)]
    out[m, plane, pl.ds(TOP + NY, 1)] = out[m, plane, pl.ds(TOP + NY - 1, 1)]

def own_plane(x, carry):
    moments = pltpu.roll(far[...], (128 - 16 * x) % 128, 1)
    terms(x + halo, source[x], moments, 0)
    return carry


def terms(table, U, E, lhs, row, plane, values, moments, start):
    lane = lanes(NY)
    head = values.astype(BF16)
    tail = (values - head.astype(F32)).astype(BF16)
    m_head = moments.astype(BF16).astype(F32)
    m_tail = moments - m_head
    side = jnp.where(
        lane < 16,
        m_head,
        jnp.where(
            lane < 32,
            pltpu.roll(m_tail, 16, 1),
            jnp.where(lane < 48, pltpu.roll(m_head, 32, 1), 0.0),
        ),
    )
    lhs[:, 0:128] = head
    lhs[:, 128:256] = tail
    lhs[:, 256:384] = head
    lhs[:, 384:512] = side.astype(BF16)
    result = jnp.dot(lhs[...], table[:, start * 128 :], preferred_element_type=F32)
    for m in range(start, POWERS):
        U[m, row, pl.ds(TOP, NY)] = result[:, (m - start) * 128 : (m - start + 1) * 128]
        ghosts(U, m, row)
    ends = result[:, (POWERS - start) * 128 :]
    group, offset = plane // 8, 16 * (plane % 8)
    E[group] += pltpu.roll(ends, offset, 1)


def own_terms_body(source, far, table, U, E, lhs):
    E[...] = jnp.zeros((3, NY, 128), F32)

    def own_plane(x, carry):
        moments = pltpu.roll(far[...], (128 - 16 * x) % 128, 1)
        terms(table, U, E, lhs, x, x + HALO, source[x], moments, 0)
        return carry

    lax.fori_loop(0, NX, own_plane, 0)


def solve_body(more, *refs):
    (flags, mid, frac, now, paired, other, table, given_U, given_E) = refs[:9]
    vel, pressure = refs[9:11]
    U, E, lhs, sem = refs[-4:]
    if more:
        faces_paired, faces_other, packed, guess = refs[11:15]
    first = flags[0] == 1
    last = flags[1] == 1
    halo = HALO
    fetch = pltpu.make_async_copy(given_U, U.at[:, pl.ds(halo, NX)], sem)
    fetch.start()
    E[...] = given_E[...]

    def inside(plane):
        kept = ((plane >= halo) | jnp.logical_not(first)) & ((plane < halo + NX) | jnp.logical_not(last))
        return jnp.where(kept, 1.0, 0.0).astype(F32)

    even = flags[2] == 1
    for k in range(1, halo + 1):
        for message, upper in ((paired, even), (other, jnp.logical_not(even))):
            x = jnp.where(upper, k - 1, NX - k)
            moments = pltpu.roll(message[NX], (128 - 16 * x) % 128, 1)
            plane = jnp.where(upper, halo + NX - 1 + k, halo - k)
            terms(table, U, E, lhs, plane, plane, message[x], moments, k - 1)

    fetch.wait()
    for m in range(POWERS - 2, -1, -1):
        reach = m + 1

        def sweep(plane, carry, m=m):
            keep = inside(plane)
            for y in range(0, NY, 32):
                here = pl.ds(TOP + y, 32)
                beside = (U[m + 1, plane - 1, here] + U[m + 1, plane + 1, here]) + (
                    U[m + 1, plane, pl.ds(TOP + y - 1, 32)]
                    + U[m + 1, plane, pl.ds(TOP + y + 1, 32)]
                )
                U[m, plane, here] += keep * beside
            ghosts(U, m, plane)
            return carry

        lax.fori_loop(halo - reach, halo + NX + reach, sweep, 0)

    lane = lanes(NY)
    row = lax.broadcasted_iota(jnp.int32, (NY, 128), 0)
    used = lane % 16 < 14
    keeps = []
    for g in range(3):
        plane = 8 * g + lane // 16
        keeps.append(jnp.where(used, inside(plane), 0.0))
    start = [E[g] for g in range(3)]
    ends = start
    for m in range(POWERS - 1):
        before = [pltpu.roll(e, 14, 1) for e in ends]
        after = [pltpu.roll(e, 110, 1) for e in ends]
        same = [pltpu.roll(e, 126, 1) for e in ends]
        updated = []
        for g in range(3):
            behind = jnp.where(lane < 16, before[g - 1], before[g]) if g else before[0]
            ahead = jnp.where(lane >= 112, after[g + 1], after[g]) if g < 2 else after[2]
            up = jnp.where(row == NY - 1, same[g], pltpu.roll(same[g], NY - 1, 0))
            down = jnp.where(row == 0, same[g], pltpu.roll(same[g], 1, 0))
            updated.append(start[g] + keeps[g] * ((behind + ahead) + (up + down)))
        ends = updated
    for g in range(3):
        E[g] = ends[g]

    def correct(x, carry):
        plane = x + halo
        lane = lanes(NY)
        turned = pltpu.roll(E[plane // 8], (128 - 16 * (plane % 8) - 1) % 128, 1)
        centre = U[0, plane, pl.ds(TOP, NY)]
        ahead = jnp.where(lane == NZ - 1, turned, pltpu.roll(centre, NZ - 1, 1))
        behind = jnp.where(lane == 0, turned, pltpu.roll(centre, 1, 1))
        vel[2, x] = mid[2, x] + 0.1 * (ahead - behind)
        for y in range(0, NY, 32):
            here = pl.ds(TOP + y, 32)
            rows = pl.ds(y, 32)
            p = -U[0, plane, here]
            pressure[x, rows] = p
            vel[0, x, rows] = mid[0, x, rows] + 0.1 * (U[0, plane + 1, here] - U[0, plane - 1, here])
            vel[1, x, rows] = mid[1, x, rows] + 0.1 * (
                U[0, plane, pl.ds(TOP + y + 1, 32)] - U[0, plane, pl.ds(TOP + y - 1, 32)]
            )
            if more:
                guess[x, rows] = 2.0 * p - now[x, rows]
        return carry

    lax.fori_loop(0, NX, correct, 0)
    if more:
        emit_faces(flags, vel, frac, guess, faces_paired, faces_other, packed)


def shape(*dims):
    return jax.ShapeDtypeStruct(dims, F32)


IN_VMEM = pl.BlockSpec(memory_space=pltpu.VMEM)
IN_SMEM = pl.BlockSpec(memory_space=pltpu.SMEM)
ANYWHERE = pl.BlockSpec(memory_space=pl.ANY)
BLOCK = (NX, NY, NZ)
MESSAGE = (NX + 1, NY, NZ)


def pack_call(flags, velocity, fraction, now, old):
    return pl.pallas_call(
        pack_body,
        out_shape=(shape(*MESSAGE), shape(*MESSAGE), shape(NY, 128), shape(*BLOCK)),
        in_specs=[IN_SMEM] + [IN_VMEM] * 4,
        out_specs=(IN_VMEM,) * 4,
        compiler_params=pltpu.CompilerParams(vmem_limit_bytes=10 * MIB),
        name="pack",
    )(flags, velocity, fraction, now, old)


PADDED = (NX, ROWS, NZ)
PREDICTED = tuple(shape(*PADDED) for _ in range(7)) + (
    shape(3, *BLOCK),
    shape(*BLOCK),
    shape(*MESSAGE),
    shape(NY, 128),
)


def inner_call(velocity, fraction, guess, sides, moments):
    return pl.pallas_call(
        inner_body,
        out_shape=PREDICTED,
        in_specs=[ANYWHERE] * 3 + [IN_VMEM] * 2,
        out_specs=(IN_VMEM,) * 11,
        scratch_shapes=[pltpu.SemaphoreType.DMA((5,))],
        compiler_params=pltpu.CompilerParams(vmem_limit_bytes=16 * MIB),
        cost_estimate=pl.CostEstimate(flops=20_000_000, bytes_accessed=16_000_000, transcendentals=100_000),
        name="inner",
    )(velocity, fraction, guess, sides, moments)


def outer_call(flags, paired, other, sides, profile, moments, inner):
    return pl.pallas_call(
        outer_body,
        out_shape=PREDICTED[7:],
        in_specs=[IN_SMEM] + [ANYWHERE] * 2 + [IN_VMEM] * 3 + [IN_VMEM] * 8 + [ANYWHERE] * 2 + [IN_VMEM],
        out_specs=(IN_VMEM,) * 4,
        scratch_shapes=[pltpu.VMEM((4, ROWS, NZ), F32)] * 7
        + [
            pltpu.VMEM((NY, 128), F32),
            pltpu.VMEM((2, NY, 128), F32),
            pltpu.VMEM((2, NY, NZ), F32),
            pltpu.SemaphoreType.DMA((12,)),
            pltpu.SemaphoreType.DMA((5,)),
        ],
        compiler_params=pltpu.CompilerParams(vmem_limit_bytes=16 * MIB),
        name="outer",
    )(flags, paired, other, sides, profile, moments, *inner)


def combine_call(packs, table, message):
    return pl.pallas_call(
        combine_body,
        out_shape=(shape(*MESSAGE), shape(NY, 128)),
        in_specs=[IN_VMEM] * 5 + [ANYWHERE],
        out_specs=(ANYWHERE, IN_VMEM),
        scratch_shapes=[pltpu.SemaphoreType.DMA],
        input_output_aliases={5: 0},
        compiler_params=pltpu.CompilerParams(vmem_limit_bytes=4 * MIB),
        name="combine",
    )(*packs, table, message)


def merge_call(before, after, right, left):
    return pl.pallas_call(
        merge_body,
        out_shape=(shape(*MESSAGE), shape(*MESSAGE), shape(NY, 128)),
        in_specs=[IN_VMEM] * 2 + [ANYWHERE] * 2,
        out_specs=(ANYWHERE, ANYWHERE, IN_VMEM),
        scratch_shapes=[pltpu.SemaphoreType.DMA((2,))],
        input_output_aliases={2: 0, 3: 1},
        compiler_params=pltpu.CompilerParams(vmem_limit_bytes=4 * MIB),
        name="merge",
    )(before, after, right, left)


OWN_TERMS = (POWERS, NX, ROWS, NZ)


def own_terms_call(source, far, table):
    return pl.pallas_call(
        own_terms_body,
        out_shape=(shape(*OWN_TERMS), shape(3, NY, 128)),
        in_specs=[IN_VMEM] * 3,
        out_specs=(IN_VMEM,) * 2,
        scratch_shapes=[pltpu.VMEM((NY, 512), BF16)],
        compiler_params=pltpu.CompilerParams(vmem_limit_bytes=20 * MIB),
        cost_estimate=pl.CostEstimate(flops=1_000_000_000, bytes_accessed=12_000_000, transcendentals=0),
        name="own_terms",
    )(source, far, table)


def solve_call(more, flags, mid, frac, now, paired, other, table, own):
    outs = [shape(3, *BLOCK), shape(*BLOCK)]
    if more:
        outs += [shape(*MESSAGE), shape(*MESSAGE), shape(NY, 128), shape(*BLOCK)]
    return pl.pallas_call(
        functools.partial(solve_body, more),
        out_shape=tuple(outs),
        in_specs=[IN_SMEM] + [IN_VMEM] * 6 + [ANYWHERE, IN_VMEM],
        out_specs=(IN_VMEM,) * len(outs),
        scratch_shapes=[
            pltpu.VMEM((POWERS, NX + 2 * HALO, ROWS, NZ), F32),
            pltpu.VMEM((3, NY, 128), F32),
            pltpu.VMEM((NY, 512), BF16),
            pltpu.SemaphoreType.DMA,
        ],
        compiler_params=pltpu.CompilerParams(vmem_limit_bytes=20 * MIB),
        name="solve",
    )(flags, mid, frac, now, paired, other, table, *own)


def per_device(velocity, fraction, pressure_now, pressure_old, inflow):
    stream = lax.axis_index("stream")
    count = lax.axis_size("stream")
    flags = jnp.stack([stream == 0, stream == count - 1, stream % 2 == 0]).astype(jnp.int32)
    pairs = [(i, i ^ 1) for i in range(count)]
    others = [(i, ((i + 1) ^ 1) - 1) for i in range(1, count - 1)]

    def exchange(block, with_pair):
        return lax.ppermute(block, "stream", pairs if with_pair else others)

    def around(block, offset):
        return lax.ppermute(
            block, "span", [((i + offset) % BLOCKS, i) for i in range(BLOCKS)]
        )

    profile = jnp.broadcast_to(inflow[:, :, None], (2, NY, NZ))
    moments = jnp.asarray(moment_table())
    combine = jnp.asarray(combine_table())
    table = jnp.asarray(solve_table())

    paired, other, packed, guess = pack_call(flags, velocity, fraction, pressure_now, pressure_old)
    now = pressure_now
    for step in range(STEPS):
        more = step < STEPS - 1
        paired, other, sides = merge_call(around(packed, -1), around(packed, 1), paired, other)
        other = exchange(other, False)
        paired = exchange(paired, True)
        inner = inner_call(velocity, fraction, guess, sides, moments)
        mid, fraction, source, pack = outer_call(flags, paired, other, sides, profile, moments, inner)
        source, far = combine_call([pack] + [around(pack, o) for o in (1, 2, 3)], combine, source)
        other = exchange(source, False)
        paired = exchange(source, True)
        own = own_terms_call(source, far, table)
        results = solve_call(more, flags, mid, fraction, now, paired, other, table, own)
        velocity, pressure = results[:2]
        old, now = now, pressure
        if more:
            paired, other, packed, guess = results[2:]
    return (velocity, fraction, now, old)


def solution(mesh):
    return jax.shard_map(
        per_device,
        mesh=mesh,
        in_specs=(
            P(None, "stream", None, "span"),
            P("stream", None, "span"),
            P("stream", None, "span"),
            P("stream", None, "span"),
            P(),
        ),
        out_specs=(
            P(None, "stream", None, "span"),
            P("stream", None, "span"),
            P("stream", None, "span"),
            P("stream", None, "span"),
        ),
        check_vma=False,
    )
```

```python
import functools
import math

import jax
import jax.numpy as jnp
import numpy as np
from jax import lax
from jax.experimental import pallas as pl
from jax.experimental.pallas import tpu as pltpu
from jax.sharding import PartitionSpec as P

STEPS = 2
POWERS = 7
NX, NY, NZ = 8, 128, 128
TOP = 8
ROWS = NY + 2 * TOP
BLOCKS = 4
F32 = jnp.float32
BF16 = jnp.bfloat16
HIGHEST = lax.Precision.HIGHEST
MIB = 1024 * 1024


def comb(n, k):
    return math.comb(n, k) if 0 <= k <= n else 0


RATIO = 3.0 - 2.0 * math.sqrt(2.0)


def line_kernel(power, n):
    return RATIO ** (power + n) * sum(
        comb(power - 1 + n + k, power - 1) * comb(power - 1 + k, power - 1) * RATIO ** (2 * k)
        for k in range(40)
    )


def far_kernel(power, j, z):
    return RATIO ** (power + 1 + z) * sum(
        comb(power - 1 + k, power - 1) * RATIO ** (2 * k) * comb(power + z + k, power - 1 - j)
        for k in range(40)
    )


@functools.cache
def solve_table():
    near = np.zeros((POWERS, 144, NZ + 2))
    for m in range(POWERS):
        kernel = np.array([line_kernel(m + 1, n) for n in range(NZ + 2)])
        z = np.arange(-1, NZ + 1)
        own = np.arange(NZ)
        near[m, :NZ] = kernel[np.abs(z[None, :] - own[:, None])]
        far = np.array([[far_kernel(m + 1, j, t) for t in z] for j in range(POWERS)])
        near[m, NZ : NZ + POWERS] = far
        near[m, NZ + POWERS : NZ + 2 * POWERS] = far[:, ::-1]
        near[m, NZ + 14] = -2.5 * near[m, 0]
        near[m, NZ + 15] = 2.5 * near[m, NZ - 1]
    wide = np.zeros((144, (POWERS + 1) * NZ))
    wide[:, : POWERS * NZ] = near[:, :, 1:-1].transpose(1, 0, 2).reshape(144, POWERS * NZ)
    for m in range(POWERS):
        wide[:, POWERS * NZ + 2 * m] = near[m, :, -1]
        wide[:, POWERS * NZ + 2 * m + 1] = near[m, :, 0]
    wide = wide.astype(np.float32)
    head = wide.astype(jnp.bfloat16)
    tail = (wide - head.astype(np.float32)).astype(jnp.bfloat16)
    table = np.zeros((512, wide.shape[1]), jnp.bfloat16)
    table[0:128] = head[:NZ]
    table[128:256] = head[:NZ]
    table[256:384] = tail[:NZ]
    table[384:400] = head[NZ:]
    table[400:416] = head[NZ:]
    table[416:432] = tail[NZ:]
    return table


@functools.cache
def moment_table():
    table = np.zeros((2, NZ, 128), np.float32)
    for z in range(NZ):
        for j in range(POWERS):
            table[0, z, j] = comb(z, j) * RATIO**z
            table[0, z, POWERS + j] = comb(NZ - 1 - z, j) * RATIO ** (NZ - 1 - z)
    table[1, 0, 14] = 1.0
    table[1, NZ - 1, 15] = 1.0
    return table


@functools.cache
def combine_table():
    small = np.zeros((BLOCKS, 16, 16))
    end = [comb(NZ - 1, a) * RATIO ** (NZ - 1) for a in range(POWERS)]
    for o in range(1, 2 * BLOCKS + 1):
        gap = NZ * (o - 1)
        for j in range(POWERS):
            for a in range(j + 1):
                factor = comb(gap, j - a) * RATIO**gap
                left = -o
                small[left % BLOCKS, POWERS + a, j] += factor
                small[(left - 1) % BLOCKS, 15, j] += factor * end[a] * -2.5
                small[(left + 1) % BLOCKS, 14, j] += factor * (2.5 if a == 0 else 0.0)
                right = o
                small[right % BLOCKS, a, POWERS + j] += factor
                small[(right - 1) % BLOCKS, 15, POWERS + j] += factor * (-2.5 if a == 0 else 0.0)
                small[(right + 1) % BLOCKS, 14, POWERS + j] += factor * end[a] * 2.5
    small[-1 % BLOCKS, 15, 14] += 1.0
    small[1 % BLOCKS, 14, 15] += 1.0
    table = np.zeros((BLOCKS, 128, 128), np.float32)
    for x in range(NX):
        table[:, 16 * x : 16 * x + 16, 16 * x : 16 * x + 16] = small
    return table


def lanes(rows):
    return lax.broadcasted_iota(jnp.int32, (rows, 128), 1)


def pack_columns(fields):
    lane = lanes(NY)
    packed = jnp.zeros((NY, 128), F32)
    for k in range(5):
        for x in range(NX):
            pair = 12 * k + x + 2
            keep = (lane == 2 * pair + 1) | (lane == 2 * pair + 2)
            packed = jnp.where(keep, pltpu.roll(fields(k, x), 2 * pair + 2, 1), packed)
    return packed


def pack_body(flags, vel_far, frac_far, now_far, old_far, paired, other, packed, guess, vel, frac, now, old, sem):
    pairs = [(now_far, now), (old_far, old), (frac_far, frac)] + [(vel_far.at[k], vel.at[k]) for k in range(3)]
    for copy in start_copies(pairs, sem):
        copy.wait()
    for x in range(NX):
        guess[x] = 2.0 * now[x] - old[x]
    emit_faces(flags, vel, frac, guess, paired, other, packed)


def emit_faces(flags, vel, frac, guess, paired, other, packed):
    even = flags[2] == 1
    for out, upper in ((paired, even), (other, jnp.logical_not(even))):
        two = jnp.where(upper, NX - 2, 0)
        one = jnp.where(upper, NX - 1, 0)
        for k in range(2):
            out[k] = vel[0, two + k]
            out[4 + k] = frac[two + k]
            out[6 + k] = guess[two + k]
        out[2] = vel[1, one]
        out[3] = vel[2, one]

    def field(k, x):
        return vel[k, x] if k < 3 else (frac[x] if k == 3 else guess[x])

    packed[...] = pack_columns(field)


def fill_shifts(buffers, ends, planes, slots):
    U, V, W, F, G, FM, FP = buffers
    own = pl.ds(TOP, NY)
    below, above = pl.ds(TOP - 1, 1), pl.ds(TOP + NY, 1)
    bottom, top = pl.ds(TOP, 1), pl.ds(TOP + NY - 1, 1)
    lane = lanes(NY)
    for e, slot in zip(planes, slots):
        centre = F[e, own]
        turned = pltpu.roll(ends, 128 - 2 * (36 + slot) - 1, 1)
        FM[e, own] = jnp.where(lane == 0, turned, pltpu.roll(centre, 1, 1))
        FP[e, own] = jnp.where(lane == 127, turned, pltpu.roll(centre, 127, 1))
        for buf in (F, FM, FP, G):
            buf[e, below] = buf[e, bottom]
            buf[e, above] = buf[e, top]
        for buf, wall in ((U, 2.0), (V, 0.0), (W, 0.0)):
            buf[e, below] = wall - buf[e, bottom]
            buf[e, above] = -buf[e, top]


def cells(low, at, high, Z, e, y, components):
    U, V, W, F, G, FM, FP = range(7)

    def get(plane, k, rows):
        return plane[0][k][plane[1], rows]

    lane = lanes(8)
    at_low = lane == 0
    at_high = lane == 127
    here, up, down = pl.ds(y + TOP, 8), pl.ds(y + TOP + 1, 8), pl.ds(y + TOP - 1, 8)
    ends_all = Z[pl.ds(y, 8), :]

    def star(k, group):
        centre = get(at, k, here)
        ends = pltpu.roll(ends_all, 128 - 2 * (12 * group + e) - 1, 1)
        behind = jnp.where(at_low, ends, pltpu.roll(centre, 1, 1))
        ahead = jnp.where(at_high, ends, pltpu.roll(centre, 127, 1))
        return centre, (
            (get(high, k, here), get(low, k, here)),
            (get(at, k, up), get(at, k, down)),
            (ahead, behind),
        )

    c = get(at, F, here)
    around = ((get(high, F, here), get(low, F, here)), (get(at, F, up), get(at, F, down)), (get(at, FP, here), get(at, FM, here)))
    d = [p - m for p, m in around]
    second = [p + m - 2.0 * c for p, m in around]
    mxy = (get(high, F, up) - get(high, F, down)) - (get(low, F, up) - get(low, F, down))
    mxz = (get(high, FP, here) - get(high, FM, here)) - (get(low, FP, here) - get(low, FM, here))
    myz = (get(at, FP, up) - get(at, FM, up)) - (get(at, FP, down) - get(at, FM, down))
    dd = [v * v for v in d]
    inverse = lax.rsqrt(jnp.maximum(dd[0] + dd[1] + dd[2], 1.0))
    bend = (dd[0] * second[0] + dd[1] * second[1] + dd[2] * second[2]) + 0.5 * (
        d[0] * (d[1] * mxy + d[2] * mxz) + d[1] * d[2] * myz
    )
    laplace = second[0] + second[1] + second[2]
    volume = 1.0 / (0.5 + 0.5 * c)
    pull = (bend * (inverse * inverse) - laplace) * (0.5 * inverse) * volume
    nu = (0.02 + 0.03 * c) * volume
    if len(components) == 3:
        stars = [star(k, k) for k in (U, V, W)]
        centres = [s[0] for s in stars]
    else:
        stars = [star(U, 0)]
        centres = [stars[0][0], get(at, V, here), get(at, W, here)]
    speeds = [jnp.abs(v) for v in centres]
    if len(components) == 3:
        guesses = star(G, 4)[1]
    else:
        guesses = ((get(high, G, here), get(low, G, here)),)
    lift = 2.0 - volume
    out = []
    for k in components:
        centre, sides_ = stars[k]
        twice = 2.0 * centre
        transport = 0.0
        diffusion = 0.0
        for a in range(3):
            p, m = sides_[a]
            curve = p + m - twice
            transport = transport + (centres[a] * (p - m) - speeds[a] * curve)
            diffusion = diffusion + curve
        change = nu * diffusion + pull * d[k] - 0.5 * transport
        p, m = guesses[k]
        out.append(centre + 0.1 * (change + 0.5 * (lift * (p - m))))
    if len(components) == 1:
        return out
    net = 0.0
    for a in range(3):
        p, m = stars[a][1][a]
        fp, fm = around[a]
        ahead = centres[a] + p
        behind = centres[a] + m
        net = net + (
            (jnp.maximum(ahead, 0.0) - jnp.minimum(behind, 0.0)) * c
            + (jnp.minimum(ahead, 0.0) * fp - jnp.maximum(behind, 0.0) * fm)
        )
    return out + [c - 0.05 * net]


def source_plane(x, before, after, v, w, moments, pack):
    lane = lanes(NY)
    row = lax.broadcasted_iota(jnp.int32, (NY, 128), 0)
    v_up = jnp.where(row == NY - 1, 0.0, pltpu.roll(v, NY - 1, 0))
    v_down = jnp.where(row == 0, 0.0, pltpu.roll(v, 1, 0))
    w_up = jnp.where(lane == NZ - 1, 0.0, pltpu.roll(w, NZ - 1, 1))
    w_down = jnp.where(lane == 0, 0.0, pltpu.roll(w, 1, 1))
    s = 2.5 * ((after - before) + (v_up - v_down) + (w_up - w_down))
    part = jnp.dot(s, moments[0], precision=HIGHEST, preferred_element_type=F32) + jnp.dot(
        w, moments[1], precision=HIGHEST, preferred_element_type=F32
    )
    pack[...] += pltpu.roll(part, 16 * x, 1) if x else part
    return s


def start_copies(pairs, sem):
    copies = [pltpu.make_async_copy(src, dst, sem.at[k]) for k, (src, dst) in enumerate(pairs)]
    for copy in copies:
        copy.start()
    return copies


def inner_body(vel, frac, guess, sides, moments, *refs):
    buffers = refs[:7]
    mid, frac_new, source, pack, sem = refs[7:]
    U, V, W, F, G = buffers[:5]
    own = pl.ds(TOP, NY)
    sources = [vel.at[0], vel.at[1], vel.at[2], frac, guess]
    copies = start_copies([(src, buf.at[pl.ds(0, NX), own]) for src, buf in zip(sources, (U, V, W, F, G))], sem)
    pack[...] = jnp.zeros((NY, 128), F32)
    for copy in copies:
        copy.wait()
    fill_shifts(buffers, sides[...], range(NX), range(2, 2 + NX))

    def block(i, carry):
        x = 1 + i // 16
        y = pl.multiple_of((i % 16) * 8, 8)
        rows = pl.ds(y, 8)
        mid[0, x, rows], mid[1, x, rows], mid[2, x, rows], frac_new[x, rows] = cells(
            (buffers, x - 1), (buffers, x), (buffers, x + 1), sides, x + 2, y, (0, 1, 2)
        )
        return carry

    lax.fori_loop(0, 16 * (NX - 2), block, 0, unroll=4)
    for x in range(2, NX - 2):
        source[x] = source_plane(x, mid[0, x - 1], mid[0, x + 1], mid[1, x], mid[2, x], moments, pack)


def side_part(up, at_end, message, sides, profile, moments, given, given_mid, mid, frac, source, pack, scratch):
    buffers, (Z, end_mid, sem) = scratch[:7], scratch[7:]
    U, V, W, F, G = buffers[:5]
    own = pl.ds(TOP, NY)
    near = 0 if up else 1
    pairs = [
        (message.at[pl.ds(0, 2)], U.at[:, own]),
        (message.at[2], V.at[near, own]),
        (message.at[3], W.at[near, own]),
        (message.at[pl.ds(4, 2)], F.at[:, own]),
        (message.at[pl.ds(6, 2)], G.at[:, own]),
        (message.at[8], Z),
    ]
    for copy in start_copies(pairs, sem):
        copy.wait()
    lane = lanes(NY)
    slot = lane // 2 % 12
    group = lane // 2 // 12
    merged = sides[...]
    if up:
        beyond = pltpu.roll(Z[...], 16, 1)
        if at_end is not None:
            wall = jnp.where(slot == 10, pltpu.roll(merged, 2, 1), pltpu.roll(merged, 4, 1))
            beyond = jnp.where(at_end, wall, beyond)
        Z[...] = jnp.where(slot >= 10, beyond, merged)
    else:
        beyond = pltpu.roll(Z[...], 112, 1)
        if at_end is not None:
            wall = jnp.where(group == 0, profile[0], jnp.where(group == 3, profile[1], 0.0))
            beyond = jnp.where(at_end, wall, beyond)
        Z[...] = jnp.where(slot < 2, beyond, merged)
    if at_end is not None:

        @pl.when(at_end)
        def _():
            for e in range(2):
                U[e, own] = given[0][NX - 1, own] if up else profile[0]
                F[e, own] = given[3][NX - 1, own] if up else profile[1]
            if up:
                V[near, own] = given[1][NX - 1, own]
                W[near, own] = given[2][NX - 1, own]

    fill_shifts(buffers, Z[...], range(2), (10, 11) if up else (0, 1))
    halo = [(buffers, 0), (buffers, 1)]
    line = [(given, NX - 2), (given, NX - 1)] + halo if up else halo + [(given, 0), (given, 1)]
    inside, outside = (line[:3], line[1:]) if up else (line[1:], line[:3])

    def block(i, carry):
        y = pl.multiple_of(i * 8, 8)
        rows = pl.ds(y, 8)
        mid[0, rows], mid[1, rows], mid[2, rows], frac[rows] = cells(*inside, Z, 9 if up else 2, y, (0, 1, 2))
        (end_mid[rows],) = cells(*outside, Z, 10 if up else 1, y, (0,))
        return carry

    lax.fori_loop(0, 16, block, 0, unroll=2)
    if up:
        source[0] = source_plane(6, given_mid[0, 5], mid[0], given_mid[1, 6], given_mid[2, 6], moments, pack)
        source[1] = source_plane(7, given_mid[0, 6], end_mid[...], mid[1], mid[2], moments, pack)
    else:
        source[0] = source_plane(0, end_mid[...], given_mid[0, 1], mid[1], mid[2], moments, pack)
        source[1] = source_plane(1, mid[0], given_mid[0, 2], given_mid[1, 1], given_mid[2, 1], moments, pack)


def paired_body(flags, message, sides, profile, moments, *refs):
    given, given_mid, given_pack = refs[:7], refs[7], refs[8]
    mid, frac, source, pack = refs[9:13]
    pack[...] = given_pack[...]
    for up in (True, False):

        @pl.when(flags[2] == int(up))
        def _(up=up):
            side_part(
                up, None, message, sides, profile, moments, given, given_mid, mid.at[:, 0], frac, source, pack, refs[13:]
            )


def other_body(flags, message, sides, profile, moments, *refs):
    given, (given_mid, given_frac, given_source) = refs[:7], refs[7:10]
    paired_frac, paired_source, given_pack = refs[10:13]
    mid, frac_new, source, pack = refs[13:17]
    scratch, keep_sem = refs[17:-1], refs[-1]
    even = flags[2] == 1
    middle = pl.ds(1, NX - 2)
    kept = [
        (given_frac.at[middle], frac_new.at[middle]),
        (paired_frac, frac_new.at[jnp.where(even, NX - 1, 0)]),
        (given_source.at[pl.ds(2, NX - 4)], source.at[pl.ds(2, NX - 4)]),
        (paired_source, source.at[pl.ds(jnp.where(even, NX - 2, 0), 2)]),
    ]
    kept = start_copies(kept, keep_sem)
    pack[...] = given_pack[...]
    for up in (True, False):

        @pl.when(flags[2] == 1 - int(up))
        def _(up=up):
            side_part(
                up,
                flags[1 if up else 0] == 1,
                message, sides, profile, moments, given, given_mid,
                mid.at[:, 0],
                frac_new.at[NX - 1 if up else 0],
                source.at[pl.ds(NX - 2 if up else 0, 2)],
                pack,
                scratch,
            )

    for copy in kept:
        copy.wait()


def combine_body(a, b, c, d, table, _, message, out, sem):
    total = 0.0
    for k, ref in enumerate((a, b, c, d)):
        total = total + jnp.dot(ref[...], table[k], precision=HIGHEST, preferred_element_type=F32)
    out[...] = total
    copy = pltpu.make_async_copy(out, message.at[NX], sem)
    copy.start()
    copy.wait()


def merge_body(before, after, _, __, right, left, out, sem):
    lane = lanes(NY)
    out[...] = jnp.where(lane % 2 == 1, before[...], pltpu.roll(after[...], 126, 1))
    copies = [pltpu.make_async_copy(out, m.at[NX], sem.at[k]) for k, m in enumerate((right, left))]
    for copy in copies:
        copy.start()
    for copy in copies:
        copy.wait()


HALO = POWERS


def put(out, m, plane, y, value):
    size = value.shape[0]
    out[m, plane, pl.ds(TOP + y, size)] = value
    if y == 0:
        out[m, plane, pl.ds(TOP - 1, 1)] = value[:1]
    if y + size == NY:
        out[m, plane, pl.ds(TOP + NY, 1)] = value[size - 1 :]


def terms(table, U, E, lhs, row, plane, values, moments, start):
    lane = lanes(NY)
    head = values.astype(BF16)
    tail = (values - head.astype(F32)).astype(BF16)
    m_head = moments.astype(BF16).astype(F32)
    m_tail = moments - m_head
    side = jnp.where(
        lane < 16,
        m_head,
        jnp.where(
            lane < 32,
            pltpu.roll(m_tail, 16, 1),
            jnp.where(lane < 48, pltpu.roll(m_head, 32, 1), 0.0),
        ),
    )
    lhs[:, 0:128] = head
    lhs[:, 128:256] = tail
    lhs[:, 256:384] = head
    lhs[:, 384:512] = side.astype(BF16)
    result = jnp.dot(lhs[...], table[:, start * 128 :], preferred_element_type=F32)
    for m in range(start, POWERS):
        put(U, m, row, 0, result[:, (m - start) * 128 : (m - start + 1) * 128])
    ends = result[:, (POWERS - start) * 128 :]
    group, offset = plane // 8, 16 * (plane % 8)
    E[group] += pltpu.roll(ends, offset, 1)


def own_terms_body(source, far, table, U, E, lhs):
    E[...] = jnp.zeros((3, NY, 128), F32)

    def own_plane(x, carry):
        moments = pltpu.roll(far[...], (128 - 16 * x) % 128, 1)
        terms(table, U, E, lhs, x, x + HALO, source[x], moments, 0)
        return carry

    lax.fori_loop(0, NX, own_plane, 0)


def side_terms_body(flags, paired, given_E, table, U, E, lhs):
    even = flags[2] == 1
    E[...] = given_E[...]
    for k in range(1, HALO + 1):
        x = jnp.where(even, k - 1, NX - k)
        moments = pltpu.roll(paired[NX], (128 - 16 * x) % 128, 1)
        plane = jnp.where(even, HALO + NX - 1 + k, HALO - k)
        place = jnp.where(even, k - 1, HALO - k)
        terms(table, U, E, lhs, place, plane, paired[x], moments, k - 1)


def solve_body(more, *refs):
    (flags, mid, mid_paired, mid_other, frac, now, other, table, given_U, given_side, given_E) = refs[:11]
    vel, pressure = refs[11:13]
    U, E, lhs, sem, side_sem = refs[-5:]
    if more:
        faces_paired, faces_other, packed, guess = refs[13:17]
    first = flags[0] == 1
    last = flags[1] == 1
    halo = HALO
    top = POWERS - 1
    fetch = pltpu.make_async_copy(given_U.at[top], U.at[top, pl.ds(halo, NX)], sem)
    fetch.start()
    even = flags[2] == 1
    fetch_side = pltpu.make_async_copy(
        given_side.at[top], U.at[top, pl.ds(jnp.where(even, halo + NX, 0), halo)], side_sem
    )
    fetch_side.start()
    E[...] = given_E[...]

    def inside(plane):
        kept = ((plane >= halo) | jnp.logical_not(first)) & ((plane < halo + NX) | jnp.logical_not(last))
        return jnp.where(kept, 1.0, 0.0).astype(F32)

    for k in range(1, halo + 1):
        x = jnp.where(even, NX - k, k - 1)
        moments = pltpu.roll(other[NX], (128 - 16 * x) % 128, 1)
        plane = jnp.where(even, halo - k, halo + NX - 1 + k)
        terms(table, U, E, lhs, plane, plane, other[x], moments, k - 1)

    fetch_side.wait()
    fetch.wait()
    for m in range(POWERS - 2, -1, -1):
        reach = m + 1

        def beside(plane, y, m=m):
            here = pl.ds(TOP + y, 32)
            return (U[m + 1, plane - 1, here] + U[m + 1, plane + 1, here]) + (
                U[m + 1, plane, pl.ds(TOP + y - 1, 32)] + U[m + 1, plane, pl.ds(TOP + y + 1, 32)]
            )

        def sweep(i, carry, m=m):
            low, high = halo - 1 - i, halo + NX + i
            plane = jnp.where(even, high, low)
            place = jnp.where(even, i, halo - 1 - i)
            far_plane = jnp.where(even, low, high)
            keep = inside(far_plane)
            for y in range(0, NY, 32):
                here = pl.ds(TOP + y, 32)
                put(U, m, plane, y, given_side[m, place, here] + beside(plane, y))
                put(U, m, far_plane, y, U[m, far_plane, here] + keep * beside(far_plane, y))
            return carry

        def sweep_own(x, carry, m=m):
            for y in range(0, NY, 32):
                put(U, m, x + halo, y, given_U[m, x, pl.ds(TOP + y, 32)] + beside(x + halo, y))
            return carry

        lax.fori_loop(0, reach, sweep, 0)
        lax.fori_loop(0, NX, sweep_own, 0, unroll=2)

    lane = lanes(NY)
    row = lax.broadcasted_iota(jnp.int32, (NY, 128), 0)
    used = lane % 16 < 14
    keeps = []
    for g in range(3):
        plane = 8 * g + lane // 16
        keeps.append(jnp.where(used, inside(plane), 0.0))
    start = [E[g] for g in range(3)]
    ends = start
    for m in range(POWERS - 1):
        before = [pltpu.roll(e, 14, 1) for e in ends]
        after = [pltpu.roll(e, 110, 1) for e in ends]
        same = [pltpu.roll(e, 126, 1) for e in ends]
        updated = []
        for g in range(3):
            behind = jnp.where(lane < 16, before[g - 1], before[g]) if g else before[0]
            ahead = jnp.where(lane >= 112, after[g + 1], after[g]) if g < 2 else after[2]
            up = jnp.where(row == NY - 1, same[g], pltpu.roll(same[g], NY - 1, 0))
            down = jnp.where(row == 0, same[g], pltpu.roll(same[g], 1, 0))
            updated.append(start[g] + keeps[g] * ((behind + ahead) + (up + down)))
        ends = updated
    for g in range(3):
        E[g] = ends[g]

    def correct(x, mid, mx):
        plane = x + halo
        lane = lanes(NY)
        turned = pltpu.roll(E[plane // 8], (128 - 16 * (plane % 8) - 1) % 128, 1)
        centre = U[0, plane, pl.ds(TOP, NY)]
        ahead = jnp.where(lane == NZ - 1, turned, pltpu.roll(centre, NZ - 1, 1))
        behind = jnp.where(lane == 0, turned, pltpu.roll(centre, 1, 1))
        vel[2, x] = mid[2, mx] + 0.1 * (ahead - behind)
        for y in range(0, NY, 32):
            here = pl.ds(TOP + y, 32)
            rows = pl.ds(y, 32)
            p = -U[0, plane, here]
            pressure[x, rows] = p
            vel[0, x, rows] = mid[0, mx, rows] + 0.1 * (U[0, plane + 1, here] - U[0, plane - 1, here])
            vel[1, x, rows] = mid[1, mx, rows] + 0.1 * (
                U[0, plane, pl.ds(TOP + y + 1, 32)] - U[0, plane, pl.ds(TOP + y - 1, 32)]
            )
            if more:
                guess[x, rows] = 2.0 * p - now[x, rows]

    def correct_inner(x, carry):
        correct(x, mid, x)
        return carry

    lax.fori_loop(1, NX - 1, correct_inner, 0, unroll=2)
    correct(jnp.where(even, NX - 1, 0), mid_paired, 0)
    correct(jnp.where(even, 0, NX - 1), mid_other, 0)
    if more:
        emit_faces(flags, vel, frac, guess, faces_paired, faces_other, packed)


def shape(*dims):
    return jax.ShapeDtypeStruct(dims, F32)


IN_VMEM = pl.BlockSpec(memory_space=pltpu.VMEM)
IN_SMEM = pl.BlockSpec(memory_space=pltpu.SMEM)
IN_HBM = pl.BlockSpec(memory_space=pltpu.HBM)
ANYWHERE = pl.BlockSpec(memory_space=pl.ANY)
BLOCK = (NX, NY, NZ)
MESSAGE = (NX + 1, NY, NZ)


def pack_call(flags, velocity, fraction, now, old):
    return pl.pallas_call(
        pack_body,
        out_shape=(shape(*MESSAGE), shape(*MESSAGE), shape(NY, 128), shape(*BLOCK)),
        in_specs=[IN_SMEM] + [IN_HBM] * 4,
        out_specs=(IN_VMEM,) * 4,
        scratch_shapes=[pltpu.VMEM((3, *BLOCK), F32)]
        + [pltpu.VMEM(BLOCK, F32)] * 3
        + [pltpu.SemaphoreType.DMA((6,))],
        compiler_params=pltpu.CompilerParams(vmem_limit_bytes=60 * MIB),
        name="pack",
    )(flags, velocity, fraction, now, old)


PADDED = (NX, ROWS, NZ)
PREDICTED = tuple(shape(*PADDED) for _ in range(7)) + (
    shape(3, *BLOCK),
    shape(*BLOCK),
    shape(*MESSAGE),
    shape(NY, 128),
)


def inner_call(velocity, fraction, guess, sides, moments):
    return pl.pallas_call(
        inner_body,
        out_shape=PREDICTED,
        in_specs=[ANYWHERE] * 3 + [IN_VMEM] * 2,
        out_specs=(IN_VMEM,) * 11,
        scratch_shapes=[pltpu.SemaphoreType.DMA((5,))],
        compiler_params=pltpu.CompilerParams(vmem_limit_bytes=16 * MIB),
        cost_estimate=pl.CostEstimate(flops=20_000_000, bytes_accessed=16_000_000, transcendentals=100_000),
        name="inner",
    )(velocity, fraction, guess, sides, moments)


SIDE_SCRATCH = [pltpu.VMEM((2, ROWS, NZ), F32)] * 7 + [
    pltpu.VMEM((NY, 128), F32),
    pltpu.VMEM((NY, NZ), F32),
    pltpu.SemaphoreType.DMA((6,)),
]


def paired_call(flags, message, sides, profile, moments, inner):
    *buffers, mid, _, _, pack = inner
    return pl.pallas_call(
        paired_body,
        out_shape=(shape(3, 1, NY, NZ), shape(NY, NZ), shape(2, NY, NZ), shape(NY, 128)),
        in_specs=[IN_SMEM] + [ANYWHERE] + [IN_VMEM] * 12,
        out_specs=(IN_VMEM,) * 4,
        scratch_shapes=SIDE_SCRATCH,
        compiler_params=pltpu.CompilerParams(vmem_limit_bytes=12 * MIB),
        cost_estimate=pl.CostEstimate(flops=6_000_000, bytes_accessed=6_000_000, transcendentals=30_000),
        name="paired_side",
    )(flags, message, sides, profile, moments, *buffers, mid, pack)


def other_call(flags, message, sides, profile, moments, inner, frac, source, pack):
    *buffers, mid, inner_frac, inner_source, _ = inner
    return pl.pallas_call(
        other_body,
        out_shape=(shape(3, 1, NY, NZ), shape(*BLOCK), shape(*MESSAGE), shape(NY, 128)),
        in_specs=[IN_SMEM] + [ANYWHERE] + [IN_VMEM] * 11 + [ANYWHERE] * 4 + [IN_VMEM],
        out_specs=(IN_VMEM,) * 4,
        scratch_shapes=SIDE_SCRATCH + [pltpu.SemaphoreType.DMA((4,))],
        compiler_params=pltpu.CompilerParams(vmem_limit_bytes=12 * MIB),
        name="other_side",
    )(flags, message, sides, profile, moments, *buffers, mid, inner_frac, inner_source, frac, source, pack)


def combine_call(packs, table, message):
    return pl.pallas_call(
        combine_body,
        out_shape=(shape(*MESSAGE), shape(NY, 128)),
        in_specs=[IN_VMEM] * 5 + [ANYWHERE],
        out_specs=(ANYWHERE, IN_VMEM),
        scratch_shapes=[pltpu.SemaphoreType.DMA],
        input_output_aliases={5: 0},
        compiler_params=pltpu.CompilerParams(vmem_limit_bytes=4 * MIB),
        name="combine",
    )(*packs, table, message)


def merge_call(before, after, right, left):
    return pl.pallas_call(
        merge_body,
        out_shape=(shape(*MESSAGE), shape(*MESSAGE), shape(NY, 128)),
        in_specs=[IN_VMEM] * 2 + [ANYWHERE] * 2,
        out_specs=(ANYWHERE, ANYWHERE, IN_VMEM),
        scratch_shapes=[pltpu.SemaphoreType.DMA((2,))],
        input_output_aliases={2: 0, 3: 1},
        compiler_params=pltpu.CompilerParams(vmem_limit_bytes=4 * MIB),
        name="merge",
    )(before, after, right, left)


OWN_TERMS = (POWERS, NX, ROWS, NZ)


def own_terms_call(source, far, table):
    return pl.pallas_call(
        own_terms_body,
        out_shape=(shape(*OWN_TERMS), shape(3, NY, 128)),
        in_specs=[IN_VMEM] * 3,
        out_specs=(IN_VMEM,) * 2,
        scratch_shapes=[pltpu.VMEM((NY, 512), BF16)],
        compiler_params=pltpu.CompilerParams(vmem_limit_bytes=20 * MIB),
        cost_estimate=pl.CostEstimate(flops=1_000_000_000, bytes_accessed=12_000_000, transcendentals=0),
        name="own_terms",
    )(source, far, table)


def side_terms_call(flags, paired, ends, table):
    return pl.pallas_call(
        side_terms_body,
        out_shape=(shape(POWERS, HALO, ROWS, NZ), shape(3, NY, 128)),
        in_specs=[IN_SMEM] + [IN_VMEM] * 3,
        out_specs=(IN_VMEM,) * 2,
        scratch_shapes=[pltpu.VMEM((NY, 512), BF16)],
        compiler_params=pltpu.CompilerParams(vmem_limit_bytes=12 * MIB),
        cost_estimate=pl.CostEstimate(flops=500_000_000, bytes_accessed=6_000_000, transcendentals=0),
        name="side_terms",
    )(flags, paired, ends, table)


def solve_call(more, flags, mid, mid_paired, mid_other, frac, now, other, table, own, side, ends):
    outs = [shape(3, *BLOCK), shape(*BLOCK)]
    if more:
        outs += [shape(*MESSAGE), shape(*MESSAGE), shape(NY, 128), shape(*BLOCK)]
    return pl.pallas_call(
        functools.partial(solve_body, more),
        out_shape=tuple(outs),
        in_specs=[IN_SMEM] + [IN_VMEM] * 10,
        out_specs=(IN_VMEM,) * len(outs),
        scratch_shapes=[
            pltpu.VMEM((POWERS, NX + 2 * HALO, ROWS, NZ), F32),
            pltpu.VMEM((3, NY, 128), F32),
            pltpu.VMEM((NY, 512), BF16),
            pltpu.SemaphoreType.DMA,
            pltpu.SemaphoreType.DMA,
        ],
        compiler_params=pltpu.CompilerParams(vmem_limit_bytes=20 * MIB),
        name="solve",
    )(flags, mid, mid_paired, mid_other, frac, now, other, table, own, side, ends)


def per_device(velocity, fraction, pressure_now, pressure_old, inflow):
    stream = lax.axis_index("stream")
    count = lax.axis_size("stream")
    flags = jnp.stack([stream == 0, stream == count - 1, stream % 2 == 0]).astype(jnp.int32)
    pairs = [(i, i ^ 1) for i in range(count)]
    others = [(i, ((i + 1) ^ 1) - 1) for i in range(1, count - 1)]

    def exchange(block, with_pair):
        return lax.ppermute(block, "stream", pairs if with_pair else others)

    def around(block, offset):
        return lax.ppermute(
            block, "span", [((i + offset) % BLOCKS, i) for i in range(BLOCKS)]
        )

    profile = jnp.broadcast_to(inflow[:, :, None], (2, NY, NZ))
    moments = jnp.asarray(moment_table())
    combine = jnp.asarray(combine_table())
    table = jnp.asarray(solve_table())

    paired, other, packed, guess = pack_call(flags, velocity, fraction, pressure_now, pressure_old)
    now = pressure_now
    for step in range(STEPS):
        more = step < STEPS - 1
        paired, other, sides = merge_call(around(packed, -1), around(packed, 1), paired, other)
        other = exchange(other, False)
        paired = exchange(paired, True)
        inner = inner_call(velocity, fraction, guess, sides, moments)
        mid_paired, frac, source, pack = paired_call(flags, paired, sides, profile, moments, inner)
        mid_other, fraction, source, pack = other_call(
            flags, other, sides, profile, moments, inner, frac, source, pack
        )
        source, far = combine_call([pack] + [around(pack, o) for o in (1, 2, 3)], combine, source)
        other = exchange(source, False)
        paired = exchange(source, True)
        own, ends = own_terms_call(source, far, table)
        side, ends = side_terms_call(flags, paired, ends, table)
        results = solve_call(
            more, flags, inner[7], mid_paired, mid_other, fraction, now, other, table, own, side, ends
        )
        velocity, pressure = results[:2]
        old, now = now, pressure
        if more:
            paired, other, packed, guess = results[2:]
    return (velocity, fraction, now, old)


def solution(mesh):
    return jax.shard_map(
        per_device,
        mesh=mesh,
        in_specs=(
            P(None, "stream", None, "span"),
            P("stream", None, "span"),
            P("stream", None, "span"),
            P("stream", None, "span"),
            P(),
        ),
        out_specs=(
            P(None, "stream", None, "span"),
            P("stream", None, "span"),
            P("stream", None, "span"),
            P("stream", None, "span"),
        ),
        check_vma=False,
    )
```

```python
import functools
import math

import jax
import jax.numpy as jnp
import numpy as np
from jax import lax
from jax.experimental import pallas as pl
from jax.experimental.pallas import tpu as pltpu
from jax.sharding import PartitionSpec as P

STEPS = 2
POWERS = 7
NX, NY, NZ = 8, 128, 128
TOP = 8
ROWS = NY + 2 * TOP
BLOCKS = 4
F32 = jnp.float32
BF16 = jnp.bfloat16
HIGHEST = lax.Precision.HIGHEST
MIB = 1024 * 1024


def comb(n, k):
    return math.comb(n, k) if 0 <= k <= n else 0


RATIO = 3.0 - 2.0 * math.sqrt(2.0)


def line_kernel(power, n):
    return RATIO ** (power + n) * sum(
        comb(power - 1 + n + k, power - 1) * comb(power - 1 + k, power - 1) * RATIO ** (2 * k)
        for k in range(40)
    )


def far_kernel(power, j, z):
    return RATIO ** (power + 1 + z) * sum(
        comb(power - 1 + k, power - 1) * RATIO ** (2 * k) * comb(power + z + k, power - 1 - j)
        for k in range(40)
    )


@functools.cache
def solve_table():
    near = np.zeros((POWERS, 144, NZ + 2))
    for m in range(POWERS):
        kernel = np.array([line_kernel(m + 1, n) for n in range(NZ + 2)])
        z = np.arange(-1, NZ + 1)
        own = np.arange(NZ)
        near[m, :NZ] = kernel[np.abs(z[None, :] - own[:, None])]
        far = np.array([[far_kernel(m + 1, j, t) for t in z] for j in range(POWERS)])
        near[m, NZ : NZ + POWERS] = far
        near[m, NZ + POWERS : NZ + 2 * POWERS] = far[:, ::-1]
        near[m, NZ + 14] = -2.5 * near[m, 0]
        near[m, NZ + 15] = 2.5 * near[m, NZ - 1]
    wide = np.zeros((144, (POWERS + 1) * NZ))
    wide[:, : POWERS * NZ] = near[:, :, 1:-1].transpose(1, 0, 2).reshape(144, POWERS * NZ)
    for m in range(POWERS):
        wide[:, POWERS * NZ + 2 * m] = near[m, :, -1]
        wide[:, POWERS * NZ + 2 * m + 1] = near[m, :, 0]
    wide = wide.astype(np.float32)
    head = wide.astype(jnp.bfloat16)
    tail = (wide - head.astype(np.float32)).astype(jnp.bfloat16)
    table = np.zeros((512, wide.shape[1]), jnp.bfloat16)
    table[0:128] = head[:NZ]
    table[128:256] = head[:NZ]
    table[256:384] = tail[:NZ]
    table[384:400] = head[NZ:]
    table[400:416] = head[NZ:]
    table[416:432] = tail[NZ:]
    return table


@functools.cache
def moment_table():
    table = np.zeros((2, NZ, 128), np.float32)
    for z in range(NZ):
        for j in range(POWERS):
            table[0, z, j] = comb(z, j) * RATIO**z
            table[0, z, POWERS + j] = comb(NZ - 1 - z, j) * RATIO ** (NZ - 1 - z)
    table[1, 0, 14] = 1.0
    table[1, NZ - 1, 15] = 1.0
    return table


@functools.cache
def combine_table():
    small = np.zeros((BLOCKS, 16, 16))
    end = [comb(NZ - 1, a) * RATIO ** (NZ - 1) for a in range(POWERS)]
    for o in range(1, 2 * BLOCKS + 1):
        gap = NZ * (o - 1)
        for j in range(POWERS):
            for a in range(j + 1):
                factor = comb(gap, j - a) * RATIO**gap
                left = -o
                small[left % BLOCKS, POWERS + a, j] += factor
                small[(left - 1) % BLOCKS, 15, j] += factor * end[a] * -2.5
                small[(left + 1) % BLOCKS, 14, j] += factor * (2.5 if a == 0 else 0.0)
                right = o
                small[right % BLOCKS, a, POWERS + j] += factor
                small[(right - 1) % BLOCKS, 15, POWERS + j] += factor * (-2.5 if a == 0 else 0.0)
                small[(right + 1) % BLOCKS, 14, POWERS + j] += factor * end[a] * 2.5
    small[-1 % BLOCKS, 15, 14] += 1.0
    small[1 % BLOCKS, 14, 15] += 1.0
    table = np.zeros((BLOCKS, 128, 128), np.float32)
    for x in range(NX):
        table[:, 16 * x : 16 * x + 16, 16 * x : 16 * x + 16] = small
    return table


def lanes(rows):
    return lax.broadcasted_iota(jnp.int32, (rows, 128), 1)


def pack_columns(fields, ready=None):
    lane = lanes(NY)
    packed = jnp.zeros((NY, 128), F32)
    for k in (4, 3, 0, 1, 2):
        if ready is not None:
            ready(k)
        for x in range(NX):
            pair = 12 * k + x + 2
            keep = (lane == 2 * pair + 1) | (lane == 2 * pair + 2)
            packed = jnp.where(keep, pltpu.roll(fields(k, x), 2 * pair + 2, 1), packed)
    return packed


def pack_body(flags, vel_far, frac_far, now_far, old_far, paired, other, packed, guess, vel, frac, now, old, sem):
    pairs = [(now_far, now), (old_far, old), (frac_far, frac)] + [(vel_far.at[k], vel.at[k]) for k in range(3)]
    copies = start_copies(pairs, sem)

    def ready(k):
        if k == 4:
            copies[0].wait()
            copies[1].wait()
            for x in range(NX):
                guess[x] = 2.0 * now[x] - old[x]
        else:
            copies[2 if k == 3 else 3 + k].wait()

    packed[...] = pack_columns(lambda k, x: fields_of(vel, frac, guess, k, x), ready)
    emit_faces(flags, vel, frac, guess, paired, other)


def fields_of(vel, frac, guess, k, x):
    return vel[k, x] if k < 3 else (frac[x] if k == 3 else guess[x])


def emit_faces(flags, vel, frac, guess, paired, other):
    even = flags[2] == 1
    for out, upper in ((paired, even), (other, jnp.logical_not(even))):
        two = jnp.where(upper, NX - 2, 0)
        one = jnp.where(upper, NX - 1, 0)
        for k in range(2):
            out[k] = vel[0, two + k]
            out[4 + k] = frac[two + k]
            out[6 + k] = guess[two + k]
        out[2] = vel[1, one]
        out[3] = vel[2, one]


def fill_shifts(buffers, ends, planes, slots):
    U, V, W, F, G, FM, FP = buffers
    own = pl.ds(TOP, NY)
    below, above = pl.ds(TOP - 1, 1), pl.ds(TOP + NY, 1)
    bottom, top = pl.ds(TOP, 1), pl.ds(TOP + NY - 1, 1)
    lane = lanes(NY)
    for e, slot in zip(planes, slots):
        centre = F[e, own]
        turned = pltpu.roll(ends, 128 - 2 * (36 + slot) - 1, 1)
        FM[e, own] = jnp.where(lane == 0, turned, pltpu.roll(centre, 1, 1))
        FP[e, own] = jnp.where(lane == 127, turned, pltpu.roll(centre, 127, 1))
        for buf in (F, FM, FP, G):
            buf[e, below] = buf[e, bottom]
            buf[e, above] = buf[e, top]
        for buf, wall in ((U, 2.0), (V, 0.0), (W, 0.0)):
            buf[e, below] = wall - buf[e, bottom]
            buf[e, above] = -buf[e, top]


def cells(low, at, high, Z, e, y, components):
    U, V, W, F, G, FM, FP = range(7)

    def get(plane, k, rows):
        return plane[0][k][plane[1], rows]

    lane = lanes(8)
    at_low = lane == 0
    at_high = lane == 127
    here, up, down = pl.ds(y + TOP, 8), pl.ds(y + TOP + 1, 8), pl.ds(y + TOP - 1, 8)
    ends_all = Z[pl.ds(y, 8), :]

    def star(k, group):
        centre = get(at, k, here)
        ends = pltpu.roll(ends_all, 128 - 2 * (12 * group + e) - 1, 1)
        behind = jnp.where(at_low, ends, pltpu.roll(centre, 1, 1))
        ahead = jnp.where(at_high, ends, pltpu.roll(centre, 127, 1))
        return centre, (
            (get(high, k, here), get(low, k, here)),
            (get(at, k, up), get(at, k, down)),
            (ahead, behind),
        )

    c = get(at, F, here)
    around = ((get(high, F, here), get(low, F, here)), (get(at, F, up), get(at, F, down)), (get(at, FP, here), get(at, FM, here)))
    d = [p - m for p, m in around]
    second = [p + m - 2.0 * c for p, m in around]
    mxy = (get(high, F, up) - get(high, F, down)) - (get(low, F, up) - get(low, F, down))
    mxz = (get(high, FP, here) - get(high, FM, here)) - (get(low, FP, here) - get(low, FM, here))
    myz = (get(at, FP, up) - get(at, FM, up)) - (get(at, FP, down) - get(at, FM, down))
    dd = [v * v for v in d]
    inverse = lax.rsqrt(jnp.maximum(dd[0] + dd[1] + dd[2], 1.0))
    bend = (dd[0] * second[0] + dd[1] * second[1] + dd[2] * second[2]) + 0.5 * (
        d[0] * (d[1] * mxy + d[2] * mxz) + d[1] * d[2] * myz
    )
    laplace = second[0] + second[1] + second[2]
    volume = 1.0 / (0.5 + 0.5 * c)
    pull = (bend * (inverse * inverse) - laplace) * (0.5 * inverse) * volume
    nu = (0.02 + 0.03 * c) * volume
    if len(components) == 3:
        stars = [star(k, k) for k in (U, V, W)]
        centres = [s[0] for s in stars]
    else:
        stars = [star(U, 0)]
        centres = [stars[0][0], get(at, V, here), get(at, W, here)]
    speeds = [jnp.abs(v) for v in centres]
    if len(components) == 3:
        guesses = star(G, 4)[1]
    else:
        guesses = ((get(high, G, here), get(low, G, here)),)
    lift = 2.0 - volume
    out = []
    for k in components:
        centre, sides_ = stars[k]
        twice = 2.0 * centre
        transport = 0.0
        diffusion = 0.0
        for a in range(3):
            p, m = sides_[a]
            curve = p + m - twice
            transport = transport + (centres[a] * (p - m) - speeds[a] * curve)
            diffusion = diffusion + curve
        change = nu * diffusion + pull * d[k] - 0.5 * transport
        p, m = guesses[k]
        out.append(centre + 0.1 * (change + 0.5 * (lift * (p - m))))
    if len(components) == 1:
        return out
    net = 0.0
    for a in range(3):
        p, m = stars[a][1][a]
        fp, fm = around[a]
        ahead = centres[a] + p
        behind = centres[a] + m
        net = net + (
            (jnp.maximum(ahead, 0.0) - jnp.minimum(behind, 0.0)) * c
            + (jnp.minimum(ahead, 0.0) * fp - jnp.maximum(behind, 0.0) * fm)
        )
    return out + [c - 0.05 * net]


def source_plane(x, before, after, v, w, moments, pack):
    lane = lanes(NY)
    row = lax.broadcasted_iota(jnp.int32, (NY, 128), 0)
    v_up = jnp.where(row == NY - 1, 0.0, pltpu.roll(v, NY - 1, 0))
    v_down = jnp.where(row == 0, 0.0, pltpu.roll(v, 1, 0))
    w_up = jnp.where(lane == NZ - 1, 0.0, pltpu.roll(w, NZ - 1, 1))
    w_down = jnp.where(lane == 0, 0.0, pltpu.roll(w, 1, 1))
    s = 2.5 * ((after - before) + (v_up - v_down) + (w_up - w_down))
    part = jnp.dot(s, moments[0], precision=HIGHEST, preferred_element_type=F32) + jnp.dot(
        w, moments[1], precision=HIGHEST, preferred_element_type=F32
    )
    pack[...] += pltpu.roll(part, 16 * x, 1) if x else part
    return s


def start_copies(pairs, sem):
    copies = [pltpu.make_async_copy(src, dst, sem.at[k]) for k, (src, dst) in enumerate(pairs)]
    for copy in copies:
        copy.start()
    return copies


def inner_body(vel, frac, guess, sides, moments, *refs):
    buffers = refs[:7]
    mid, frac_new, source, pack, sem = refs[7:]
    U, V, W, F, G = buffers[:5]
    own = pl.ds(TOP, NY)
    sources = [vel.at[0], vel.at[1], vel.at[2], frac, guess]
    copies = start_copies([(src, buf.at[pl.ds(0, NX), own]) for src, buf in zip(sources, (U, V, W, F, G))], sem)
    pack[...] = jnp.zeros((NY, 128), F32)
    for copy in copies:
        copy.wait()
    fill_shifts(buffers, sides[...], range(NX), range(2, 2 + NX))

    def block(i, carry):
        x = 1 + i // 16
        y = pl.multiple_of((i % 16) * 8, 8)
        rows = pl.ds(y, 8)
        mid[0, x, rows], mid[1, x, rows], mid[2, x, rows], frac_new[x, rows] = cells(
            (buffers, x - 1), (buffers, x), (buffers, x + 1), sides, x + 2, y, (0, 1, 2)
        )
        return carry

    lax.fori_loop(0, 16 * (NX - 2), block, 0, unroll=4)
    for x in range(2, NX - 2):
        source[x] = source_plane(x, mid[0, x - 1], mid[0, x + 1], mid[1, x], mid[2, x], moments, pack)


def side_part(up, at_end, message, sides, profile, moments, given, given_mid, mid, frac, source, pack, scratch):
    buffers, (Z, end_mid, sem) = scratch[:7], scratch[7:]
    U, V, W, F, G = buffers[:5]
    own = pl.ds(TOP, NY)
    near = 0 if up else 1
    pairs = [
        (message.at[pl.ds(0, 2)], U.at[:, own]),
        (message.at[2], V.at[near, own]),
        (message.at[3], W.at[near, own]),
        (message.at[pl.ds(4, 2)], F.at[:, own]),
        (message.at[pl.ds(6, 2)], G.at[:, own]),
        (message.at[8], Z),
    ]
    for copy in start_copies(pairs, sem):
        copy.wait()
    lane = lanes(NY)
    slot = lane // 2 % 12
    group = lane // 2 // 12
    merged = sides[...]
    if up:
        beyond = pltpu.roll(Z[...], 16, 1)
        if at_end is not None:
            wall = jnp.where(slot == 10, pltpu.roll(merged, 2, 1), pltpu.roll(merged, 4, 1))
            beyond = jnp.where(at_end, wall, beyond)
        Z[...] = jnp.where(slot >= 10, beyond, merged)
    else:
        beyond = pltpu.roll(Z[...], 112, 1)
        if at_end is not None:
            wall = jnp.where(group == 0, profile[0], jnp.where(group == 3, profile[1], 0.0))
            beyond = jnp.where(at_end, wall, beyond)
        Z[...] = jnp.where(slot < 2, beyond, merged)
    if at_end is not None:

        @pl.when(at_end)
        def _():
            for e in range(2):
                U[e, own] = given[0][NX - 1, own] if up else profile[0]
                F[e, own] = given[3][NX - 1, own] if up else profile[1]
            if up:
                V[near, own] = given[1][NX - 1, own]
                W[near, own] = given[2][NX - 1, own]

    fill_shifts(buffers, Z[...], range(2), (10, 11) if up else (0, 1))
    halo = [(buffers, 0), (buffers, 1)]
    line = [(given, NX - 2), (given, NX - 1)] + halo if up else halo + [(given, 0), (given, 1)]
    inside, outside = (line[:3], line[1:]) if up else (line[1:], line[:3])

    def block(i, carry):
        y = pl.multiple_of(i * 8, 8)
        rows = pl.ds(y, 8)
        mid[0, rows], mid[1, rows], mid[2, rows], frac[rows] = cells(*inside, Z, 9 if up else 2, y, (0, 1, 2))
        (end_mid[rows],) = cells(*outside, Z, 10 if up else 1, y, (0,))
        return carry

    lax.fori_loop(0, 16, block, 0, unroll=2)
    if up:
        source[0] = source_plane(6, given_mid[0, 5], mid[0], given_mid[1, 6], given_mid[2, 6], moments, pack)
        source[1] = source_plane(7, given_mid[0, 6], end_mid[...], mid[1], mid[2], moments, pack)
    else:
        source[0] = source_plane(0, end_mid[...], given_mid[0, 1], mid[1], mid[2], moments, pack)
        source[1] = source_plane(1, mid[0], given_mid[0, 2], given_mid[1, 1], given_mid[2, 1], moments, pack)


def paired_body(flags, message, sides, profile, moments, *refs):
    given, given_mid, given_pack = refs[:7], refs[7], refs[8]
    mid, frac, source, pack = refs[9:13]
    pack[...] = given_pack[...]
    for up in (True, False):

        @pl.when(flags[2] == int(up))
        def _(up=up):
            side_part(
                up, None, message, sides, profile, moments, given, given_mid, mid.at[:, 0], frac, source, pack, refs[13:]
            )


def other_body(flags, message, sides, profile, moments, *refs):
    given, (given_mid, given_frac, given_source) = refs[:7], refs[7:10]
    paired_frac, paired_source, given_pack = refs[10:13]
    mid, frac_new, source, pack = refs[13:17]
    scratch, keep_sem = refs[17:-1], refs[-1]
    even = flags[2] == 1
    middle = pl.ds(1, NX - 2)
    kept = [
        (given_frac.at[middle], frac_new.at[middle]),
        (paired_frac, frac_new.at[jnp.where(even, NX - 1, 0)]),
        (given_source.at[pl.ds(2, NX - 4)], source.at[pl.ds(2, NX - 4)]),
        (paired_source, source.at[pl.ds(jnp.where(even, NX - 2, 0), 2)]),
    ]
    kept = start_copies(kept, keep_sem)
    pack[...] = given_pack[...]
    for up in (True, False):

        @pl.when(flags[2] == 1 - int(up))
        def _(up=up):
            side_part(
                up,
                flags[1 if up else 0] == 1,
                message, sides, profile, moments, given, given_mid,
                mid.at[:, 0],
                frac_new.at[NX - 1 if up else 0],
                source.at[pl.ds(NX - 2 if up else 0, 2)],
                pack,
                scratch,
            )

    for copy in kept:
        copy.wait()


def combine_body(a, b, c, d, table, _, message, out, sem):
    total = 0.0
    for k, ref in enumerate((a, b, c, d)):
        total = total + jnp.dot(ref[...], table[k], precision=HIGHEST, preferred_element_type=F32)
    out[...] = total
    copy = pltpu.make_async_copy(out, message.at[NX], sem)
    copy.start()
    copy.wait()


def merge_body(before, after, _, __, right, left, out, sem):
    lane = lanes(NY)
    out[...] = jnp.where(lane % 2 == 1, before[...], pltpu.roll(after[...], 126, 1))
    copies = [pltpu.make_async_copy(out, m.at[NX], sem.at[k]) for k, m in enumerate((right, left))]
    for copy in copies:
        copy.start()
    for copy in copies:
        copy.wait()


HALO = POWERS


def put(out, m, plane, y, value):
    size = value.shape[0]
    out[m, plane, pl.ds(TOP + y, size)] = value
    if y == 0:
        out[m, plane, pl.ds(TOP - 1, 1)] = value[:1]
    if y + size == NY:
        out[m, plane, pl.ds(TOP + NY, 1)] = value[size - 1 :]


def terms(table, U, E, lhs, row, plane, values, moments, start, first_group=0):
    lane = lanes(NY)
    head = values.astype(BF16)
    tail = (values - head.astype(F32)).astype(BF16)
    m_head = moments.astype(BF16).astype(F32)
    m_tail = moments - m_head
    side = jnp.where(
        lane < 16,
        m_head,
        jnp.where(
            lane < 32,
            pltpu.roll(m_tail, 16, 1),
            jnp.where(lane < 48, pltpu.roll(m_head, 32, 1), 0.0),
        ),
    )
    lhs[:, 0:128] = head
    lhs[:, 128:256] = tail
    lhs[:, 256:384] = head
    lhs[:, 384:512] = side.astype(BF16)
    result = jnp.dot(lhs[...], table[:, start * 128 :], preferred_element_type=F32)
    for m in range(start, POWERS):
        put(U, m, row, 0, result[:, (m - start) * 128 : (m - start + 1) * 128])
    ends = result[:, (POWERS - start) * 128 :]
    group, offset = plane // 8 - first_group, 16 * (plane % 8)
    E[group] += pltpu.roll(ends, offset, 1)


def own_terms_body(source, far, table, U, E, lhs):
    E[...] = jnp.zeros((3, NY, 128), F32)

    def own_plane(x, carry):
        moments = pltpu.roll(far[...], (128 - 16 * x) % 128, 1)
        terms(table, U, E, lhs, x, x + HALO, source[x], moments, 0)
        return carry

    lax.fori_loop(0, NX, own_plane, 0)


def side_terms_body(flags, paired, given_E, table, U, E, lhs):
    even = flags[2] == 1
    E[...] = given_E[...]
    for k in range(1, HALO + 1):
        x = jnp.where(even, k - 1, NX - k)
        moments = pltpu.roll(paired[NX], (128 - 16 * x) % 128, 1)
        plane = jnp.where(even, HALO + NX - 1 + k, HALO - k)
        place = jnp.where(even, k - 1, HALO - k)
        terms(table, U, E, lhs, place, plane, paired[x], moments, k - 1)


def domain(flags):
    first = flags[0] == 1
    last = flags[1] == 1

    def inside(plane):
        kept = ((plane >= HALO) | jnp.logical_not(first)) & ((plane < HALO + NX) | jnp.logical_not(last))
        return jnp.where(kept, 1.0, 0.0).astype(F32)

    return inside


def beside(U, m, plane, y):
    here = pl.ds(TOP + y, 32)
    return (U[m, plane - 1, here] + U[m, plane + 1, here]) + (
        U[m, plane, pl.ds(TOP + y - 1, 32)] + U[m, plane, pl.ds(TOP + y + 1, 32)]
    )


def sweep_ends(start, first_plane, inside):
    count = len(start)
    lane = lanes(NY)
    row = lax.broadcasted_iota(jnp.int32, (NY, 128), 0)
    used = lane % 16 < 14
    keeps = [jnp.where(used, inside(first_plane + 8 * g + lane // 16), 0.0) for g in range(count)]
    ends = start
    for m in range(POWERS - 1):
        before = [pltpu.roll(e, 14, 1) for e in ends]
        after = [pltpu.roll(e, 110, 1) for e in ends]
        same = [pltpu.roll(e, 126, 1) for e in ends]
        updated = []
        for g in range(count):
            behind = jnp.where(lane < 16, before[g - 1] if g else 0.0, before[g])
            ahead = jnp.where(lane >= 112, after[g + 1] if g < count - 1 else 0.0, after[g])
            up = jnp.where(row == NY - 1, same[g], pltpu.roll(same[g], NY - 1, 0))
            down = jnp.where(row == 0, same[g], pltpu.roll(same[g], 1, 0))
            updated.append(start[g] + keeps[g] * ((behind + ahead) + (up + down)))
        ends = updated
    return ends


def first_sweeps_body(flags, given_U, given_side, given_E, out, E, U, sem, side_sem):
    inside = domain(flags)
    even = flags[2] == 1
    top = POWERS - 1
    fetches = [
        pltpu.make_async_copy(given_U.at[top], U.at[top, pl.ds(HALO, NX)], sem),
        pltpu.make_async_copy(given_side.at[top], U.at[top, pl.ds(jnp.where(even, HALO + NX, 0), HALO)], side_sem),
    ]
    for fetch in fetches:
        fetch.start()

    def clear(i, carry):
        U[top, jnp.where(even, i, HALO + NX + i)] = jnp.zeros((ROWS, NZ), F32)
        return carry

    lax.fori_loop(0, HALO, clear, 0)
    for g, value in enumerate(sweep_ends([given_E[g] for g in range(3)], 0, inside)):
        E[g] = value
    for fetch in fetches:
        fetch.wait()

    for m in range(top - 1, -1, -1):

        def sweep(i, carry, m=m):
            low, high = HALO - 1 - i, HALO + NX + i
            plane = jnp.where(even, high, low)
            place = jnp.where(even, i, HALO - 1 - i)
            far_plane = jnp.where(even, low, high)
            keep = inside(far_plane)
            for y in range(0, NY, 32):
                here = pl.ds(TOP + y, 32)
                put(U, m, plane, y, given_side[m, place, here] + beside(U, m + 1, plane, y))
                put(U, m, far_plane, y, keep * beside(U, m + 1, far_plane, y))
            return carry

        def sweep_own(x, carry, m=m):
            for y in range(0, NY, 32):
                put(
                    U, m, x + HALO, y,
                    given_U[m, x, pl.ds(TOP + y, 32)] + beside(U, m + 1, x + HALO, y),
                )
            return carry

        lax.fori_loop(0, m + 1, sweep, 0)
        lax.fori_loop(0, NX, sweep_own, 0, unroll=2)

    def emit(j, carry):
        out[j] = U[0, HALO - 1 + j]
        return carry

    lax.fori_loop(0, NX + 2, emit, 0)


def solve_body(more, *refs):
    (flags, mid, mid_paired, mid_other, frac, now, other, table, given_sum, given_E) = refs[:10]
    vel, pressure = refs[10:12]
    if more:
        faces_paired, faces_other, packed, guess = refs[12:16]
    U, T, E, beyond, lhs = refs[-5:]
    inside = domain(flags)
    even = flags[2] == 1
    top = POWERS - 1
    first_group = jnp.where(even, 0, 1)

    def halo_plane(k):
        return jnp.where(even, HALO - k, HALO + NX - 1 + k)

    def own_plane(depth):
        return jnp.where(even, HALO + depth, HALO + NX - 1 - depth)

    E[...] = jnp.zeros((2, NY, 128), F32)
    for k in range(1, HALO + 1):
        x = jnp.where(even, NX - k, k - 1)
        moments = pltpu.roll(other[NX], (128 - 16 * x) % 128, 1)
        plane = halo_plane(k)
        terms(table, U, E, lhs, plane, plane, other[x], moments, k - 1, first_group)
    for m in range(top, -1, -1):
        for depth in (top - m, top + 1 - m):
            U[m, own_plane(depth)] = jnp.zeros((ROWS, NZ), F32)
    U[0, jnp.where(even, HALO + NX, HALO - 1)] = jnp.zeros((ROWS, NZ), F32)

    for m in range(top - 1, -1, -1):

        def sweep(i, carry, m=m):
            plane = halo_plane(1 + i)
            keep = inside(plane)
            for y in range(0, NY, 32):
                put(U, m, plane, y, U[m, plane, pl.ds(TOP + y, 32)] + keep * beside(U, m + 1, plane, y))
            return carry

        def sweep_own(depth, carry, m=m):
            plane = own_plane(depth)
            for y in range(0, NY, 32):
                put(U, m, plane, y, beside(U, m + 1, plane, y))
            return carry

        lax.fori_loop(0, m + 1, sweep, 0)
        lax.fori_loop(0, top - m, sweep_own, 0)

    for j in range(NX + 2):
        T[j] = given_sum[j] + U[0, HALO - 1 + j]
    ends = sweep_ends([E[0], E[1]], 8 * first_group, inside)
    beyond[...] = given_E[...]
    beyond[first_group] += ends[0]
    beyond[first_group + 1] += ends[1]

    def correct(x, mid, mx):
        plane = x + 1
        slot = x + HALO
        lane = lanes(NY)
        turned = pltpu.roll(beyond[slot // 8], (128 - 16 * (slot % 8) - 1) % 128, 1)
        centre = T[plane, pl.ds(TOP, NY)]
        ahead = jnp.where(lane == NZ - 1, turned, pltpu.roll(centre, NZ - 1, 1))
        behind = jnp.where(lane == 0, turned, pltpu.roll(centre, 1, 1))
        vel[2, x] = mid[2, mx] + 0.1 * (ahead - behind)
        for y in range(0, NY, 32):
            here = pl.ds(TOP + y, 32)
            rows = pl.ds(y, 32)
            p = -T[plane, here]
            pressure[x, rows] = p
            vel[0, x, rows] = mid[0, mx, rows] + 0.1 * (T[plane + 1, here] - T[plane - 1, here])
            vel[1, x, rows] = mid[1, mx, rows] + 0.1 * (
                T[plane, pl.ds(TOP + y + 1, 32)] - T[plane, pl.ds(TOP + y - 1, 32)]
            )
            if more:
                guess[x, rows] = 2.0 * p - now[x, rows]

    def correct_inner(x, carry):
        correct(x, mid, x)
        return carry

    lax.fori_loop(1, NX - 1, correct_inner, 0, unroll=2)
    correct(jnp.where(even, NX - 1, 0), mid_paired, 0)
    correct(jnp.where(even, 0, NX - 1), mid_other, 0)
    if more:
        emit_faces(flags, vel, frac, guess, faces_paired, faces_other)
        packed[...] = pack_columns(lambda k, x: fields_of(vel, frac, guess, k, x))


def shape(*dims):
    return jax.ShapeDtypeStruct(dims, F32)


IN_VMEM = pl.BlockSpec(memory_space=pltpu.VMEM)
IN_SMEM = pl.BlockSpec(memory_space=pltpu.SMEM)
IN_HBM = pl.BlockSpec(memory_space=pltpu.HBM)
ANYWHERE = pl.BlockSpec(memory_space=pl.ANY)
BLOCK = (NX, NY, NZ)
MESSAGE = (NX + 1, NY, NZ)


def pack_call(flags, velocity, fraction, now, old):
    return pl.pallas_call(
        pack_body,
        out_shape=(shape(*MESSAGE), shape(*MESSAGE), shape(NY, 128), shape(*BLOCK)),
        in_specs=[IN_SMEM] + [IN_HBM] * 4,
        out_specs=(IN_VMEM,) * 4,
        scratch_shapes=[pltpu.VMEM((3, *BLOCK), F32)]
        + [pltpu.VMEM(BLOCK, F32)] * 3
        + [pltpu.SemaphoreType.DMA((6,))],
        compiler_params=pltpu.CompilerParams(vmem_limit_bytes=60 * MIB),
        name="pack",
    )(flags, velocity, fraction, now, old)


PADDED = (NX, ROWS, NZ)
PREDICTED = tuple(shape(*PADDED) for _ in range(7)) + (
    shape(3, *BLOCK),
    shape(*BLOCK),
    shape(*MESSAGE),
    shape(NY, 128),
)


def inner_call(velocity, fraction, guess, sides, moments):
    return pl.pallas_call(
        inner_body,
        out_shape=PREDICTED,
        in_specs=[ANYWHERE] * 3 + [IN_VMEM] * 2,
        out_specs=(IN_VMEM,) * 11,
        scratch_shapes=[pltpu.SemaphoreType.DMA((5,))],
        compiler_params=pltpu.CompilerParams(vmem_limit_bytes=16 * MIB),
        cost_estimate=pl.CostEstimate(flops=20_000_000, bytes_accessed=16_000_000, transcendentals=100_000),
        name="inner",
    )(velocity, fraction, guess, sides, moments)


SIDE_SCRATCH = [pltpu.VMEM((2, ROWS, NZ), F32)] * 7 + [
    pltpu.VMEM((NY, 128), F32),
    pltpu.VMEM((NY, NZ), F32),
    pltpu.SemaphoreType.DMA((6,)),
]


def paired_call(flags, message, sides, profile, moments, inner):
    *buffers, mid, _, _, pack = inner
    return pl.pallas_call(
        paired_body,
        out_shape=(shape(3, 1, NY, NZ), shape(NY, NZ), shape(2, NY, NZ), shape(NY, 128)),
        in_specs=[IN_SMEM] + [ANYWHERE] + [IN_VMEM] * 12,
        out_specs=(IN_VMEM,) * 4,
        scratch_shapes=SIDE_SCRATCH,
        compiler_params=pltpu.CompilerParams(vmem_limit_bytes=12 * MIB),
        cost_estimate=pl.CostEstimate(flops=6_000_000, bytes_accessed=6_000_000, transcendentals=30_000),
        name="paired_side",
    )(flags, message, sides, profile, moments, *buffers, mid, pack)


def other_call(flags, message, sides, profile, moments, inner, frac, source, pack):
    *buffers, mid, inner_frac, inner_source, _ = inner
    return pl.pallas_call(
        other_body,
        out_shape=(shape(3, 1, NY, NZ), shape(*BLOCK), shape(*MESSAGE), shape(NY, 128)),
        in_specs=[IN_SMEM] + [ANYWHERE] + [IN_VMEM] * 11 + [ANYWHERE] * 4 + [IN_VMEM],
        out_specs=(IN_VMEM,) * 4,
        scratch_shapes=SIDE_SCRATCH + [pltpu.SemaphoreType.DMA((4,))],
        compiler_params=pltpu.CompilerParams(vmem_limit_bytes=12 * MIB),
        name="other_side",
    )(flags, message, sides, profile, moments, *buffers, mid, inner_frac, inner_source, frac, source, pack)


def combine_call(packs, table, message):
    return pl.pallas_call(
        combine_body,
        out_shape=(shape(*MESSAGE), shape(NY, 128)),
        in_specs=[IN_VMEM] * 5 + [ANYWHERE],
        out_specs=(ANYWHERE, IN_VMEM),
        scratch_shapes=[pltpu.SemaphoreType.DMA],
        input_output_aliases={5: 0},
        compiler_params=pltpu.CompilerParams(vmem_limit_bytes=4 * MIB),
        name="combine",
    )(*packs, table, message)


def merge_call(before, after, right, left):
    return pl.pallas_call(
        merge_body,
        out_shape=(shape(*MESSAGE), shape(*MESSAGE), shape(NY, 128)),
        in_specs=[IN_VMEM] * 2 + [ANYWHERE] * 2,
        out_specs=(ANYWHERE, ANYWHERE, IN_VMEM),
        scratch_shapes=[pltpu.SemaphoreType.DMA((2,))],
        input_output_aliases={2: 0, 3: 1},
        compiler_params=pltpu.CompilerParams(vmem_limit_bytes=4 * MIB),
        name="merge",
    )(before, after, right, left)


OWN_TERMS = (POWERS, NX, ROWS, NZ)


def own_terms_call(source, far, table):
    return pl.pallas_call(
        own_terms_body,
        out_shape=(shape(*OWN_TERMS), shape(3, NY, 128)),
        in_specs=[IN_VMEM] * 3,
        out_specs=(IN_VMEM,) * 2,
        scratch_shapes=[pltpu.VMEM((NY, 512), BF16)],
        compiler_params=pltpu.CompilerParams(vmem_limit_bytes=20 * MIB),
        cost_estimate=pl.CostEstimate(flops=1_000_000_000, bytes_accessed=12_000_000, transcendentals=0),
        name="own_terms",
    )(source, far, table)


def side_terms_call(flags, paired, ends, table):
    return pl.pallas_call(
        side_terms_body,
        out_shape=(shape(POWERS, HALO, ROWS, NZ), shape(3, NY, 128)),
        in_specs=[IN_SMEM] + [IN_VMEM] * 3,
        out_specs=(IN_VMEM,) * 2,
        scratch_shapes=[pltpu.VMEM((NY, 512), BF16)],
        compiler_params=pltpu.CompilerParams(vmem_limit_bytes=12 * MIB),
        cost_estimate=pl.CostEstimate(flops=500_000_000, bytes_accessed=6_000_000, transcendentals=0),
        name="side_terms",
    )(flags, paired, ends, table)


SUM = (NX + 2, ROWS, NZ)
TERMS_SCRATCH = pltpu.VMEM((POWERS, NX + 2 * HALO, ROWS, NZ), F32)


def first_sweeps_call(flags, own, side, ends):
    return pl.pallas_call(
        first_sweeps_body,
        out_shape=(shape(*SUM), shape(3, NY, 128)),
        in_specs=[IN_SMEM] + [IN_VMEM] * 3,
        out_specs=(IN_VMEM,) * 2,
        scratch_shapes=[TERMS_SCRATCH, pltpu.SemaphoreType.DMA, pltpu.SemaphoreType.DMA],
        compiler_params=pltpu.CompilerParams(vmem_limit_bytes=18 * MIB),
        cost_estimate=pl.CostEstimate(flops=10_000_000, bytes_accessed=14_000_000, transcendentals=0),
        name="first_sweeps",
    )(flags, own, side, ends)


def solve_call(more, flags, mid, mid_paired, mid_other, frac, now, other, table, part, ends):
    outs = [shape(3, *BLOCK), shape(*BLOCK)]
    if more:
        outs += [shape(*MESSAGE), shape(*MESSAGE), shape(NY, 128), shape(*BLOCK)]
    return pl.pallas_call(
        functools.partial(solve_body, more),
        out_shape=tuple(outs),
        in_specs=[IN_SMEM] + [IN_VMEM] * 9,
        out_specs=(IN_VMEM,) * len(outs),
        scratch_shapes=[
            TERMS_SCRATCH,
            pltpu.VMEM(SUM, F32),
            pltpu.VMEM((2, NY, 128), F32),
            pltpu.VMEM((3, NY, 128), F32),
            pltpu.VMEM((NY, 512), BF16),
        ],
        compiler_params=pltpu.CompilerParams(vmem_limit_bytes=20 * MIB),
        name="solve",
    )(flags, mid, mid_paired, mid_other, frac, now, other, table, part, ends)


def per_device(velocity, fraction, pressure_now, pressure_old, inflow):
    stream = lax.axis_index("stream")
    count = lax.axis_size("stream")
    flags = jnp.stack([stream == 0, stream == count - 1, stream % 2 == 0]).astype(jnp.int32)
    pairs = [(i, i ^ 1) for i in range(count)]
    others = [(i, ((i + 1) ^ 1) - 1) for i in range(1, count - 1)]

    def exchange(block, with_pair):
        return lax.ppermute(block, "stream", pairs if with_pair else others)

    def around(block, offset):
        return lax.ppermute(
            block, "span", [((i + offset) % BLOCKS, i) for i in range(BLOCKS)]
        )

    profile = jnp.broadcast_to(inflow[:, :, None], (2, NY, NZ))
    moments = jnp.asarray(moment_table())
    combine = jnp.asarray(combine_table())
    table = jnp.asarray(solve_table())

    paired, other, packed, guess = pack_call(flags, velocity, fraction, pressure_now, pressure_old)
    now = pressure_now
    for step in range(STEPS):
        more = step < STEPS - 1
        paired, other, sides = merge_call(around(packed, -1), around(packed, 1), paired, other)
        other = exchange(other, False)
        paired = exchange(paired, True)
        inner = inner_call(velocity, fraction, guess, sides, moments)
        mid_paired, frac, source, pack = paired_call(flags, paired, sides, profile, moments, inner)
        mid_other, fraction, source, pack = other_call(
            flags, other, sides, profile, moments, inner, frac, source, pack
        )
        source, far = combine_call([pack] + [around(pack, o) for o in (1, 2, 3)], combine, source)
        other = exchange(source, False)
        paired = exchange(source, True)
        own, ends = own_terms_call(source, far, table)
        side, ends = side_terms_call(flags, paired, ends, table)
        part, ends = first_sweeps_call(flags, own, side, ends)
        results = solve_call(
            more, flags, inner[7], mid_paired, mid_other, fraction, now, other, table, part, ends
        )
        velocity, pressure = results[:2]
        old, now = now, pressure
        if more:
            paired, other, packed, guess = results[2:]
    return (velocity, fraction, now, old)


def solution(mesh):
    return jax.shard_map(
        per_device,
        mesh=mesh,
        in_specs=(
            P(None, "stream", None, "span"),
            P("stream", None, "span"),
            P("stream", None, "span"),
            P("stream", None, "span"),
            P(),
        ),
        out_specs=(
            P(None, "stream", None, "span"),
            P("stream", None, "span"),
            P("stream", None, "span"),
            P("stream", None, "span"),
        ),
        check_vma=False,
    )
```

```python
import functools
import math

import jax
import jax.numpy as jnp
import numpy as np
from jax import lax
from jax.experimental import pallas as pl
from jax.experimental.pallas import tpu as pltpu
from jax.sharding import PartitionSpec as P

STEPS = 2
POWERS = 7
NX, NY, NZ = 8, 128, 128
TOP = 8
ROWS = NY + 2 * TOP
BLOCKS = 4
F32 = jnp.float32
BF16 = jnp.bfloat16
HIGHEST = lax.Precision.HIGHEST
MIB = 1024 * 1024


def comb(n, k):
    return math.comb(n, k) if 0 <= k <= n else 0


RATIO = 3.0 - 2.0 * math.sqrt(2.0)


def line_kernel(power, n):
    return RATIO ** (power + n) * sum(
        comb(power - 1 + n + k, power - 1) * comb(power - 1 + k, power - 1) * RATIO ** (2 * k)
        for k in range(40)
    )


def far_kernel(power, j, z):
    return RATIO ** (power + 1 + z) * sum(
        comb(power - 1 + k, power - 1) * RATIO ** (2 * k) * comb(power + z + k, power - 1 - j)
        for k in range(40)
    )


@functools.cache
def solve_table():
    near = np.zeros((POWERS, 144, NZ + 2))
    for m in range(POWERS):
        kernel = np.array([line_kernel(m + 1, n) for n in range(NZ + 2)])
        z = np.arange(-1, NZ + 1)
        own = np.arange(NZ)
        near[m, :NZ] = kernel[np.abs(z[None, :] - own[:, None])]
        far = np.array([[far_kernel(m + 1, j, t) for t in z] for j in range(POWERS)])
        near[m, NZ : NZ + POWERS] = far
        near[m, NZ + POWERS : NZ + 2 * POWERS] = far[:, ::-1]
        near[m, NZ + 14] = -2.5 * near[m, 0]
        near[m, NZ + 15] = 2.5 * near[m, NZ - 1]
    wide = np.zeros((144, (POWERS + 1) * NZ))
    wide[:, : POWERS * NZ] = near[:, :, 1:-1].transpose(1, 0, 2).reshape(144, POWERS * NZ)
    for m in range(POWERS):
        wide[:, POWERS * NZ + 2 * m] = near[m, :, -1]
        wide[:, POWERS * NZ + 2 * m + 1] = near[m, :, 0]
    wide = wide.astype(np.float32)
    head = wide.astype(jnp.bfloat16)
    tail = (wide - head.astype(np.float32)).astype(jnp.bfloat16)
    table = np.zeros((512, wide.shape[1]), jnp.bfloat16)
    table[0:128] = head[:NZ]
    table[128:256] = head[:NZ]
    table[256:384] = tail[:NZ]
    table[384:400] = head[NZ:]
    table[400:416] = head[NZ:]
    table[416:432] = tail[NZ:]
    return table


@functools.cache
def moment_table():
    table = np.zeros((2, NZ, 128), np.float32)
    for z in range(NZ):
        for j in range(POWERS):
            table[0, z, j] = comb(z, j) * RATIO**z
            table[0, z, POWERS + j] = comb(NZ - 1 - z, j) * RATIO ** (NZ - 1 - z)
    table[1, 0, 14] = 1.0
    table[1, NZ - 1, 15] = 1.0
    return table


@functools.cache
def combine_table():
    small = np.zeros((BLOCKS, 16, 16))
    end = [comb(NZ - 1, a) * RATIO ** (NZ - 1) for a in range(POWERS)]
    for o in range(1, 2 * BLOCKS + 1):
        gap = NZ * (o - 1)
        for j in range(POWERS):
            for a in range(j + 1):
                factor = comb(gap, j - a) * RATIO**gap
                left = -o
                small[left % BLOCKS, POWERS + a, j] += factor
                small[(left - 1) % BLOCKS, 15, j] += factor * end[a] * -2.5
                small[(left + 1) % BLOCKS, 14, j] += factor * (2.5 if a == 0 else 0.0)
                right = o
                small[right % BLOCKS, a, POWERS + j] += factor
                small[(right - 1) % BLOCKS, 15, POWERS + j] += factor * (-2.5 if a == 0 else 0.0)
                small[(right + 1) % BLOCKS, 14, POWERS + j] += factor * end[a] * 2.5
    small[-1 % BLOCKS, 15, 14] += 1.0
    small[1 % BLOCKS, 14, 15] += 1.0
    table = np.zeros((BLOCKS, 128, 128), np.float32)
    for x in range(NX):
        table[:, 16 * x : 16 * x + 16, 16 * x : 16 * x + 16] = small
    return table


def lanes(rows):
    return lax.broadcasted_iota(jnp.int32, (rows, 128), 1)


def pack_columns(fields, ready=None):
    lane = lanes(NY)
    packed = jnp.zeros((NY, 128), F32)
    for k in (4, 3, 0, 1, 2):
        if ready is not None:
            ready(k)
        for x in range(NX):
            pair = 12 * k + x + 2
            keep = (lane == 2 * pair + 1) | (lane == 2 * pair + 2)
            packed = jnp.where(keep, pltpu.roll(fields(k, x), 2 * pair + 2, 1), packed)
    return packed


def pack_body(flags, vel_far, frac_far, now_far, old_far, paired, other, packed, guess, vel, frac, now, old, sem):
    pairs = [(now_far, now), (old_far, old), (frac_far, frac)] + [(vel_far.at[k], vel.at[k]) for k in range(3)]
    copies = start_copies(pairs, sem)

    def ready(k):
        if k == 4:
            copies[0].wait()
            copies[1].wait()
            for x in range(NX):
                guess[x] = 2.0 * now[x] - old[x]
        else:
            copies[2 if k == 3 else 3 + k].wait()

    packed[...] = pack_columns(lambda k, x: fields_of(vel, frac, guess, k, x), ready)
    emit_faces(flags, vel, frac, guess, paired, other)


def fields_of(vel, frac, guess, k, x):
    return vel[k, x] if k < 3 else (frac[x] if k == 3 else guess[x])


def emit_faces(flags, vel, frac, guess, paired, other):
    even = flags[2] == 1
    for out, upper in ((paired, even), (other, jnp.logical_not(even))):
        two = jnp.where(upper, NX - 2, 0)
        one = jnp.where(upper, NX - 1, 0)
        for k in range(2):
            out[k] = vel[0, two + k]
            out[4 + k] = frac[two + k]
            out[6 + k] = guess[two + k]
        out[2] = vel[1, one]
        out[3] = vel[2, one]


def fill_shifts(buffers, ends, planes, slots):
    U, V, W, F, G, FM, FP = buffers
    own = pl.ds(TOP, NY)
    below, above = pl.ds(TOP - 1, 1), pl.ds(TOP + NY, 1)
    bottom, top = pl.ds(TOP, 1), pl.ds(TOP + NY - 1, 1)
    lane = lanes(NY)
    for e, slot in zip(planes, slots):
        centre = F[e, own]
        turned = pltpu.roll(ends, 128 - 2 * (36 + slot) - 1, 1)
        FM[e, own] = jnp.where(lane == 0, turned, pltpu.roll(centre, 1, 1))
        FP[e, own] = jnp.where(lane == 127, turned, pltpu.roll(centre, 127, 1))
        for buf in (F, FM, FP, G):
            buf[e, below] = buf[e, bottom]
            buf[e, above] = buf[e, top]
        for buf, wall in ((U, 2.0), (V, 0.0), (W, 0.0)):
            buf[e, below] = wall - buf[e, bottom]
            buf[e, above] = -buf[e, top]


def cells(low, at, high, Z, e, y, components):
    U, V, W, F, G, FM, FP = range(7)

    def get(plane, k, rows):
        return plane[0][k][plane[1], rows]

    lane = lanes(8)
    at_low = lane == 0
    at_high = lane == 127
    here, up, down = pl.ds(y + TOP, 8), pl.ds(y + TOP + 1, 8), pl.ds(y + TOP - 1, 8)
    ends_all = Z[pl.ds(y, 8), :]

    def star(k, group):
        centre = get(at, k, here)
        ends = pltpu.roll(ends_all, 128 - 2 * (12 * group + e) - 1, 1)
        behind = jnp.where(at_low, ends, pltpu.roll(centre, 1, 1))
        ahead = jnp.where(at_high, ends, pltpu.roll(centre, 127, 1))
        return centre, (
            (get(high, k, here), get(low, k, here)),
            (get(at, k, up), get(at, k, down)),
            (ahead, behind),
        )

    c = get(at, F, here)
    around = ((get(high, F, here), get(low, F, here)), (get(at, F, up), get(at, F, down)), (get(at, FP, here), get(at, FM, here)))
    d = [p - m for p, m in around]
    second = [p + m - 2.0 * c for p, m in around]
    mxy = (get(high, F, up) - get(high, F, down)) - (get(low, F, up) - get(low, F, down))
    mxz = (get(high, FP, here) - get(high, FM, here)) - (get(low, FP, here) - get(low, FM, here))
    myz = (get(at, FP, up) - get(at, FM, up)) - (get(at, FP, down) - get(at, FM, down))
    dd = [v * v for v in d]
    inverse = lax.rsqrt(jnp.maximum(dd[0] + dd[1] + dd[2], 1.0))
    bend = (dd[0] * second[0] + dd[1] * second[1] + dd[2] * second[2]) + 0.5 * (
        d[0] * (d[1] * mxy + d[2] * mxz) + d[1] * d[2] * myz
    )
    laplace = second[0] + second[1] + second[2]
    volume = 1.0 / (0.5 + 0.5 * c)
    pull = (bend * (inverse * inverse) - laplace) * (0.5 * inverse) * volume
    nu = (0.02 + 0.03 * c) * volume
    if len(components) == 3:
        stars = [star(k, k) for k in (U, V, W)]
        centres = [s[0] for s in stars]
    else:
        stars = [star(U, 0)]
        centres = [stars[0][0], get(at, V, here), get(at, W, here)]
    speeds = [jnp.abs(v) for v in centres]
    if len(components) == 3:
        guesses = star(G, 4)[1]
    else:
        guesses = ((get(high, G, here), get(low, G, here)),)
    lift = 2.0 - volume
    out = []
    for k in components:
        centre, sides_ = stars[k]
        twice = 2.0 * centre
        transport = 0.0
        diffusion = 0.0
        for a in range(3):
            p, m = sides_[a]
            curve = p + m - twice
            transport = transport + (centres[a] * (p - m) - speeds[a] * curve)
            diffusion = diffusion + curve
        change = nu * diffusion + pull * d[k] - 0.5 * transport
        p, m = guesses[k]
        out.append(centre + 0.1 * (change + 0.5 * (lift * (p - m))))
    if len(components) == 1:
        return out
    net = 0.0
    for a in range(3):
        p, m = stars[a][1][a]
        fp, fm = around[a]
        ahead = centres[a] + p
        behind = centres[a] + m
        net = net + (
            (jnp.maximum(ahead, 0.0) - jnp.minimum(behind, 0.0)) * c
            + (jnp.minimum(ahead, 0.0) * fp - jnp.maximum(behind, 0.0) * fm)
        )
    return out + [c - 0.05 * net]


def source_plane(x, before, after, v, w, moments, pack):
    lane = lanes(NY)
    row = lax.broadcasted_iota(jnp.int32, (NY, 128), 0)
    v_up = jnp.where(row == NY - 1, 0.0, pltpu.roll(v, NY - 1, 0))
    v_down = jnp.where(row == 0, 0.0, pltpu.roll(v, 1, 0))
    w_up = jnp.where(lane == NZ - 1, 0.0, pltpu.roll(w, NZ - 1, 1))
    w_down = jnp.where(lane == 0, 0.0, pltpu.roll(w, 1, 1))
    s = 2.5 * ((after - before) + (v_up - v_down) + (w_up - w_down))
    part = jnp.dot(s, moments[0], precision=HIGHEST, preferred_element_type=F32) + jnp.dot(
        w, moments[1], precision=HIGHEST, preferred_element_type=F32
    )
    pack[...] += pltpu.roll(part, 16 * x, 1) if x else part
    return s


def start_copies(pairs, sem):
    copies = [pltpu.make_async_copy(src, dst, sem.at[k]) for k, (src, dst) in enumerate(pairs)]
    for copy in copies:
        copy.start()
    return copies


def inner_body(vel, frac, guess, sides, moments, *refs):
    buffers = refs[:7]
    mid, frac_new, source, pack, sem = refs[7:]
    U, V, W, F, G = buffers[:5]
    own = pl.ds(TOP, NY)
    sources = [vel.at[0], vel.at[1], vel.at[2], frac, guess]
    copies = start_copies([(src, buf.at[pl.ds(0, NX), own]) for src, buf in zip(sources, (U, V, W, F, G))], sem)
    pack[...] = jnp.zeros((NY, 128), F32)
    for copy in copies:
        copy.wait()
    fill_shifts(buffers, sides[...], range(NX), range(2, 2 + NX))

    def block(i, carry):
        x = 1 + i // 16
        y = pl.multiple_of((i % 16) * 8, 8)
        rows = pl.ds(y, 8)
        mid[0, x, rows], mid[1, x, rows], mid[2, x, rows], frac_new[x, rows] = cells(
            (buffers, x - 1), (buffers, x), (buffers, x + 1), sides, x + 2, y, (0, 1, 2)
        )
        return carry

    lax.fori_loop(0, 16 * (NX - 2), block, 0, unroll=4)
    for x in range(2, NX - 2):
        source[x] = source_plane(x, mid[0, x - 1], mid[0, x + 1], mid[1, x], mid[2, x], moments, pack)


def side_part(up, at_end, message, sides, profile, moments, given, given_mid, mid, frac, source, pack, scratch):
    buffers, (Z, end_mid, sem) = scratch[:7], scratch[7:]
    U, V, W, F, G = buffers[:5]
    own = pl.ds(TOP, NY)
    near = 0 if up else 1
    pairs = [
        (message.at[pl.ds(0, 2)], U.at[:, own]),
        (message.at[2], V.at[near, own]),
        (message.at[3], W.at[near, own]),
        (message.at[pl.ds(4, 2)], F.at[:, own]),
        (message.at[pl.ds(6, 2)], G.at[:, own]),
        (message.at[8], Z),
    ]
    for copy in start_copies(pairs, sem):
        copy.wait()
    lane = lanes(NY)
    slot = lane // 2 % 12
    group = lane // 2 // 12
    merged = sides[...]
    if up:
        beyond = pltpu.roll(Z[...], 16, 1)
        if at_end is not None:
            wall = jnp.where(slot == 10, pltpu.roll(merged, 2, 1), pltpu.roll(merged, 4, 1))
            beyond = jnp.where(at_end, wall, beyond)
        Z[...] = jnp.where(slot >= 10, beyond, merged)
    else:
        beyond = pltpu.roll(Z[...], 112, 1)
        if at_end is not None:
            wall = jnp.where(group == 0, profile[0], jnp.where(group == 3, profile[1], 0.0))
            beyond = jnp.where(at_end, wall, beyond)
        Z[...] = jnp.where(slot < 2, beyond, merged)
    if at_end is not None:

        @pl.when(at_end)
        def _():
            for e in range(2):
                U[e, own] = given[0][NX - 1, own] if up else profile[0]
                F[e, own] = given[3][NX - 1, own] if up else profile[1]
            if up:
                V[near, own] = given[1][NX - 1, own]
                W[near, own] = given[2][NX - 1, own]

    fill_shifts(buffers, Z[...], range(2), (10, 11) if up else (0, 1))
    halo = [(buffers, 0), (buffers, 1)]
    line = [(given, NX - 2), (given, NX - 1)] + halo if up else halo + [(given, 0), (given, 1)]
    inside, outside = (line[:3], line[1:]) if up else (line[1:], line[:3])

    def block(i, carry):
        y = pl.multiple_of(i * 8, 8)
        rows = pl.ds(y, 8)
        mid[0, rows], mid[1, rows], mid[2, rows], frac[rows] = cells(*inside, Z, 9 if up else 2, y, (0, 1, 2))
        (end_mid[rows],) = cells(*outside, Z, 10 if up else 1, y, (0,))
        return carry

    lax.fori_loop(0, 16, block, 0, unroll=2)
    if up:
        source[0] = source_plane(6, given_mid[0, 5], mid[0], given_mid[1, 6], given_mid[2, 6], moments, pack)
        source[1] = source_plane(7, given_mid[0, 6], end_mid[...], mid[1], mid[2], moments, pack)
    else:
        source[0] = source_plane(0, end_mid[...], given_mid[0, 1], mid[1], mid[2], moments, pack)
        source[1] = source_plane(1, mid[0], given_mid[0, 2], given_mid[1, 1], given_mid[2, 1], moments, pack)


def paired_body(flags, message, sides, profile, moments, *refs):
    given, given_mid, given_pack = refs[:7], refs[7], refs[8]
    mid, frac, source, pack = refs[9:13]
    pack[...] = given_pack[...]
    for up in (True, False):

        @pl.when(flags[2] == int(up))
        def _(up=up):
            side_part(
                up, None, message, sides, profile, moments, given, given_mid, mid.at[:, 0], frac, source, pack, refs[13:]
            )


def other_body(flags, message, sides, profile, moments, *refs):
    given, (given_mid, given_frac, given_source) = refs[:7], refs[7:10]
    paired_frac, paired_source, given_pack = refs[10:13]
    mid, frac_new, source, to_paired, to_other, pack = refs[13:19]
    scratch, keep_sem = refs[19:-1], refs[-1]
    even = flags[2] == 1
    middle = pl.ds(1, NX - 2)
    kept = [
        (given_frac.at[middle], frac_new.at[middle]),
        (paired_frac, frac_new.at[jnp.where(even, NX - 1, 0)]),
        (paired_source, source.at[pl.ds(jnp.where(even, NX - 2, 0), 2)]),
        (paired_source, to_paired.at[pl.ds(jnp.where(even, NX - 3, 0), 2)]),
        (paired_source.at[jnp.where(even, 0, 1)], to_other.at[jnp.where(even, NX - 2, 0)]),
    ]
    for out, place in ((source, 2), (to_paired, jnp.where(even, 1, 2)), (to_other, jnp.where(even, 2, 1))):
        kept.append((given_source.at[pl.ds(2, NX - 4)], out.at[pl.ds(place, NX - 4)]))
    kept = start_copies(kept, keep_sem)
    pack[...] = given_pack[...]
    for up in (True, False):

        @pl.when(flags[2] == 1 - int(up))
        def _(up=up):
            side_part(
                up,
                flags[1 if up else 0] == 1,
                message, sides, profile, moments, given, given_mid,
                mid.at[:, 0],
                frac_new.at[NX - 1 if up else 0],
                source.at[pl.ds(NX - 2 if up else 0, 2)],
                pack,
                scratch,
            )

    place = jnp.where(even, 0, NX - 2)
    for k in range(2):
        to_other[jnp.where(even, 0, NX - 3) + k] = source[place + k]
    to_paired[place] = source[jnp.where(even, 1, NX - 2)]
    for copy in kept:
        copy.wait()


def combine_body(a, b, c, d, table, _, __, to_paired, to_other, out, sem):
    total = 0.0
    for k, ref in enumerate((a, b, c, d)):
        total = total + jnp.dot(ref[...], table[k], precision=HIGHEST, preferred_element_type=F32)
    out[...] = total
    for copy in start_copies([(out, message.at[NX - 1]) for message in (to_paired, to_other)], sem):
        copy.wait()


def merge_body(before, after, _, __, right, left, out, sem):
    lane = lanes(NY)
    out[...] = jnp.where(lane % 2 == 1, before[...], pltpu.roll(after[...], 126, 1))
    copies = [pltpu.make_async_copy(out, m.at[NX], sem.at[k]) for k, m in enumerate((right, left))]
    for copy in copies:
        copy.start()
    for copy in copies:
        copy.wait()


HALO = POWERS


def put(out, m, plane, y, value):
    size = value.shape[0]
    out[m, plane, pl.ds(TOP + y, size)] = value
    if y == 0:
        out[m, plane, pl.ds(TOP - 1, 1)] = value[:1]
    if y + size == NY:
        out[m, plane, pl.ds(TOP + NY, 1)] = value[size - 1 :]


def terms(table, U, E, lhs, row, plane, values, moments, start, first_group=0):
    lane = lanes(NY)
    head = values.astype(BF16)
    tail = (values - head.astype(F32)).astype(BF16)
    m_head = moments.astype(BF16).astype(F32)
    m_tail = moments - m_head
    side = jnp.where(
        lane < 16,
        m_head,
        jnp.where(
            lane < 32,
            pltpu.roll(m_tail, 16, 1),
            jnp.where(lane < 48, pltpu.roll(m_head, 32, 1), 0.0),
        ),
    )
    lhs[:, 0:128] = head
    lhs[:, 128:256] = tail
    lhs[:, 256:384] = head
    lhs[:, 384:512] = side.astype(BF16)
    result = jnp.dot(lhs[...], table[:, start * 128 :], preferred_element_type=F32)
    for m in range(start, POWERS):
        put(U, m, row, 0, result[:, (m - start) * 128 : (m - start + 1) * 128])
    ends = result[:, (POWERS - start) * 128 :]
    group, offset = plane // 8 - first_group, 16 * (plane % 8)
    E[group] += pltpu.roll(ends, offset, 1)


def own_terms_body(source, far, table, U, E, lhs):
    E[...] = jnp.zeros((3, NY, 128), F32)

    def own_plane(x, carry):
        moments = pltpu.roll(far[...], (128 - 16 * x) % 128, 1)
        terms(table, U, E, lhs, x, x + HALO, source[x], moments, 0)
        return carry

    lax.fori_loop(0, NX, own_plane, 0)


def side_terms_body(flags, paired, given_E, table, U, E, lhs):
    even = flags[2] == 1
    E[...] = given_E[...]
    for k in range(1, HALO + 1):
        x = jnp.where(even, k - 1, NX - k)
        moments = pltpu.roll(paired[NX - 1], (128 - 16 * x) % 128, 1)
        plane = jnp.where(even, HALO + NX - 1 + k, HALO - k)
        place = jnp.where(even, k - 1, HALO - k)
        terms(table, U, E, lhs, place, plane, paired[place], moments, k - 1)


def domain(flags):
    first = flags[0] == 1
    last = flags[1] == 1

    def inside(plane):
        kept = ((plane >= HALO) | jnp.logical_not(first)) & ((plane < HALO + NX) | jnp.logical_not(last))
        return jnp.where(kept, 1.0, 0.0).astype(F32)

    return inside


def beside(U, m, plane, y):
    here = pl.ds(TOP + y, 32)
    return (U[m, plane - 1, here] + U[m, plane + 1, here]) + (
        U[m, plane, pl.ds(TOP + y - 1, 32)] + U[m, plane, pl.ds(TOP + y + 1, 32)]
    )


def sweep_ends(start, first_plane, inside):
    count = len(start)
    lane = lanes(NY)
    row = lax.broadcasted_iota(jnp.int32, (NY, 128), 0)
    used = lane % 16 < 14
    keeps = [jnp.where(used, inside(first_plane + 8 * g + lane // 16), 0.0) for g in range(count)]
    ends = start
    for m in range(POWERS - 1):
        before = [pltpu.roll(e, 14, 1) for e in ends]
        after = [pltpu.roll(e, 110, 1) for e in ends]
        same = [pltpu.roll(e, 126, 1) for e in ends]
        updated = []
        for g in range(count):
            behind = jnp.where(lane < 16, before[g - 1] if g else 0.0, before[g])
            ahead = jnp.where(lane >= 112, after[g + 1] if g < count - 1 else 0.0, after[g])
            up = jnp.where(row == NY - 1, same[g], pltpu.roll(same[g], NY - 1, 0))
            down = jnp.where(row == 0, same[g], pltpu.roll(same[g], 1, 0))
            updated.append(start[g] + keeps[g] * ((behind + ahead) + (up + down)))
        ends = updated
    return ends


def first_sweeps_body(flags, given_U, given_side, given_E, out, E, U, sem, side_sem):
    inside = domain(flags)
    even = flags[2] == 1
    top = POWERS - 1
    fetches = [
        pltpu.make_async_copy(given_U.at[top], U.at[top, pl.ds(HALO, NX)], sem),
        pltpu.make_async_copy(given_side.at[top], U.at[top, pl.ds(jnp.where(even, HALO + NX, 0), HALO)], side_sem),
    ]
    for fetch in fetches:
        fetch.start()

    def clear(i, carry):
        U[top, jnp.where(even, i, HALO + NX + i)] = jnp.zeros((ROWS, NZ), F32)
        return carry

    lax.fori_loop(0, HALO, clear, 0)
    for g, value in enumerate(sweep_ends([given_E[g] for g in range(3)], 0, inside)):
        E[g] = value
    for fetch in fetches:
        fetch.wait()

    for m in range(top - 1, -1, -1):

        def sweep(i, carry, m=m):
            low, high = HALO - 1 - i, HALO + NX + i
            plane = jnp.where(even, high, low)
            place = jnp.where(even, i, HALO - 1 - i)
            far_plane = jnp.where(even, low, high)
            keep = inside(far_plane)
            for y in range(0, NY, 32):
                here = pl.ds(TOP + y, 32)
                put(U, m, plane, y, given_side[m, place, here] + beside(U, m + 1, plane, y))
                put(U, m, far_plane, y, keep * beside(U, m + 1, far_plane, y))
            return carry

        def sweep_own(x, carry, m=m):
            for y in range(0, NY, 32):
                put(
                    U, m, x + HALO, y,
                    given_U[m, x, pl.ds(TOP + y, 32)] + beside(U, m + 1, x + HALO, y),
                )
            return carry

        lax.fori_loop(0, m + 1, sweep, 0)
        lax.fori_loop(0, NX, sweep_own, 0, unroll=2)

    def emit(j, carry):
        out[j] = U[0, HALO - 1 + j]
        return carry

    lax.fori_loop(0, NX + 2, emit, 0)


def solve_body(more, *refs):
    (flags, mid, mid_paired, mid_other, frac, now, other, table, given_sum, given_E) = refs[:10]
    vel, pressure = refs[10:12]
    if more:
        faces_paired, faces_other, packed, guess = refs[12:16]
    U, T, E, beyond, lhs = refs[-5:]
    inside = domain(flags)
    even = flags[2] == 1
    top = POWERS - 1
    first_group = jnp.where(even, 0, 1)

    def halo_plane(k):
        return jnp.where(even, HALO - k, HALO + NX - 1 + k)

    def own_plane(depth):
        return jnp.where(even, HALO + depth, HALO + NX - 1 - depth)

    E[...] = jnp.zeros((2, NY, 128), F32)
    for k in range(1, HALO + 1):
        x = jnp.where(even, NX - k, k - 1)
        moments = pltpu.roll(other[NX - 1], (128 - 16 * x) % 128, 1)
        plane = halo_plane(k)
        place = jnp.where(even, HALO - k, k - 1)
        terms(table, U, E, lhs, plane, plane, other[place], moments, k - 1, first_group)
    for m in range(top, -1, -1):
        for depth in (top - m, top + 1 - m):
            U[m, own_plane(depth)] = jnp.zeros((ROWS, NZ), F32)
    U[0, jnp.where(even, HALO + NX, HALO - 1)] = jnp.zeros((ROWS, NZ), F32)

    for m in range(top - 1, -1, -1):

        def sweep(i, carry, m=m):
            plane = halo_plane(1 + i)
            keep = inside(plane)
            for y in range(0, NY, 32):
                put(U, m, plane, y, U[m, plane, pl.ds(TOP + y, 32)] + keep * beside(U, m + 1, plane, y))
            return carry

        def sweep_own(depth, carry, m=m):
            plane = own_plane(depth)
            for y in range(0, NY, 32):
                put(U, m, plane, y, beside(U, m + 1, plane, y))
            return carry

        lax.fori_loop(0, m + 1, sweep, 0)
        lax.fori_loop(0, top - m, sweep_own, 0)

    for j in range(NX + 2):
        T[j] = given_sum[j] + U[0, HALO - 1 + j]
    ends = sweep_ends([E[0], E[1]], 8 * first_group, inside)
    beyond[...] = given_E[...]
    beyond[first_group] += ends[0]
    beyond[first_group + 1] += ends[1]

    def correct(x, mid, mx):
        plane = x + 1
        slot = x + HALO
        lane = lanes(NY)
        turned = pltpu.roll(beyond[slot // 8], (128 - 16 * (slot % 8) - 1) % 128, 1)
        centre = T[plane, pl.ds(TOP, NY)]
        ahead = jnp.where(lane == NZ - 1, turned, pltpu.roll(centre, NZ - 1, 1))
        behind = jnp.where(lane == 0, turned, pltpu.roll(centre, 1, 1))
        vel[2, x] = mid[2, mx] + 0.1 * (ahead - behind)
        for y in range(0, NY, 32):
            here = pl.ds(TOP + y, 32)
            rows = pl.ds(y, 32)
            p = -T[plane, here]
            pressure[x, rows] = p
            vel[0, x, rows] = mid[0, mx, rows] + 0.1 * (T[plane + 1, here] - T[plane - 1, here])
            vel[1, x, rows] = mid[1, mx, rows] + 0.1 * (
                T[plane, pl.ds(TOP + y + 1, 32)] - T[plane, pl.ds(TOP + y - 1, 32)]
            )
            if more:
                guess[x, rows] = 2.0 * p - now[x, rows]

    def correct_inner(x, carry):
        correct(x, mid, x)
        return carry

    lax.fori_loop(1, NX - 1, correct_inner, 0, unroll=2)
    correct(jnp.where(even, NX - 1, 0), mid_paired, 0)
    correct(jnp.where(even, 0, NX - 1), mid_other, 0)
    if more:
        emit_faces(flags, vel, frac, guess, faces_paired, faces_other)
        packed[...] = pack_columns(lambda k, x: fields_of(vel, frac, guess, k, x))


def shape(*dims):
    return jax.ShapeDtypeStruct(dims, F32)


IN_VMEM = pl.BlockSpec(memory_space=pltpu.VMEM)
IN_SMEM = pl.BlockSpec(memory_space=pltpu.SMEM)
IN_HBM = pl.BlockSpec(memory_space=pltpu.HBM)
ANYWHERE = pl.BlockSpec(memory_space=pl.ANY)
BLOCK = (NX, NY, NZ)
MESSAGE = (NX + 1, NY, NZ)


def pack_call(flags, velocity, fraction, now, old):
    return pl.pallas_call(
        pack_body,
        out_shape=(shape(*MESSAGE), shape(*MESSAGE), shape(NY, 128), shape(*BLOCK)),
        in_specs=[IN_SMEM] + [IN_HBM] * 4,
        out_specs=(IN_VMEM,) * 4,
        scratch_shapes=[pltpu.VMEM((3, *BLOCK), F32)]
        + [pltpu.VMEM(BLOCK, F32)] * 3
        + [pltpu.SemaphoreType.DMA((6,))],
        compiler_params=pltpu.CompilerParams(vmem_limit_bytes=60 * MIB),
        name="pack",
    )(flags, velocity, fraction, now, old)


PADDED = (NX, ROWS, NZ)
PREDICTED = tuple(shape(*PADDED) for _ in range(7)) + (
    shape(3, *BLOCK),
    shape(*BLOCK),
    shape(*BLOCK),
    shape(NY, 128),
)


def inner_call(velocity, fraction, guess, sides, moments):
    return pl.pallas_call(
        inner_body,
        out_shape=PREDICTED,
        in_specs=[ANYWHERE] * 3 + [IN_VMEM] * 2,
        out_specs=(IN_VMEM,) * 11,
        scratch_shapes=[pltpu.SemaphoreType.DMA((5,))],
        compiler_params=pltpu.CompilerParams(vmem_limit_bytes=16 * MIB),
        cost_estimate=pl.CostEstimate(flops=20_000_000, bytes_accessed=16_000_000, transcendentals=100_000),
        name="inner",
    )(velocity, fraction, guess, sides, moments)


SIDE_SCRATCH = [pltpu.VMEM((2, ROWS, NZ), F32)] * 7 + [
    pltpu.VMEM((NY, 128), F32),
    pltpu.VMEM((NY, NZ), F32),
    pltpu.SemaphoreType.DMA((6,)),
]


def paired_call(flags, message, sides, profile, moments, inner):
    *buffers, mid, _, _, pack = inner
    return pl.pallas_call(
        paired_body,
        out_shape=(shape(3, 1, NY, NZ), shape(NY, NZ), shape(2, NY, NZ), shape(NY, 128)),
        in_specs=[IN_SMEM] + [ANYWHERE] + [IN_VMEM] * 12,
        out_specs=(IN_VMEM,) * 4,
        scratch_shapes=SIDE_SCRATCH,
        compiler_params=pltpu.CompilerParams(vmem_limit_bytes=12 * MIB),
        cost_estimate=pl.CostEstimate(flops=6_000_000, bytes_accessed=6_000_000, transcendentals=30_000),
        name="paired_side",
    )(flags, message, sides, profile, moments, *buffers, mid, pack)


def other_call(flags, message, sides, profile, moments, inner, frac, source, pack):
    *buffers, mid, inner_frac, inner_source, _ = inner
    return pl.pallas_call(
        other_body,
        out_shape=(shape(3, 1, NY, NZ), *[shape(*BLOCK)] * 4, shape(NY, 128)),
        in_specs=[IN_SMEM] + [ANYWHERE] + [IN_VMEM] * 11 + [ANYWHERE] * 4 + [IN_VMEM],
        out_specs=(IN_VMEM,) * 6,
        scratch_shapes=SIDE_SCRATCH + [pltpu.SemaphoreType.DMA((8,))],
        compiler_params=pltpu.CompilerParams(vmem_limit_bytes=12 * MIB),
        name="other_side",
    )(flags, message, sides, profile, moments, *buffers, mid, inner_frac, inner_source, frac, source, pack)


def combine_call(packs, table, to_paired, to_other):
    return pl.pallas_call(
        combine_body,
        out_shape=(shape(*BLOCK), shape(*BLOCK), shape(NY, 128)),
        in_specs=[IN_VMEM] * 5 + [ANYWHERE] * 2,
        out_specs=(ANYWHERE, ANYWHERE, IN_VMEM),
        scratch_shapes=[pltpu.SemaphoreType.DMA((2,))],
        input_output_aliases={5: 0, 6: 1},
        compiler_params=pltpu.CompilerParams(vmem_limit_bytes=4 * MIB),
        name="combine",
    )(*packs, table, to_paired, to_other)


def merge_call(before, after, right, left):
    return pl.pallas_call(
        merge_body,
        out_shape=(shape(*MESSAGE), shape(*MESSAGE), shape(NY, 128)),
        in_specs=[IN_VMEM] * 2 + [ANYWHERE] * 2,
        out_specs=(ANYWHERE, ANYWHERE, IN_VMEM),
        scratch_shapes=[pltpu.SemaphoreType.DMA((2,))],
        input_output_aliases={2: 0, 3: 1},
        compiler_params=pltpu.CompilerParams(vmem_limit_bytes=4 * MIB),
        name="merge",
    )(before, after, right, left)


OWN_TERMS = (POWERS, NX, ROWS, NZ)


def own_terms_call(source, far, table):
    return pl.pallas_call(
        own_terms_body,
        out_shape=(shape(*OWN_TERMS), shape(3, NY, 128)),
        in_specs=[IN_VMEM] * 3,
        out_specs=(IN_VMEM,) * 2,
        scratch_shapes=[pltpu.VMEM((NY, 512), BF16)],
        compiler_params=pltpu.CompilerParams(vmem_limit_bytes=20 * MIB),
        cost_estimate=pl.CostEstimate(flops=1_000_000_000, bytes_accessed=12_000_000, transcendentals=0),
        name="own_terms",
    )(source, far, table)


def side_terms_call(flags, paired, ends, table):
    return pl.pallas_call(
        side_terms_body,
        out_shape=(shape(POWERS, HALO, ROWS, NZ), shape(3, NY, 128)),
        in_specs=[IN_SMEM] + [IN_VMEM] * 3,
        out_specs=(IN_VMEM,) * 2,
        scratch_shapes=[pltpu.VMEM((NY, 512), BF16)],
        compiler_params=pltpu.CompilerParams(vmem_limit_bytes=12 * MIB),
        cost_estimate=pl.CostEstimate(flops=500_000_000, bytes_accessed=6_000_000, transcendentals=0),
        name="side_terms",
    )(flags, paired, ends, table)


SUM = (NX + 2, ROWS, NZ)
TERMS_SCRATCH = pltpu.VMEM((POWERS, NX + 2 * HALO, ROWS, NZ), F32)


def first_sweeps_call(flags, own, side, ends):
    return pl.pallas_call(
        first_sweeps_body,
        out_shape=(shape(*SUM), shape(3, NY, 128)),
        in_specs=[IN_SMEM] + [IN_VMEM] * 3,
        out_specs=(IN_VMEM,) * 2,
        scratch_shapes=[TERMS_SCRATCH, pltpu.SemaphoreType.DMA, pltpu.SemaphoreType.DMA],
        compiler_params=pltpu.CompilerParams(vmem_limit_bytes=18 * MIB),
        cost_estimate=pl.CostEstimate(flops=10_000_000, bytes_accessed=14_000_000, transcendentals=0),
        name="first_sweeps",
    )(flags, own, side, ends)


def solve_call(more, flags, mid, mid_paired, mid_other, frac, now, other, table, part, ends):
    outs = [shape(3, *BLOCK), shape(*BLOCK)]
    if more:
        outs += [shape(*MESSAGE), shape(*MESSAGE), shape(NY, 128), shape(*BLOCK)]
    return pl.pallas_call(
        functools.partial(solve_body, more),
        out_shape=tuple(outs),
        in_specs=[IN_SMEM] + [IN_VMEM] * 9,
        out_specs=(IN_VMEM,) * len(outs),
        scratch_shapes=[
            TERMS_SCRATCH,
            pltpu.VMEM(SUM, F32),
            pltpu.VMEM((2, NY, 128), F32),
            pltpu.VMEM((3, NY, 128), F32),
            pltpu.VMEM((NY, 512), BF16),
        ],
        compiler_params=pltpu.CompilerParams(vmem_limit_bytes=20 * MIB),
        name="solve",
    )(flags, mid, mid_paired, mid_other, frac, now, other, table, part, ends)


def per_device(velocity, fraction, pressure_now, pressure_old, inflow):
    stream = lax.axis_index("stream")
    count = lax.axis_size("stream")
    flags = jnp.stack([stream == 0, stream == count - 1, stream % 2 == 0]).astype(jnp.int32)
    pairs = [(i, i ^ 1) for i in range(count)]
    others = [(i, ((i + 1) ^ 1) - 1) for i in range(1, count - 1)]

    def exchange(block, with_pair):
        return lax.ppermute(block, "stream", pairs if with_pair else others)

    def around(block, offset):
        return lax.ppermute(
            block, "span", [((i + offset) % BLOCKS, i) for i in range(BLOCKS)]
        )

    profile = jnp.broadcast_to(inflow[:, :, None], (2, NY, NZ))
    moments = jnp.asarray(moment_table())
    combine = jnp.asarray(combine_table())
    table = jnp.asarray(solve_table())

    paired, other, packed, guess = pack_call(flags, velocity, fraction, pressure_now, pressure_old)
    now = pressure_now
    for step in range(STEPS):
        more = step < STEPS - 1
        paired, other, sides = merge_call(around(packed, -1), around(packed, 1), paired, other)
        other = exchange(other, False)
        paired = exchange(paired, True)
        inner = inner_call(velocity, fraction, guess, sides, moments)
        mid_paired, frac, source, pack = paired_call(flags, paired, sides, profile, moments, inner)
        mid_other, fraction, source, to_paired, to_other, pack = other_call(
            flags, other, sides, profile, moments, inner, frac, source, pack
        )
        packs = [pack] + [around(pack, o) for o in (1, 2, 3)]
        to_paired, to_other, far = combine_call(packs, combine, to_paired, to_other)
        other = exchange(to_other, False)
        paired = exchange(to_paired, True)
        own, ends = own_terms_call(source, far, table)
        side, ends = side_terms_call(flags, paired, ends, table)
        part, ends = first_sweeps_call(flags, own, side, ends)
        results = solve_call(
            more, flags, inner[7], mid_paired, mid_other, fraction, now, other, table, part, ends
        )
        velocity, pressure = results[:2]
        old, now = now, pressure
        if more:
            paired, other, packed, guess = results[2:]
    return (velocity, fraction, now, old)


def solution(mesh):
    return jax.shard_map(
        per_device,
        mesh=mesh,
        in_specs=(
            P(None, "stream", None, "span"),
            P("stream", None, "span"),
            P("stream", None, "span"),
            P("stream", None, "span"),
            P(),
        ),
        out_specs=(
            P(None, "stream", None, "span"),
            P("stream", None, "span"),
            P("stream", None, "span"),
            P("stream", None, "span"),
        ),
        check_vma=False,
    )
```

```python
import functools
import math

import jax
import jax.numpy as jnp
import numpy as np
from jax import lax
from jax.experimental import pallas as pl
from jax.experimental.pallas import tpu as pltpu
from jax.sharding import PartitionSpec as P

STEPS = 2
POWERS = 7
NX, NY, NZ = 8, 128, 128
TOP = 8
ROWS = NY + 2 * TOP
BLOCKS = 4
F32 = jnp.float32
BF16 = jnp.bfloat16
HIGHEST = lax.Precision.HIGHEST
MIB = 1024 * 1024


def comb(n, k):
    return math.comb(n, k) if 0 <= k <= n else 0


RATIO = 3.0 - 2.0 * math.sqrt(2.0)


def line_kernel(power, n):
    return RATIO ** (power + n) * sum(
        comb(power - 1 + n + k, power - 1) * comb(power - 1 + k, power - 1) * RATIO ** (2 * k)
        for k in range(40)
    )


def far_kernel(power, j, z):
    return RATIO ** (power + 1 + z) * sum(
        comb(power - 1 + k, power - 1) * RATIO ** (2 * k) * comb(power + z + k, power - 1 - j)
        for k in range(40)
    )


@functools.cache
def solve_table():
    near = np.zeros((POWERS, 144, NZ + 2))
    for m in range(POWERS):
        kernel = np.array([line_kernel(m + 1, n) for n in range(NZ + 2)])
        z = np.arange(-1, NZ + 1)
        own = np.arange(NZ)
        near[m, :NZ] = kernel[np.abs(z[None, :] - own[:, None])]
        far = np.array([[far_kernel(m + 1, j, t) for t in z] for j in range(POWERS)])
        near[m, NZ : NZ + POWERS] = far
        near[m, NZ + POWERS : NZ + 2 * POWERS] = far[:, ::-1]
        near[m, NZ + 14] = -2.5 * near[m, 0]
        near[m, NZ + 15] = 2.5 * near[m, NZ - 1]
    wide = np.zeros((144, (POWERS + 1) * NZ))
    wide[:, : POWERS * NZ] = near[:, :, 1:-1].transpose(1, 0, 2).reshape(144, POWERS * NZ)
    for m in range(POWERS):
        wide[:, POWERS * NZ + 2 * m] = near[m, :, -1]
        wide[:, POWERS * NZ + 2 * m + 1] = near[m, :, 0]
    wide = wide.astype(np.float32)
    head = wide.astype(jnp.bfloat16)
    tail = (wide - head.astype(np.float32)).astype(jnp.bfloat16)
    table = np.zeros((512, wide.shape[1]), jnp.bfloat16)
    table[0:128] = head[:NZ]
    table[128:256] = head[:NZ]
    table[256:384] = tail[:NZ]
    table[384:400] = head[NZ:]
    table[400:416] = head[NZ:]
    table[416:432] = tail[NZ:]
    return table


@functools.cache
def moment_table():
    table = np.zeros((2, NZ, 128), np.float32)
    for z in range(NZ):
        for j in range(POWERS):
            table[0, z, j] = comb(z, j) * RATIO**z
            table[0, z, POWERS + j] = comb(NZ - 1 - z, j) * RATIO ** (NZ - 1 - z)
    table[1, 0, 14] = 1.0
    table[1, NZ - 1, 15] = 1.0
    return table


@functools.cache
def combine_table():
    small = np.zeros((BLOCKS, 16, 16))
    end = [comb(NZ - 1, a) * RATIO ** (NZ - 1) for a in range(POWERS)]
    for o in range(1, 2 * BLOCKS + 1):
        gap = NZ * (o - 1)
        for j in range(POWERS):
            for a in range(j + 1):
                factor = comb(gap, j - a) * RATIO**gap
                left = -o
                small[left % BLOCKS, POWERS + a, j] += factor
                small[(left - 1) % BLOCKS, 15, j] += factor * end[a] * -2.5
                small[(left + 1) % BLOCKS, 14, j] += factor * (2.5 if a == 0 else 0.0)
                right = o
                small[right % BLOCKS, a, POWERS + j] += factor
                small[(right - 1) % BLOCKS, 15, POWERS + j] += factor * (-2.5 if a == 0 else 0.0)
                small[(right + 1) % BLOCKS, 14, POWERS + j] += factor * end[a] * 2.5
    small[-1 % BLOCKS, 15, 14] += 1.0
    small[1 % BLOCKS, 14, 15] += 1.0
    table = np.zeros((BLOCKS, 128, 128), np.float32)
    for x in range(NX):
        table[:, 16 * x : 16 * x + 16, 16 * x : 16 * x + 16] = small
    return table


def lanes(rows):
    return lax.broadcasted_iota(jnp.int32, (rows, 128), 1)


def pack_columns(fields, ready=None):
    lane = lanes(NY)
    packed = jnp.zeros((NY, 128), F32)
    for k in (4, 3, 0, 1, 2):
        if ready is not None:
            ready(k)
        for x in range(NX):
            pair = 12 * k + x + 2
            keep = (lane == 2 * pair + 1) | (lane == 2 * pair + 2)
            packed = jnp.where(keep, pltpu.roll(fields(k, x), 2 * pair + 2, 1), packed)
    return packed


def pack_body(flags, vel_far, frac_far, now_far, old_far, paired, other, packed, guess, vel, frac, now, old, sem):
    pairs = [(now_far, now), (old_far, old), (frac_far, frac)] + [(vel_far.at[k], vel.at[k]) for k in range(3)]
    copies = start_copies(pairs, sem)

    def ready(k):
        if k == 4:
            copies[0].wait()
            copies[1].wait()
            for x in range(NX):
                guess[x] = 2.0 * now[x] - old[x]
        else:
            copies[2 if k == 3 else 3 + k].wait()

    packed[...] = pack_columns(lambda k, x: fields_of(vel, frac, guess, k, x), ready)
    emit_faces(flags, vel, frac, guess, paired, other)


def fields_of(vel, frac, guess, k, x):
    return vel[k, x] if k < 3 else (frac[x] if k == 3 else guess[x])


def emit_faces(flags, vel, frac, guess, paired, other):
    even = flags[2] == 1
    for out, upper in ((paired, even), (other, jnp.logical_not(even))):
        two = jnp.where(upper, NX - 2, 0)
        one = jnp.where(upper, NX - 1, 0)
        for k in range(2):
            out[k] = vel[0, two + k]
            out[4 + k] = frac[two + k]
            out[6 + k] = guess[two + k]
        out[2] = vel[1, one]
        out[3] = vel[2, one]


def fill_shifts(buffers, ends, planes, slots):
    U, V, W, F, G, FM, FP = buffers
    own = pl.ds(TOP, NY)
    below, above = pl.ds(TOP - 1, 1), pl.ds(TOP + NY, 1)
    bottom, top = pl.ds(TOP, 1), pl.ds(TOP + NY - 1, 1)
    lane = lanes(NY)
    for e, slot in zip(planes, slots):
        centre = F[e, own]
        turned = pltpu.roll(ends, 128 - 2 * (36 + slot) - 1, 1)
        FM[e, own] = jnp.where(lane == 0, turned, pltpu.roll(centre, 1, 1))
        FP[e, own] = jnp.where(lane == 127, turned, pltpu.roll(centre, 127, 1))
        for buf in (F, FM, FP, G):
            buf[e, below] = buf[e, bottom]
            buf[e, above] = buf[e, top]
        for buf, wall in ((U, 2.0), (V, 0.0), (W, 0.0)):
            buf[e, below] = wall - buf[e, bottom]
            buf[e, above] = -buf[e, top]


def cells(low, at, high, Z, e, y, components):
    U, V, W, F, G, FM, FP = range(7)

    def get(plane, k, rows):
        return plane[0][k][plane[1], rows]

    lane = lanes(8)
    at_low = lane == 0
    at_high = lane == 127
    here, up, down = pl.ds(y + TOP, 8), pl.ds(y + TOP + 1, 8), pl.ds(y + TOP - 1, 8)
    ends_all = Z[pl.ds(y, 8), :]

    def star(k, group):
        centre = get(at, k, here)
        ends = pltpu.roll(ends_all, 128 - 2 * (12 * group + e) - 1, 1)
        behind = jnp.where(at_low, ends, pltpu.roll(centre, 1, 1))
        ahead = jnp.where(at_high, ends, pltpu.roll(centre, 127, 1))
        return centre, (
            (get(high, k, here), get(low, k, here)),
            (get(at, k, up), get(at, k, down)),
            (ahead, behind),
        )

    c = get(at, F, here)
    around = ((get(high, F, here), get(low, F, here)), (get(at, F, up), get(at, F, down)), (get(at, FP, here), get(at, FM, here)))
    d = [p - m for p, m in around]
    second = [p + m - 2.0 * c for p, m in around]
    mxy = (get(high, F, up) - get(high, F, down)) - (get(low, F, up) - get(low, F, down))
    mxz = (get(high, FP, here) - get(high, FM, here)) - (get(low, FP, here) - get(low, FM, here))
    myz = (get(at, FP, up) - get(at, FM, up)) - (get(at, FP, down) - get(at, FM, down))
    dd = [v * v for v in d]
    inverse = lax.rsqrt(jnp.maximum(dd[0] + dd[1] + dd[2], 1.0))
    bend = (dd[0] * second[0] + dd[1] * second[1] + dd[2] * second[2]) + 0.5 * (
        d[0] * (d[1] * mxy + d[2] * mxz) + d[1] * d[2] * myz
    )
    laplace = second[0] + second[1] + second[2]
    volume = 1.0 / (0.5 + 0.5 * c)
    pull = (bend * (inverse * inverse) - laplace) * (0.5 * inverse) * volume
    nu = (0.02 + 0.03 * c) * volume
    if len(components) == 3:
        stars = [star(k, k) for k in (U, V, W)]
        centres = [s[0] for s in stars]
    else:
        stars = [star(U, 0)]
        centres = [stars[0][0], get(at, V, here), get(at, W, here)]
    speeds = [jnp.abs(v) for v in centres]
    if len(components) == 3:
        guesses = star(G, 4)[1]
    else:
        guesses = ((get(high, G, here), get(low, G, here)),)
    lift = 2.0 - volume
    out = []
    for k in components:
        centre, sides_ = stars[k]
        twice = 2.0 * centre
        transport = 0.0
        diffusion = 0.0
        for a in range(3):
            p, m = sides_[a]
            curve = p + m - twice
            transport = transport + (centres[a] * (p - m) - speeds[a] * curve)
            diffusion = diffusion + curve
        change = nu * diffusion + pull * d[k] - 0.5 * transport
        p, m = guesses[k]
        out.append(centre + 0.1 * (change + 0.5 * (lift * (p - m))))
    if len(components) == 1:
        return out
    net = 0.0
    for a in range(3):
        p, m = stars[a][1][a]
        fp, fm = around[a]
        ahead = centres[a] + p
        behind = centres[a] + m
        net = net + (
            (jnp.maximum(ahead, 0.0) - jnp.minimum(behind, 0.0)) * c
            + (jnp.minimum(ahead, 0.0) * fp - jnp.maximum(behind, 0.0) * fm)
        )
    return out + [c - 0.05 * net]


def source_plane(x, before, after, v, w, moments, pack):
    lane = lanes(NY)
    row = lax.broadcasted_iota(jnp.int32, (NY, 128), 0)
    v_up = jnp.where(row == NY - 1, 0.0, pltpu.roll(v, NY - 1, 0))
    v_down = jnp.where(row == 0, 0.0, pltpu.roll(v, 1, 0))
    w_up = jnp.where(lane == NZ - 1, 0.0, pltpu.roll(w, NZ - 1, 1))
    w_down = jnp.where(lane == 0, 0.0, pltpu.roll(w, 1, 1))
    s = 2.5 * ((after - before) + (v_up - v_down) + (w_up - w_down))
    part = jnp.dot(s, moments[0], precision=HIGHEST, preferred_element_type=F32) + jnp.dot(
        w, moments[1], precision=HIGHEST, preferred_element_type=F32
    )
    pack[...] += pltpu.roll(part, 16 * x, 1) if x else part
    return s


def start_copies(pairs, sem):
    copies = [pltpu.make_async_copy(src, dst, sem.at[k]) for k, (src, dst) in enumerate(pairs)]
    for copy in copies:
        copy.start()
    return copies


def inner_body(vel, frac, guess, sides, moments, *refs):
    buffers = refs[:7]
    mid, frac_new, source, pack, sem = refs[7:]
    U, V, W, F, G = buffers[:5]
    own = pl.ds(TOP, NY)
    sources = [vel.at[0], vel.at[1], vel.at[2], frac, guess]
    copies = start_copies([(src, buf.at[pl.ds(0, NX), own]) for src, buf in zip(sources, (U, V, W, F, G))], sem)
    pack[...] = jnp.zeros((NY, 128), F32)
    for copy in copies:
        copy.wait()
    fill_shifts(buffers, sides[...], range(NX), range(2, 2 + NX))

    def block(i, carry):
        x = 1 + i // 16
        y = pl.multiple_of((i % 16) * 8, 8)
        rows = pl.ds(y, 8)
        mid[0, x, rows], mid[1, x, rows], mid[2, x, rows], frac_new[x, rows] = cells(
            (buffers, x - 1), (buffers, x), (buffers, x + 1), sides, x + 2, y, (0, 1, 2)
        )
        return carry

    lax.fori_loop(0, 16 * (NX - 2), block, 0, unroll=4)
    for x in range(2, NX - 2):
        source[x] = source_plane(x, mid[0, x - 1], mid[0, x + 1], mid[1, x], mid[2, x], moments, pack)


def side_part(up, at_end, message, sides, profile, moments, given, given_mid, mid, frac, source, pack, scratch):
    buffers, (Z, end_mid, sem) = scratch[:7], scratch[7:]
    U, V, W, F, G = buffers[:5]
    own = pl.ds(TOP, NY)
    near = 0 if up else 1
    pairs = [
        (message.at[pl.ds(0, 2)], U.at[:, own]),
        (message.at[2], V.at[near, own]),
        (message.at[3], W.at[near, own]),
        (message.at[pl.ds(4, 2)], F.at[:, own]),
        (message.at[pl.ds(6, 2)], G.at[:, own]),
        (message.at[8], Z),
    ]
    for copy in start_copies(pairs, sem):
        copy.wait()
    lane = lanes(NY)
    slot = lane // 2 % 12
    group = lane // 2 // 12
    merged = sides[...]
    if up:
        beyond = pltpu.roll(Z[...], 16, 1)
        if at_end is not None:
            wall = jnp.where(slot == 10, pltpu.roll(merged, 2, 1), pltpu.roll(merged, 4, 1))
            beyond = jnp.where(at_end, wall, beyond)
        Z[...] = jnp.where(slot >= 10, beyond, merged)
    else:
        beyond = pltpu.roll(Z[...], 112, 1)
        if at_end is not None:
            wall = jnp.where(group == 0, profile[0], jnp.where(group == 3, profile[1], 0.0))
            beyond = jnp.where(at_end, wall, beyond)
        Z[...] = jnp.where(slot < 2, beyond, merged)
    if at_end is not None:

        @pl.when(at_end)
        def _():
            for e in range(2):
                U[e, own] = given[0][NX - 1, own] if up else profile[0]
                F[e, own] = given[3][NX - 1, own] if up else profile[1]
            if up:
                V[near, own] = given[1][NX - 1, own]
                W[near, own] = given[2][NX - 1, own]

    fill_shifts(buffers, Z[...], range(2), (10, 11) if up else (0, 1))
    halo = [(buffers, 0), (buffers, 1)]
    line = [(given, NX - 2), (given, NX - 1)] + halo if up else halo + [(given, 0), (given, 1)]
    inside, outside = (line[:3], line[1:]) if up else (line[1:], line[:3])

    def block(i, carry):
        y = pl.multiple_of(i * 8, 8)
        rows = pl.ds(y, 8)
        mid[0, rows], mid[1, rows], mid[2, rows], frac[rows] = cells(*inside, Z, 9 if up else 2, y, (0, 1, 2))
        (end_mid[rows],) = cells(*outside, Z, 10 if up else 1, y, (0,))
        return carry

    lax.fori_loop(0, 16, block, 0, unroll=4)
    if up:
        source[0] = source_plane(6, given_mid[0, 5], mid[0], given_mid[1, 6], given_mid[2, 6], moments, pack)
        source[1] = source_plane(7, given_mid[0, 6], end_mid[...], mid[1], mid[2], moments, pack)
    else:
        source[0] = source_plane(0, end_mid[...], given_mid[0, 1], mid[1], mid[2], moments, pack)
        source[1] = source_plane(1, mid[0], given_mid[0, 2], given_mid[1, 1], given_mid[2, 1], moments, pack)


def paired_body(flags, message, sides, profile, moments, *refs):
    given, given_mid, given_pack = refs[:7], refs[7], refs[8]
    mid, frac, source, pack = refs[9:13]
    pack[...] = given_pack[...]
    for up in (True, False):

        @pl.when(flags[2] == int(up))
        def _(up=up):
            side_part(
                up, None, message, sides, profile, moments, given, given_mid, mid.at[:, 0], frac, source, pack, refs[13:]
            )


def other_body(flags, message, sides, profile, moments, *refs):
    given, (given_mid, given_frac, given_source) = refs[:7], refs[7:10]
    paired_frac, paired_source, given_pack = refs[10:13]
    mid, frac_new, source, to_paired, to_other, pack = refs[13:19]
    scratch, keep_sem = refs[19:-1], refs[-1]
    even = flags[2] == 1
    middle = pl.ds(1, NX - 2)
    kept = [
        (given_frac.at[middle], frac_new.at[middle]),
        (paired_frac, frac_new.at[jnp.where(even, NX - 1, 0)]),
        (paired_source, source.at[pl.ds(jnp.where(even, NX - 2, 0), 2)]),
        (paired_source, to_paired.at[pl.ds(jnp.where(even, NX - 3, 0), 2)]),
        (paired_source.at[jnp.where(even, 0, 1)], to_other.at[jnp.where(even, NX - 2, 0)]),
    ]
    for out, place in ((source, 2), (to_paired, jnp.where(even, 1, 2)), (to_other, jnp.where(even, 2, 1))):
        kept.append((given_source.at[pl.ds(2, NX - 4)], out.at[pl.ds(place, NX - 4)]))
    kept = start_copies(kept, keep_sem)
    pack[...] = given_pack[...]
    for up in (True, False):

        @pl.when(flags[2] == 1 - int(up))
        def _(up=up):
            side_part(
                up,
                flags[1 if up else 0] == 1,
                message, sides, profile, moments, given, given_mid,
                mid.at[:, 0],
                frac_new.at[NX - 1 if up else 0],
                source.at[pl.ds(NX - 2 if up else 0, 2)],
                pack,
                scratch,
            )

    place = jnp.where(even, 0, NX - 2)
    for k in range(2):
        to_other[jnp.where(even, 0, NX - 3) + k] = source[place + k]
    to_paired[place] = source[jnp.where(even, 1, NX - 2)]
    for copy in kept:
        copy.wait()


def combine_body(a, b, c, d, table, _, __, to_paired, to_other, out, sem):
    total = 0.0
    for k, ref in enumerate((a, b, c, d)):
        total = total + jnp.dot(ref[...], table[k], precision=HIGHEST, preferred_element_type=F32)
    out[...] = total
    for copy in start_copies([(out, message.at[NX - 1]) for message in (to_paired, to_other)], sem):
        copy.wait()


def merge_body(before, after, _, __, right, left, out, sem):
    lane = lanes(NY)
    out[...] = jnp.where(lane % 2 == 1, before[...], pltpu.roll(after[...], 126, 1))
    copies = [pltpu.make_async_copy(out, m.at[NX], sem.at[k]) for k, m in enumerate((right, left))]
    for copy in copies:
        copy.start()
    for copy in copies:
        copy.wait()


HALO = POWERS


def put(out, m, plane, y, value):
    size = value.shape[0]
    out[m, plane, pl.ds(TOP + y, size)] = value
    if y == 0:
        out[m, plane, pl.ds(TOP - 1, 1)] = value[:1]
    if y + size == NY:
        out[m, plane, pl.ds(TOP + NY, 1)] = value[size - 1 :]


def terms(table, U, E, lhs, row, plane, values, moments, start, first_group=0):
    lane = lanes(NY)
    head = values.astype(BF16)
    tail = (values - head.astype(F32)).astype(BF16)
    m_head = moments.astype(BF16).astype(F32)
    m_tail = moments - m_head
    side = jnp.where(
        lane < 16,
        m_head,
        jnp.where(
            lane < 32,
            pltpu.roll(m_tail, 16, 1),
            jnp.where(lane < 48, pltpu.roll(m_head, 32, 1), 0.0),
        ),
    )
    lhs[:, 0:128] = head
    lhs[:, 128:256] = tail
    lhs[:, 256:384] = head
    lhs[:, 384:512] = side.astype(BF16)
    result = jnp.dot(lhs[...], table[:, start * 128 :], preferred_element_type=F32)
    for m in range(start, POWERS):
        put(U, m, row, 0, result[:, (m - start) * 128 : (m - start + 1) * 128])
    ends = result[:, (POWERS - start) * 128 :]
    group, offset = plane // 8 - first_group, 16 * (plane % 8)
    E[group] += pltpu.roll(ends, offset, 1)


def own_terms_body(source, far, table, U, E, lhs):
    E[...] = jnp.zeros((3, NY, 128), F32)

    def own_plane(x, carry):
        moments = pltpu.roll(far[...], (128 - 16 * x) % 128, 1)
        terms(table, U, E, lhs, x, x + HALO, source[x], moments, 0)
        return carry

    lax.fori_loop(0, NX, own_plane, 0, unroll=2)


def side_terms_body(flags, paired, given_E, table, U, E, lhs):
    even = flags[2] == 1
    E[...] = given_E[...]
    for k in range(1, HALO + 1):
        x = jnp.where(even, k - 1, NX - k)
        moments = pltpu.roll(paired[NX - 1], (128 - 16 * x) % 128, 1)
        plane = jnp.where(even, HALO + NX - 1 + k, HALO - k)
        place = jnp.where(even, k - 1, HALO - k)
        terms(table, U, E, lhs, place, plane, paired[place], moments, k - 1)


def domain(flags):
    first = flags[0] == 1
    last = flags[1] == 1

    def inside(plane):
        kept = ((plane >= HALO) | jnp.logical_not(first)) & ((plane < HALO + NX) | jnp.logical_not(last))
        return jnp.where(kept, 1.0, 0.0).astype(F32)

    return inside


def beside(U, m, plane, y):
    here = pl.ds(TOP + y, 32)
    return (U[m, plane - 1, here] + U[m, plane + 1, here]) + (
        U[m, plane, pl.ds(TOP + y - 1, 32)] + U[m, plane, pl.ds(TOP + y + 1, 32)]
    )


def sweep_ends(start, first_plane, inside):
    count = len(start)
    lane = lanes(NY)
    row = lax.broadcasted_iota(jnp.int32, (NY, 128), 0)
    used = lane % 16 < 14
    keeps = [jnp.where(used, inside(first_plane + 8 * g + lane // 16), 0.0) for g in range(count)]
    ends = start
    for m in range(POWERS - 1):
        before = [pltpu.roll(e, 14, 1) for e in ends]
        after = [pltpu.roll(e, 110, 1) for e in ends]
        same = [pltpu.roll(e, 126, 1) for e in ends]
        updated = []
        for g in range(count):
            behind = jnp.where(lane < 16, before[g - 1] if g else 0.0, before[g])
            ahead = jnp.where(lane >= 112, after[g + 1] if g < count - 1 else 0.0, after[g])
            up = jnp.where(row == NY - 1, same[g], pltpu.roll(same[g], NY - 1, 0))
            down = jnp.where(row == 0, same[g], pltpu.roll(same[g], 1, 0))
            updated.append(start[g] + keeps[g] * ((behind + ahead) + (up + down)))
        ends = updated
    return ends


def first_sweeps_body(flags, given_U, given_side, given_E, out, E, U, sem, side_sem):
    inside = domain(flags)
    even = flags[2] == 1
    top = POWERS - 1
    fetches = [
        pltpu.make_async_copy(given_U.at[top], U.at[top, pl.ds(HALO, NX)], sem),
        pltpu.make_async_copy(given_side.at[top], U.at[top, pl.ds(jnp.where(even, HALO + NX, 0), HALO)], side_sem),
    ]
    for fetch in fetches:
        fetch.start()

    def clear(i, carry):
        U[top, jnp.where(even, i, HALO + NX + i)] = jnp.zeros((ROWS, NZ), F32)
        return carry

    lax.fori_loop(0, HALO, clear, 0)
    for g, value in enumerate(sweep_ends([given_E[g] for g in range(3)], 0, inside)):
        E[g] = value
    for fetch in fetches:
        fetch.wait()

    for m in range(top - 1, -1, -1):

        def sweep(i, carry, m=m):
            low, high = HALO - 1 - i, HALO + NX + i
            plane = jnp.where(even, high, low)
            place = jnp.where(even, i, HALO - 1 - i)
            far_plane = jnp.where(even, low, high)
            keep = inside(far_plane)
            for y in range(0, NY, 32):
                here = pl.ds(TOP + y, 32)
                put(U, m, plane, y, given_side[m, place, here] + beside(U, m + 1, plane, y))
                put(U, m, far_plane, y, keep * beside(U, m + 1, far_plane, y))
            return carry

        def sweep_own(x, carry, m=m):
            for y in range(0, NY, 32):
                put(
                    U, m, x + HALO, y,
                    given_U[m, x, pl.ds(TOP + y, 32)] + beside(U, m + 1, x + HALO, y),
                )
            return carry

        lax.fori_loop(0, m + 1, sweep, 0, unroll=2 if m % 2 == 1 else 1)
        lax.fori_loop(0, NX, sweep_own, 0, unroll=2)

    def emit(j, carry):
        out[j] = U[0, HALO - 1 + j]
        return carry

    lax.fori_loop(0, NX + 2, emit, 0)


def solve_body(more, *refs):
    (flags, mid, mid_paired, mid_other, frac, now, other, table, given_sum, given_E) = refs[:10]
    vel, pressure = refs[10:12]
    if more:
        faces_paired, faces_other, packed, guess = refs[12:16]
    U, T, E, beyond, lhs = refs[-5:]
    inside = domain(flags)
    even = flags[2] == 1
    top = POWERS - 1
    first_group = jnp.where(even, 0, 1)

    def halo_plane(k):
        return jnp.where(even, HALO - k, HALO + NX - 1 + k)

    def own_plane(depth):
        return jnp.where(even, HALO + depth, HALO + NX - 1 - depth)

    E[...] = jnp.zeros((2, NY, 128), F32)
    for k in range(1, HALO + 1):
        x = jnp.where(even, NX - k, k - 1)
        moments = pltpu.roll(other[NX - 1], (128 - 16 * x) % 128, 1)
        plane = halo_plane(k)
        place = jnp.where(even, HALO - k, k - 1)
        terms(table, U, E, lhs, plane, plane, other[place], moments, k - 1, first_group)
    for m in range(top, -1, -1):
        for depth in (top - m, top + 1 - m):
            U[m, own_plane(depth)] = jnp.zeros((ROWS, NZ), F32)
    U[0, jnp.where(even, HALO + NX, HALO - 1)] = jnp.zeros((ROWS, NZ), F32)

    for m in range(top - 1, -1, -1):

        def sweep(i, carry, m=m):
            plane = halo_plane(1 + i)
            keep = inside(plane)
            for y in range(0, NY, 32):
                put(U, m, plane, y, U[m, plane, pl.ds(TOP + y, 32)] + keep * beside(U, m + 1, plane, y))
            return carry

        def sweep_own(depth, carry, m=m):
            plane = own_plane(depth)
            for y in range(0, NY, 32):
                put(U, m, plane, y, beside(U, m + 1, plane, y))
            return carry

        lax.fori_loop(0, m + 1, sweep, 0, unroll=2 if m % 2 == 1 else 1)
        lax.fori_loop(0, top - m, sweep_own, 0, unroll=2 if (top - m) % 2 == 0 else 1)

    for j in range(NX + 2):
        T[j] = given_sum[j] + U[0, HALO - 1 + j]
    ends = sweep_ends([E[0], E[1]], 8 * first_group, inside)
    beyond[...] = given_E[...]
    beyond[first_group] += ends[0]
    beyond[first_group + 1] += ends[1]

    def correct(x, mid, mx):
        plane = x + 1
        slot = x + HALO
        lane = lanes(NY)
        turned = pltpu.roll(beyond[slot // 8], (128 - 16 * (slot % 8) - 1) % 128, 1)
        centre = T[plane, pl.ds(TOP, NY)]
        ahead = jnp.where(lane == NZ - 1, turned, pltpu.roll(centre, NZ - 1, 1))
        behind = jnp.where(lane == 0, turned, pltpu.roll(centre, 1, 1))
        vel[2, x] = mid[2, mx] + 0.1 * (ahead - behind)
        for y in range(0, NY, 32):
            here = pl.ds(TOP + y, 32)
            rows = pl.ds(y, 32)
            p = -T[plane, here]
            pressure[x, rows] = p
            vel[0, x, rows] = mid[0, mx, rows] + 0.1 * (T[plane + 1, here] - T[plane - 1, here])
            vel[1, x, rows] = mid[1, mx, rows] + 0.1 * (
                T[plane, pl.ds(TOP + y + 1, 32)] - T[plane, pl.ds(TOP + y - 1, 32)]
            )
            if more:
                guess[x, rows] = 2.0 * p - now[x, rows]

    def correct_inner(x, carry):
        correct(x, mid, x)
        return carry

    lax.fori_loop(1, NX - 1, correct_inner, 0, unroll=2)
    correct(jnp.where(even, NX - 1, 0), mid_paired, 0)
    correct(jnp.where(even, 0, NX - 1), mid_other, 0)
    if more:
        emit_faces(flags, vel, frac, guess, faces_paired, faces_other)
        packed[...] = pack_columns(lambda k, x: fields_of(vel, frac, guess, k, x))


def shape(*dims):
    return jax.ShapeDtypeStruct(dims, F32)


IN_VMEM = pl.BlockSpec(memory_space=pltpu.VMEM)
IN_SMEM = pl.BlockSpec(memory_space=pltpu.SMEM)
IN_HBM = pl.BlockSpec(memory_space=pltpu.HBM)
ANYWHERE = pl.BlockSpec(memory_space=pl.ANY)
BLOCK = (NX, NY, NZ)
MESSAGE = (NX + 1, NY, NZ)


def pack_call(flags, velocity, fraction, now, old):
    return pl.pallas_call(
        pack_body,
        out_shape=(shape(*MESSAGE), shape(*MESSAGE), shape(NY, 128), shape(*BLOCK)),
        in_specs=[IN_SMEM] + [IN_HBM] * 4,
        out_specs=(IN_VMEM,) * 4,
        scratch_shapes=[pltpu.VMEM((3, *BLOCK), F32)]
        + [pltpu.VMEM(BLOCK, F32)] * 3
        + [pltpu.SemaphoreType.DMA((6,))],
        compiler_params=pltpu.CompilerParams(vmem_limit_bytes=60 * MIB),
        name="pack",
    )(flags, velocity, fraction, now, old)


PADDED = (NX, ROWS, NZ)
PREDICTED = tuple(shape(*PADDED) for _ in range(7)) + (
    shape(3, *BLOCK),
    shape(*BLOCK),
    shape(*BLOCK),
    shape(NY, 128),
)


def inner_call(velocity, fraction, guess, sides, moments):
    return pl.pallas_call(
        inner_body,
        out_shape=PREDICTED,
        in_specs=[ANYWHERE] * 3 + [IN_VMEM] * 2,
        out_specs=(IN_VMEM,) * 11,
        scratch_shapes=[pltpu.SemaphoreType.DMA((5,))],
        compiler_params=pltpu.CompilerParams(vmem_limit_bytes=16 * MIB),
        cost_estimate=pl.CostEstimate(flops=20_000_000, bytes_accessed=16_000_000, transcendentals=100_000),
        name="inner",
    )(velocity, fraction, guess, sides, moments)


SIDE_SCRATCH = [pltpu.VMEM((2, ROWS, NZ), F32)] * 7 + [
    pltpu.VMEM((NY, 128), F32),
    pltpu.VMEM((NY, NZ), F32),
    pltpu.SemaphoreType.DMA((6,)),
]


def paired_call(flags, message, sides, profile, moments, inner):
    *buffers, mid, _, _, pack = inner
    return pl.pallas_call(
        paired_body,
        out_shape=(shape(3, 1, NY, NZ), shape(NY, NZ), shape(2, NY, NZ), shape(NY, 128)),
        in_specs=[IN_SMEM] + [ANYWHERE] + [IN_VMEM] * 12,
        out_specs=(IN_VMEM,) * 4,
        scratch_shapes=SIDE_SCRATCH,
        compiler_params=pltpu.CompilerParams(vmem_limit_bytes=12 * MIB),
        cost_estimate=pl.CostEstimate(flops=6_000_000, bytes_accessed=6_000_000, transcendentals=30_000),
        name="paired_side",
    )(flags, message, sides, profile, moments, *buffers, mid, pack)


def other_call(flags, message, sides, profile, moments, inner, frac, source, pack):
    *buffers, mid, inner_frac, inner_source, _ = inner
    return pl.pallas_call(
        other_body,
        out_shape=(shape(3, 1, NY, NZ), *[shape(*BLOCK)] * 4, shape(NY, 128)),
        in_specs=[IN_SMEM] + [ANYWHERE] + [IN_VMEM] * 11 + [ANYWHERE] * 4 + [IN_VMEM],
        out_specs=(IN_VMEM,) * 6,
        scratch_shapes=SIDE_SCRATCH + [pltpu.SemaphoreType.DMA((8,))],
        compiler_params=pltpu.CompilerParams(vmem_limit_bytes=12 * MIB),
        name="other_side",
    )(flags, message, sides, profile, moments, *buffers, mid, inner_frac, inner_source, frac, source, pack)


def combine_call(packs, table, to_paired, to_other):
    return pl.pallas_call(
        combine_body,
        out_shape=(shape(*BLOCK), shape(*BLOCK), shape(NY, 128)),
        in_specs=[IN_VMEM] * 5 + [ANYWHERE] * 2,
        out_specs=(ANYWHERE, ANYWHERE, IN_VMEM),
        scratch_shapes=[pltpu.SemaphoreType.DMA((2,))],
        input_output_aliases={5: 0, 6: 1},
        compiler_params=pltpu.CompilerParams(vmem_limit_bytes=4 * MIB),
        name="combine",
    )(*packs, table, to_paired, to_other)


def merge_call(before, after, right, left):
    return pl.pallas_call(
        merge_body,
        out_shape=(shape(*MESSAGE), shape(*MESSAGE), shape(NY, 128)),
        in_specs=[IN_VMEM] * 2 + [ANYWHERE] * 2,
        out_specs=(ANYWHERE, ANYWHERE, IN_VMEM),
        scratch_shapes=[pltpu.SemaphoreType.DMA((2,))],
        input_output_aliases={2: 0, 3: 1},
        compiler_params=pltpu.CompilerParams(vmem_limit_bytes=4 * MIB),
        name="merge",
    )(before, after, right, left)


OWN_TERMS = (POWERS, NX, ROWS, NZ)


def own_terms_call(source, far, table):
    return pl.pallas_call(
        own_terms_body,
        out_shape=(shape(*OWN_TERMS), shape(3, NY, 128)),
        in_specs=[IN_VMEM] * 3,
        out_specs=(IN_VMEM,) * 2,
        scratch_shapes=[pltpu.VMEM((NY, 512), BF16)],
        compiler_params=pltpu.CompilerParams(vmem_limit_bytes=20 * MIB),
        cost_estimate=pl.CostEstimate(flops=1_000_000_000, bytes_accessed=12_000_000, transcendentals=0),
        name="own_terms",
    )(source, far, table)


def side_terms_call(flags, paired, ends, table):
    return pl.pallas_call(
        side_terms_body,
        out_shape=(shape(POWERS, HALO, ROWS, NZ), shape(3, NY, 128)),
        in_specs=[IN_SMEM] + [IN_VMEM] * 3,
        out_specs=(IN_VMEM,) * 2,
        scratch_shapes=[pltpu.VMEM((NY, 512), BF16)],
        compiler_params=pltpu.CompilerParams(vmem_limit_bytes=12 * MIB),
        cost_estimate=pl.CostEstimate(flops=500_000_000, bytes_accessed=6_000_000, transcendentals=0),
        name="side_terms",
    )(flags, paired, ends, table)


SUM = (NX + 2, ROWS, NZ)
TERMS_SCRATCH = pltpu.VMEM((POWERS, NX + 2 * HALO, ROWS, NZ), F32)


def first_sweeps_call(flags, own, side, ends):
    return pl.pallas_call(
        first_sweeps_body,
        out_shape=(shape(*SUM), shape(3, NY, 128)),
        in_specs=[IN_SMEM] + [IN_VMEM] * 3,
        out_specs=(IN_VMEM,) * 2,
        scratch_shapes=[TERMS_SCRATCH, pltpu.SemaphoreType.DMA, pltpu.SemaphoreType.DMA],
        compiler_params=pltpu.CompilerParams(vmem_limit_bytes=18 * MIB),
        cost_estimate=pl.CostEstimate(flops=10_000_000, bytes_accessed=14_000_000, transcendentals=0),
        name="first_sweeps",
    )(flags, own, side, ends)


def solve_call(more, flags, mid, mid_paired, mid_other, frac, now, other, table, part, ends):
    outs = [shape(3, *BLOCK), shape(*BLOCK)]
    if more:
        outs += [shape(*MESSAGE), shape(*MESSAGE), shape(NY, 128), shape(*BLOCK)]
    return pl.pallas_call(
        functools.partial(solve_body, more),
        out_shape=tuple(outs),
        in_specs=[IN_SMEM] + [IN_VMEM] * 9,
        out_specs=(IN_VMEM,) * len(outs),
        scratch_shapes=[
            TERMS_SCRATCH,
            pltpu.VMEM(SUM, F32),
            pltpu.VMEM((2, NY, 128), F32),
            pltpu.VMEM((3, NY, 128), F32),
            pltpu.VMEM((NY, 512), BF16),
        ],
        compiler_params=pltpu.CompilerParams(vmem_limit_bytes=20 * MIB),
        name="solve",
    )(flags, mid, mid_paired, mid_other, frac, now, other, table, part, ends)


def per_device(velocity, fraction, pressure_now, pressure_old, inflow):
    stream = lax.axis_index("stream")
    count = lax.axis_size("stream")
    flags = jnp.stack([stream == 0, stream == count - 1, stream % 2 == 0]).astype(jnp.int32)
    pairs = [(i, i ^ 1) for i in range(count)]
    others = [(i, ((i + 1) ^ 1) - 1) for i in range(1, count - 1)]

    def exchange(block, with_pair):
        return lax.ppermute(block, "stream", pairs if with_pair else others)

    def around(block, offset):
        return lax.ppermute(
            block, "span", [((i + offset) % BLOCKS, i) for i in range(BLOCKS)]
        )

    profile = jnp.broadcast_to(inflow[:, :, None], (2, NY, NZ))
    moments = jnp.asarray(moment_table())
    combine = jnp.asarray(combine_table())
    table = jnp.asarray(solve_table())

    paired, other, packed, guess = pack_call(flags, velocity, fraction, pressure_now, pressure_old)
    now = pressure_now
    for step in range(STEPS):
        more = step < STEPS - 1
        paired, other, sides = merge_call(around(packed, -1), around(packed, 1), paired, other)
        other = exchange(other, False)
        paired = exchange(paired, True)
        inner = inner_call(velocity, fraction, guess, sides, moments)
        mid_paired, frac, source, pack = paired_call(flags, paired, sides, profile, moments, inner)
        mid_other, fraction, source, to_paired, to_other, pack = other_call(
            flags, other, sides, profile, moments, inner, frac, source, pack
        )
        packs = [pack] + [around(pack, o) for o in (1, 2, 3)]
        to_paired, to_other, far = combine_call(packs, combine, to_paired, to_other)
        other = exchange(to_other, False)
        paired = exchange(to_paired, True)
        own, ends = own_terms_call(source, far, table)
        side, ends = side_terms_call(flags, paired, ends, table)
        part, ends = first_sweeps_call(flags, own, side, ends)
        results = solve_call(
            more, flags, inner[7], mid_paired, mid_other, fraction, now, other, table, part, ends
        )
        velocity, pressure = results[:2]
        old, now = now, pressure
        if more:
            paired, other, packed, guess = results[2:]
    return (velocity, fraction, now, old)


def solution(mesh):
    return jax.shard_map(
        per_device,
        mesh=mesh,
        in_specs=(
            P(None, "stream", None, "span"),
            P("stream", None, "span"),
            P("stream", None, "span"),
            P("stream", None, "span"),
            P(),
        ),
        out_specs=(
            P(None, "stream", None, "span"),
            P("stream", None, "span"),
            P("stream", None, "span"),
            P("stream", None, "span"),
        ),
        check_vma=False,
    )
```
